32 devices in a mesh: dp: 8 (over z, y), head: 4 (over x, core).
Axes of the slice: x: 2, y: 2, z: 4, core: 2. Of those that a mesh axis runs over, the one named last changes fastest.
Arguments:
- layer_input: bfloat16 [2, 16384, 768], P(None, ('dp', 'head')), may hold values from -6 to 6
- output_grad: bfloat16 [2, 16384, 768], P(None, ('dp', 'head')), may hold values from -6 to 6
- lengths: int32 [2, 32], P(None, 'dp'), may hold values from 64 to 512, as said below
- w_qkv: bfloat16 [3, 768, 768], P(None, 'dp', 'head'), may hold values from -0.21875 to 0.21875
- w_out: bfloat16 [768, 768], P('head', 'dp'), may hold values from -4 to 4
- w_up: bfloat16 [768, 3072], P('dp', 'head'), may hold values from -0.21875 to 0.21875
- w_down: bfloat16 [3072, 768], P('head', 'dp'), may hold values from -0.109375 to 0.109375
- norm_gains: float32 [2, 768], replicated, may hold values from 0.5 to 1.5
- norm_biases: float32 [2, 768], replicated, may hold values from -3 to 3
- mask_logits: float32 [12, 512, 512], P('head', 'dp'), may hold values from -9 to 9
- mask_noise: float32 [12, 512, 512], P('head', 'dp'), may hold values from -6 to 6
Outputs:
- layer_output: bfloat16 [2, 16384, 768], P(None, ('dp', 'head'))
- input_grad: float32 [2, 16384, 768], P(None, ('dp', 'head'))
- w_qkv_grad: float32 [3, 768, 768], P(None, 'dp', 'head')
- w_out_grad: float32 [768, 768], P('head', 'dp')
- w_up_grad: float32 [768, 3072], P('dp', 'head')
- w_down_grad: float32 [3072, 768], P('head', 'dp')
- gains_grad: float32 [2, 768], replicated
- biases_grad: float32 [2, 768], replicated
- logits_grad: float32 [12, 512, 512], P('head', 'dp')
The draws below stay inside these ranges and needn't reach their ends.
Inputs may be any that keep to these rules, and one draw needn't show every extreme that they name: `lengths`: each sequence's number of valid tokens; in each micro-batch the first sequence of each index of dp has 512.
All inputs are finite; a program needn't handle non-finite values.
Results may differ from the reference program's by a relative error of at most 0.013.
The reference program's roundings to bfloat16 on the way count: a program that leaves them out, or rounds other values in their place, can miss the bound.
Values may be sent and summed in bfloat16 or wider, within the bound.
No kernel may reach another device: no remote copies, remote signals or barrier semaphores. Data moves between devices by JAX's collectives and lax.ppermute only.
A program may use at most 192 MiB of HBM per device.

```python
import math
import jax
import jax.numpy as jnp
from jax import lax

D = 768
HEADS = 12
HEAD_DIM = 64
FF = 3072
SEQ_LEN = 512
MIN_LEN = 64
SEQ_MB = 4
MICRO = 2
MB_SEQS = 32
MB_ROWS = 16384
SEQS = 64


def draw_lengths(key, part):
    values = jax.random.randint(key, (MICRO, MB_SEQS), MIN_LEN, SEQ_LEN + 1, dtype=jnp.int32)
    values = values.at[0, 1].set(MIN_LEN)
    return values.at[:, ::SEQ_MB].set(SEQ_LEN)


def shard_levels(stream_key, extent, pieces, low, top_value):
    def one(axis_at, parts):
        draws = jax.random.uniform(jax.random.fold_in(jax.random.fold_in(stream_key, 6), axis_at), (parts,), jnp.float32, low / len(pieces), top_value / len(pieces))
        return jnp.repeat(jnp.exp(draws), extent[axis_at] // parts).reshape((-1,) + (1,) * (len(extent) - axis_at - 1))

    level = one(*pieces[0])
    for cut in pieces[1:]:
        level = level * one(*cut)
    return level


def centred(own_key, extent, scale, reach, pieces=(), kind=jnp.bfloat16):
    values = jax.random.normal(own_key, extent, jnp.float32) * scale
    if len(pieces) > 0:
        values = shard_levels(own_key, extent, pieces, -0.22, 0.18) * values
    return jnp.clip(values, min=-reach, max=reach).astype(kind)


def setup_inputs(seed: int = 0) -> dict:
    key_of = jax.random.split(jax.random.key(seed), 12)
    layer_input = centred(key_of[0], (MICRO, MB_ROWS, D), 1.0, 6.0, ((1, 32),))
    output_grad = centred(key_of[1], (MICRO, MB_ROWS, D), 1.0, 6.0, ((1, 32),))
    lengths = draw_lengths(jax.random.fold_in(key_of[11], 71), 0)
    w_qkv = centred(key_of[3], (3, D, D), D ** -0.5, 0.21875, ((1, 8), (2, 4)))
    w_out = centred(key_of[4], (D, D), 2 ** -0.5, 4.0, ((0, 4), (1, 8)))
    w_up = centred(key_of[5], (D, FF), D ** -0.5, 0.21875, ((0, 8), (1, 4)))
    w_down = centred(key_of[6], (FF, D), FF ** -0.5, 0.109375, ((0, 4), (1, 8)))
    norm_gains = jnp.clip(1.0 + 0.1 * jax.random.normal(key_of[7], (2, D), jnp.float32), 0.5, 1.5)
    norm_biases = centred(key_of[8], (2, D), 0.5, 3.0, (), jnp.float32)
    mask_logits = centred(key_of[9], (HEADS, SEQ_LEN, SEQ_LEN), 1.5, 9.0, ((0, 4), (1, 8)), jnp.float32)
    mask_noise = centred(key_of[10], (HEADS, SEQ_LEN, SEQ_LEN), 1.0, 6.0, ((0, 4), (1, 8)), jnp.float32)
    return dict(layer_input=layer_input, output_grad=output_grad, lengths=lengths, w_qkv=w_qkv, w_out=w_out, w_up=w_up, w_down=w_down, norm_gains=norm_gains, norm_biases=norm_biases, mask_logits=mask_logits, mask_noise=mask_noise)


@jax.custom_vjp
def low(v):
    return lax.optimization_barrier(v.astype(jnp.bfloat16)).astype(jnp.float32)

@jax.custom_vjp
def low_back(v):
    return v

def low_keep(v):
    return (low(v), None)

def low_pass(kept, grad):
    return (grad,)

def back_keep(v):
    return (v, None)

def back_low(kept, grad):
    return (low(grad),)
low.defvjp(low_keep, low_pass)
low_back.defvjp(back_keep, back_low)
epsilon = 1e-05

def mat_mul(left, right):
    return jnp.dot(left, right, precision=lax.Precision.HIGHEST)

def normalize(rows, gain, bias):
    mean = lax.optimization_barrier(jnp.mean(rows, axis=-1, keepdims=True))
    centered = rows - mean
    spread = lax.optimization_barrier(jnp.mean(centered * centered, axis=-1, keepdims=True))
    return centered * lax.rsqrt(spread + epsilon) * gain + bias

def forward(rows, w_qkv, w_out, w_up, w_down, gains, biases, gate, lens):
    group = lens.shape[0]
    proj = [low_back(low(mat_mul(rows, w_qkv[i]))) for i in range(3)]
    query, key, value = [p.reshape(group, SEQ_LEN, HEADS, HEAD_DIM) for p in proj]
    scores = jnp.einsum('gqhe,gkhe->ghqk', query, key, precision=lax.Precision.HIGHEST) / math.sqrt(HEAD_DIM)
    scores = low_back(scores)
    position = jnp.arange(SEQ_LEN, dtype=jnp.int32)
    key_ok = position[None, :] < lens[:, None]
    scores = jnp.where(key_ok[:, None, None, :], scores, jnp.float32(-1e+30))
    probs = jax.nn.softmax(scores, axis=-1)
    weights = low(probs * gate[None])
    mixed = jnp.einsum('ghqk,gkhe->gqhe', weights, value, precision=lax.Precision.HIGHEST)
    mixed = low_back(low(mixed.reshape(group * SEQ_LEN, D)))
    attn = low_back(mat_mul(mixed, w_out))
    hidden = low(normalize(rows + attn, gains[0], biases[0]))
    up = low_back(mat_mul(hidden, w_up))
    act = low(jax.nn.gelu(up, approximate=False))
    ffn = low_back(mat_mul(act, w_down))
    result = normalize(hidden + ffn, gains[1], biases[1])
    row_ok = key_ok.reshape(group * SEQ_LEN, 1)
    return jnp.where(row_ok, result, jnp.float32(0.0))

def reference(layer_input, output_grad, lengths, w_qkv, w_out, w_up, w_down, norm_gains, norm_biases, mask_logits, mask_noise):
    params = tuple((a.astype(jnp.float32) for a in (w_qkv, w_out, w_up, w_down, norm_gains, norm_biases, mask_logits)))
    noise = mask_noise.astype(jnp.float32)
    group = MICRO * SEQ_MB
    count = SEQS // group
    inputs = layer_input.astype(jnp.float32).reshape(count, group * SEQ_LEN, D)
    cotangents = output_grad.astype(jnp.float32).reshape(count, group * SEQ_LEN, D)
    lens_all = lengths.reshape(count, group)

    def step(totals, item):
        rows, dout, lens = item

        def layer(rows, wq, wo, wu, wd, gains, biases, logits):
            gate = jax.nn.sigmoid(logits + noise)
            return forward(rows, wq, wo, wu, wd, gains, biases, gate, lens)
        result, pull = jax.vjp(layer, rows, *params)
        grads = pull(dout)
        totals = tuple((t + g for t, g in zip(totals, grads[1:])))
        return (totals, (result.astype(jnp.bfloat16), grads[0]))
    start = tuple((jnp.zeros_like(p) for p in params))
    totals, (results, dinputs) = lax.scan(step, start, (inputs, cotangents, lens_all))
    return (results.reshape(MICRO, MB_ROWS, D), dinputs.reshape(MICRO, MB_ROWS, D), totals[0], totals[1], totals[2], totals[3], totals[4], totals[5], totals[6])
```

```python
import functools, math
import jax, jax.numpy as jnp
from jax import lax
from jax.experimental import pallas as pl
from jax.experimental.pallas import tpu as pltpu
from jax.sharding import PartitionSpec as P

HEAD_DIM = 64
EPS = 1e-05
F32 = jnp.float32
BF16 = jnp.bfloat16
SCALE = 1.0 / math.sqrt(HEAD_DIM)
LOG2E = math.log2(math.e)
NEG = -1e30
INV_SQRT2 = 1.0 / math.sqrt(2.0)
INV_SQRT2PI = 1.0 / math.sqrt(2.0 * math.pi)


def dot_nn(a, b):
    return lax.dot_general(a, b, (((1,), (0,)), ((), ())), preferred_element_type=F32)


def dot_nt(a, b):
    return lax.dot_general(a, b, (((1,), (1,)), ((), ())), preferred_element_type=F32)


def dot_tn(a, b):
    return lax.dot_general(a, b, (((0,), (0,)), ((), ())), preferred_element_type=F32)


def piece(ref, bits, d, flip):
    y = bits[0] ^ (d & 1)
    z1 = bits[1] ^ ((d >> 1) & 1)
    z2 = bits[2] ^ ((d >> 2) & 1)
    if flip:
        return ref.at[y, 0, z1, z2]
    return ref.at[0, y, z1, z2]


def assemble(dst, ref, bits, flip):
    rows = ref.shape[-2]
    for d in range(8):
        dst[pl.ds(d * rows, rows), :] = piece(ref, bits, d, flip)[...]


def scatter(ref, src, bits, flip):
    rows = ref.shape[-2]
    for d in range(8):
        piece(ref, bits, d, flip)[...] = src[pl.ds(d * rows, rows), :]


def spec_a(tail, pick):
    zeros = (0,) * len(tail)
    return pl.BlockSpec((1, 2, 2, 2) + tail, lambda k, *_: (pick(k), 0, 0, 0) + zeros)


def spec_b(tail, pick):
    zeros = (0,) * len(tail)
    return pl.BlockSpec((2, 1, 2, 2) + tail, lambda k, *_: (0, pick(k), 0, 0) + zeros)


def whole(shape):
    zeros = (0,) * len(shape)
    return pl.BlockSpec(shape, lambda *_: zeros)


def low_pick(k):
    return jnp.minimum(k, 1)


def high_pick(k):
    return jnp.maximum(k - 2, 0)


def norm_stats(z):
    mean = jnp.mean(z, axis=1, keepdims=True)
    centered = z - mean
    inverse = lax.rsqrt(jnp.mean(centered * centered, axis=1, keepdims=True) + EPS)
    return centered * inverse, inverse


def norm_back(du, unit, inverse):
    return inverse * (
        du
        - jnp.mean(du, axis=1, keepdims=True)
        - unit * jnp.mean(du * unit, axis=1, keepdims=True)
    )


def gelu_pair(up):
    cdf = 0.5 + 0.5 * lax.erf(up * INV_SQRT2)
    pdf = INV_SQRT2PI * jnp.exp(-0.5 * (up * up))
    return up * cdf, cdf + up * pdf


def params(mib=56, n=1):
    return pltpu.CompilerParams(
        dimension_semantics=("arbitrary",) * n, vmem_limit_bytes=mib * 1024 * 1024
    )


def ffn_fwd_kernel(chunk, bits, lens, hid, ua0, ua1, db0, db1, gain, bias, dout,
                   out, dsec, dffn, dffnt, act_o, gp_o, dgain, dbias, wu, wd, acc):
    k = pl.program_id(0)
    rows = hid.shape[0]

    @pl.when(k < 2)
    def _():
        assemble(wu, ua0, bits, False)
        assemble(wd, db0, bits, True)

    @pl.when(k >= 2)
    def _():
        assemble(wu, ua1, bits, False)
        assemble(wd, db1, bits, True)

    @pl.when(k == 0)
    def _():
        acc[...] = jnp.zeros_like(acc)

    def step(r, c):
        at = pl.ds(pl.multiple_of(r * chunk, chunk), chunk)
        up = dot_nn(hid[at, :], wu[...])
        act, gp = gelu_pair(up)
        act = act.astype(BF16)
        act_o[0, at, :] = act
        gp_o[0, at, :] = gp.astype(gp_o.dtype)
        acc[at, :] += dot_nt(act, wd[...])
        return c

    lax.fori_loop(0, rows // chunk, step, 0)

    @pl.when(k == 3)
    def _():
        dgain[...] = jnp.zeros_like(dgain)
        dbias[...] = jnp.zeros_like(dbias)
        length = rows // lens.shape[0]
        small = 128

        def fin(r, c):
            start = pl.multiple_of(r * small, small)
            at = pl.ds(start, small)
            size = lens[start // length]
            pos = (start % length) + lax.broadcasted_iota(jnp.int32, (small, 1), 0)
            valid = pos < size
            second = hid[at, :].astype(F32) + acc[at, :]
            unit, inverse = norm_stats(second)
            g = gain[...]
            out[at, :] = jnp.where(valid, unit * g + bias[...], 0.0).astype(BF16)
            dy = jnp.where(valid, dout[at, :].astype(F32), 0.0)
            dgain[...] += jnp.sum(dy * unit, axis=0, keepdims=True)
            dbias[...] += jnp.sum(dy, axis=0, keepdims=True)
            dz = norm_back(dy * g, unit, inverse)
            dsec[at, :] = dz
            low = dz.astype(BF16)
            dffn[at, :] = low
            dffnt[:, at] = low.T
            return c

        lax.fori_loop(0, rows // small, fin, 0)


def ffn_forward(bits, lens, hid, ua0, ua1, db0, db1, gain, bias, dout, chunk=512, gp_dt=F32):
    rows, width = hid.shape
    n = ua0.shape[-1]
    p = ua0.shape[-2]
    sds = jax.ShapeDtypeStruct
    return pl.pallas_call(
        functools.partial(ffn_fwd_kernel, chunk),
        out_shape=(
            sds((rows, width), BF16), sds((rows, width), F32), sds((rows, width), BF16), sds((width, rows), BF16),
            sds((4, rows, n), BF16), sds((4, rows, n), gp_dt),
            sds((1, width), F32), sds((1, width), F32),
        ),
        grid_spec=pltpu.PrefetchScalarGridSpec(
            num_scalar_prefetch=2, grid=(4,),
            in_specs=[
                whole((rows, width)),
                spec_a((p, n), low_pick), spec_a((p, n), high_pick),
                spec_b((p, n), low_pick), spec_b((p, n), high_pick),
                whole((1, width)), whole((1, width)), whole((rows, width)),
            ],
            out_specs=[
                whole((rows, width)), whole((rows, width)), whole((rows, width)), whole((width, rows)),
                pl.BlockSpec((1, rows, n), lambda k, *_: (k, 0, 0)),
                pl.BlockSpec((1, rows, n), lambda k, *_: (k, 0, 0)),
                whole((1, width)), whole((1, width)),
            ],
            scratch_shapes=[
                pltpu.VMEM((width, n), BF16), pltpu.VMEM((width, n), BF16),
                pltpu.VMEM((rows, width), F32),
            ],
        ),
        compiler_params=params(),
        cost_estimate=pl.CostEstimate(
            flops=4 * rows * width * 4 * n, bytes_accessed=40 * rows * width, transcendentals=0
        ),
    )(bits, lens, hid, ua0, ua1, db0, db1, gain, bias, dout)


def ffn_bwd_kernel(chunk, last, bits, ht, dt, dffn, ua, db, act, gp, *rest):
    if last:
        dsec, part, unit, inverse, gain, gu, gd, dfirst, dattn, dattnt, dgain, dbias, wu, wd, dup_s, acc, tmp = rest
    else:
        gu, gd, dh_o, wu, wd, dup_s, acc, tmp = rest
    k = pl.program_id(0)
    rows, width = dffn.shape

    assemble(wu, ua, bits, False)
    assemble(wd, db, bits, True)

    @pl.when(k == 0)
    def _():
        if last:
            acc[...] = part[...] + dsec[...]
        else:
            acc[...] = jnp.zeros_like(acc)

    def step(r, c):
        at = pl.ds(pl.multiple_of(r * chunk, chunk), chunk)
        dact = dot_nn(dffn[at, :], wd[...])
        dup = (dact * gp[0, at, :].astype(F32)).astype(BF16)
        dup_s[at, :] = dup
        acc[at, :] += dot_nt(dup, wu[...])
        return c

    lax.fori_loop(0, rows // chunk, step, 0)

    tmp[...] = dot_nn(ht[...], dup_s[...]).astype(BF16)
    scatter(gu, tmp, bits, False)
    tmp[...] = dot_nn(dt[...], act[0]).astype(BF16)
    scatter(gd, tmp, bits, True)

    @pl.when(k == 1)
    def _():
        if not last:
            dh_o[...] = acc[...]
        else:
            dgain[...] = jnp.zeros_like(dgain)
            dbias[...] = jnp.zeros_like(dbias)
            small = 128

            def fin(r, c):
                at = pl.ds(pl.multiple_of(r * small, small), small)
                dh = acc[at, :]
                u = unit[at, :]
                dgain[...] += jnp.sum(dh * u, axis=0, keepdims=True)
                dbias[...] += jnp.sum(dh, axis=0, keepdims=True)
                dz = norm_back(dh * gain[...], u, inverse[at, :])
                dfirst[at, :] = dz
                low = dz.astype(BF16)
                dattn[at, :] = low
                dattnt[:, at] = low.T
                return c

            lax.fori_loop(0, rows // small, fin, 0)


def ffn_backward(last, bits, ht, dt, dffn, ua, db, act, gp, extra=(), chunk=512):
    rows, width = dffn.shape
    n = ua.shape[-1]
    p = ua.shape[-2]
    sds = jax.ShapeDtypeStruct
    half = (1 - last) * 2
    pick = lambda k: k
    out_shape = [sds((2, 2, 2, 2, p, n), BF16), sds((2, 2, 2, 2, p, n), BF16)]
    out_specs = [spec_a((p, n), pick), spec_b((p, n), pick)]
    in_specs = [
        whole((width, rows)), whole((width, rows)), whole((rows, width)),
        spec_a((p, n), pick), spec_b((p, n), pick),
        pl.BlockSpec((1, rows, n), lambda k, *_: (k + half, 0, 0)),
        pl.BlockSpec((1, rows, n), lambda k, *_: (k + half, 0, 0)),
    ]
    if last:
        in_specs += [whole((rows, width))] * 3 + [whole((rows, 1)), whole((1, width))]
        out_shape += [sds((rows, width), F32), sds((rows, width), BF16), sds((width, rows), BF16), sds((1, width), F32), sds((1, width), F32)]
        out_specs += [whole((rows, width))] * 2 + [whole((width, rows))] + [whole((1, width))] * 2
    else:
        out_shape += [sds((rows, width), F32)]
        out_specs += [whole((rows, width))]
    return pl.pallas_call(
        functools.partial(ffn_bwd_kernel, chunk, last),
        out_shape=out_shape,
        grid_spec=pltpu.PrefetchScalarGridSpec(
            num_scalar_prefetch=1, grid=(2,), in_specs=in_specs, out_specs=out_specs,
            scratch_shapes=[
                pltpu.VMEM((width, n), BF16), pltpu.VMEM((width, n), BF16),
                pltpu.VMEM((rows, n), BF16), pltpu.VMEM((rows, width), F32),
                pltpu.VMEM((width, n), BF16),
            ],
        ),
        compiler_params=params(),
        cost_estimate=pl.CostEstimate(
            flops=8 * rows * width * 2 * n, bytes_accessed=30 * rows * width, transcendentals=0
        ),
    )(bits, ht, dt, dffn, ua, db, act, gp, *extra)


def key_bias(size, length):
    pos = lax.broadcasted_iota(jnp.int32, (1, length), 1)
    return jnp.where(pos < size, 0.0, NEG).astype(F32)


def gate_rows(ga, gb, bits, i, d0, count):
    parts = []
    for j in range(count):
        d = d0 + j
        y = bits[0] ^ (d & 1)
        z1 = bits[1] ^ ((d >> 1) & 1)
        z2 = bits[2] ^ ((d >> 2) & 1)
        parts.append(ga[0, y, z1, z2, i])
        parts.append(gb[y, 0, z1, z2, i])
    return jnp.concatenate(parts, axis=0).astype(F32)


def att_fwd_kernel(chunk, bits, lens, qk, v, ga, gb, mixed, lse):
    length = qk.shape[1]
    heads = v.shape[2] // HEAD_DIM
    size = lens[pl.program_id(1)]
    bias = key_bias(size, length)
    per = 2 * ga.shape[-2]

    def step(r, c):
        at = pl.ds(pl.multiple_of(r * chunk, chunk), chunk)
        outs = []
        stats = []
        for i in range(heads):
            q = qk[0, at, pl.ds(i * HEAD_DIM, HEAD_DIM)]
            key = qk[0, :, pl.ds((heads + i) * HEAD_DIM, HEAD_DIM)]
            s = dot_nt(q, key) * (SCALE * LOG2E) + bias
            top = jnp.max(s, axis=1, keepdims=True)
            e = jnp.exp2(s - top)
            total = jnp.sum(e, axis=1, keepdims=True)
            g = gate_rows(ga, gb, bits, i, r * (chunk // per), chunk // per)
            w = (e * (1.0 / total) * g).astype(BF16)
            outs.append(dot_nn(w, v[0, :, pl.ds(i * HEAD_DIM, HEAD_DIM)]))
            stats.append(top + jnp.log2(total))
        mixed[0, at, :] = jnp.concatenate(outs, axis=1).astype(BF16)
        lse[0, at, :] = jnp.concatenate(stats, axis=1)
        return c

    for r in range(length // chunk):
        step(r, 0)


def attention_forward(half, bits, lens, qk, v, ga, gb, chunk=512):
    _, rows, w2 = qk.shape
    w1 = v.shape[2]
    count = lens.shape[0]
    length = rows // count
    heads, sub, keys = ga.shape[-3:]
    sds = jax.ShapeDtypeStruct
    off = half * 2
    return pl.pallas_call(
        functools.partial(att_fwd_kernel, chunk),
        out_shape=(sds((2, rows, w1), BF16), sds((2, rows, heads), F32)),
        grid_spec=pltpu.PrefetchScalarGridSpec(
            num_scalar_prefetch=2, grid=(2, count),
            in_specs=[
                pl.BlockSpec((1, length, w2), lambda k, s, *_: (k + off, s, 0)),
                pl.BlockSpec((1, length, w1), lambda k, s, *_: (k + off, s, 0)),
                spec_a((heads, sub, keys), lambda k: k), spec_b((heads, sub, keys), lambda k: k),
            ],
            out_specs=[
                pl.BlockSpec((1, length, w1), lambda k, s, *_: (k, s, 0)),
                pl.BlockSpec((1, length, heads), lambda k, s, *_: (k, s, 0)),
            ],
        ),
        compiler_params=params(n=2),
        cost_estimate=pl.CostEstimate(
            flops=16 * 2 * rows * length * w1, bytes_accessed=16 * rows * w1, transcendentals=0
        ),
    )(bits, lens, qk, v, ga, gb)


def att_bwd_kernel(chunk, bits, lens, qk, v, ga, gb, lse, dattn, wo,
                   dqk, dv, oga, ogb, dm_s, dmt, qt, acc, dvt, dkt):
    length = qk.shape[1]
    heads = v.shape[2] // HEAD_DIM
    hw = heads * HEAD_DIM
    seq = pl.program_id(1)
    size = lens[seq]
    bias = key_bias(size, length)
    per = 2 * ga.shape[-2]

    dm = dot_nn(dattn[...], wo[0]).astype(BF16)
    dm_s[...] = dm
    dmt[...] = dm.T
    qt[...] = qk[0, :, pl.ds(0, hw)].T
    dvt[...] = jnp.zeros_like(dvt)
    dkt[...] = jnp.zeros_like(dkt)

    @pl.when(seq == 0)
    def _():
        acc[...] = jnp.zeros_like(acc)

    for r in range(length // chunk):
        at = pl.ds(r * chunk, chunk)
        dqs = []
        for i in range(heads):
            cols = pl.ds(i * HEAD_DIM, HEAD_DIM)
            q = qk[0, at, cols]
            key = qk[0, :, pl.ds((heads + i) * HEAD_DIM, HEAD_DIM)]
            p = jnp.exp2(dot_nt(q, key) * (SCALE * LOG2E) + bias - lse[0, at, pl.ds(i, 1)])
            g = gate_rows(ga, gb, bits, i, r * (chunk // per), chunk // per)
            w = (p * g).astype(BF16)
            dw = dot_nt(dm_s[at, cols], v[0, :, cols])
            t = dw * p
            acc[i, at, :] += t
            u = t * g
            ds = (u - p * jnp.sum(u, axis=1, keepdims=True)).astype(BF16)
            dqs.append(dot_nn(ds, key) * SCALE)
            dvt[cols, :] += dot_nn(dmt[cols, at], w)
            dkt[cols, :] += dot_nn(qt[cols, at], ds)
        dqk[0, at, pl.ds(0, hw)] = jnp.concatenate(dqs, axis=1).astype(BF16)

    dqk[0, :, pl.ds(hw, hw)] = (dkt[...] * SCALE).astype(BF16).T
    dv[0] = dvt[...].astype(BF16).T

    @pl.when(seq == pl.num_programs(1) - 1)
    def _():
        sub = per // 2
        for d in range(length // per):
            y = bits[0] ^ (d & 1)
            z1 = bits[1] ^ ((d >> 1) & 1)
            z2 = bits[2] ^ ((d >> 2) & 1)
            for i in range(heads):
                oga[0, y, z1, z2, i] = acc[i, pl.ds(d * per, sub), :].astype(oga.dtype)
                ogb[y, 0, z1, z2, i] = acc[i, pl.ds(d * per + sub, sub), :].astype(ogb.dtype)


def attention_backward(half, bits, lens, qk, v, ga, gb, lse, dattn, wo, chunk=512):
    _, rows, w2 = qk.shape
    w1 = v.shape[2]
    width = dattn.shape[1]
    count = lens.shape[0]
    length = rows // count
    heads, sub, keys = ga.shape[-3:]
    sds = jax.ShapeDtypeStruct
    off = half * 2
    gates = (2, 2, 2, 2, heads, sub, keys)
    return pl.pallas_call(
        functools.partial(att_bwd_kernel, chunk),
        out_shape=(sds((2, rows, w2), BF16), sds((2, rows, w1), BF16), sds(gates, BF16), sds(gates, BF16)),
        grid_spec=pltpu.PrefetchScalarGridSpec(
            num_scalar_prefetch=2, grid=(2, count),
            in_specs=[
                pl.BlockSpec((1, length, w2), lambda k, s, *_: (k + off, s, 0)),
                pl.BlockSpec((1, length, w1), lambda k, s, *_: (k + off, s, 0)),
                spec_a((heads, sub, keys), lambda k: k), spec_b((heads, sub, keys), lambda k: k),
                pl.BlockSpec((1, length, heads), lambda k, s, *_: (k, s, 0)),
                pl.BlockSpec((length, width), lambda k, s, *_: (s, 0)),
                pl.BlockSpec((1, width, w1), lambda k, s, *_: (k + off, 0, 0)),
            ],
            out_specs=[
                pl.BlockSpec((1, length, w2), lambda k, s, *_: (k, s, 0)),
                pl.BlockSpec((1, length, w1), lambda k, s, *_: (k, s, 0)),
                spec_a((heads, sub, keys), lambda k: k), spec_b((heads, sub, keys), lambda k: k),
            ],
            scratch_shapes=[
                pltpu.VMEM((length, w1), BF16), pltpu.VMEM((w1, length), BF16),
                pltpu.VMEM((w1, length), BF16), pltpu.VMEM((heads, length, keys), F32),
                pltpu.VMEM((w1, keys), F32), pltpu.VMEM((w1, keys), F32),
            ],
        ),
        compiler_params=params(n=2),
        cost_estimate=pl.CostEstimate(
            flops=40 * 2 * rows * length * w1, bytes_accessed=30 * rows * w1, transcendentals=0
        ),
    )(bits, lens, qk, v, ga, gb, lse, dattn, wo)


def qkv_kernel(bits, x, wa0, wa1, wb0, wb1, qk, v, wqk, wv, wo, xt, wb):
    k = pl.program_id(0)
    w2 = qk.shape[2]
    w1 = v.shape[2]

    @pl.when(k < 2)
    def _():
        assemble(wqk.at[0], wa0, bits, False)
        assemble(wb, wb0, bits, True)

    @pl.when(k >= 2)
    def _():
        assemble(wqk.at[0], wa1, bits, False)
        assemble(wb, wb1, bits, True)

    @pl.when(k == 0)
    def _():
        xt[...] = x[...].T

    wv[0] = wb[:, pl.ds(0, w1)]
    wo[0] = wb[:, pl.ds(w1, w1)]
    qk[0] = dot_nn(x[...], wqk[0]).astype(BF16)
    v[0] = dot_nn(x[...], wv[0]).astype(BF16)


def project(bits, x, wa0, wa1, wb0, wb1):
    rows, width = x.shape
    p, w2 = wa0.shape[-2:]
    w1 = w2 // 2
    sds = jax.ShapeDtypeStruct
    head = lambda s: pl.BlockSpec((1,) + s, lambda k, *_: (k, 0, 0))
    return pl.pallas_call(
        qkv_kernel,
        out_shape=(sds((4, rows, w2), BF16), sds((4, rows, w1), BF16), sds((4, width, w2), BF16),
                   sds((4, width, w1), BF16), sds((4, width, w1), BF16), sds((width, rows), BF16)),
        grid_spec=pltpu.PrefetchScalarGridSpec(
            num_scalar_prefetch=1, grid=(4,),
            in_specs=[whole((rows, width)), spec_a((p, w2), low_pick), spec_a((p, w2), high_pick),
                      spec_b((p, w2), low_pick), spec_b((p, w2), high_pick)],
            out_specs=[head((rows, w2)), head((rows, w1)), head((width, w2)), head((width, w1)), head((width, w1)),
                       whole((width, rows))],
            scratch_shapes=[pltpu.VMEM((width, w2), BF16)],
        ),
        compiler_params=params(),
        cost_estimate=pl.CostEstimate(flops=2 * rows * width * 4 * (w1 + w2), bytes_accessed=16 * rows * width, transcendentals=0),
    )(bits, x, wa0, wa1, wb0, wb1)


def out_kernel(x, m0, m1, wo, gain, bias, hid, unit, inverse, hidt):
    attn = dot_nt(m0[0], wo[0]) + dot_nt(m0[1], wo[1]) + dot_nt(m1[0], wo[2]) + dot_nt(m1[1], wo[3])
    u, inv = norm_stats(x[...].astype(F32) + attn)
    h = (u * gain[...] + bias[...]).astype(BF16)
    hid[...] = h
    hidt[...] = h.T
    unit[...] = u
    inverse[...] = inv


def out_forward(x, m0, m1, wo, gain, bias, block=256):
    rows, width = x.shape
    w1 = wo.shape[2]
    sds = jax.ShapeDtypeStruct
    row = lambda w: pl.BlockSpec((block, w), lambda r: (r, 0))
    mix = pl.BlockSpec((2, block, w1), lambda r: (0, r, 0))
    return pl.pallas_call(
        out_kernel,
        grid=(rows // block,),
        out_shape=(sds((rows, width), BF16), sds((rows, width), F32), sds((rows, 1), F32), sds((width, rows), BF16)),
        in_specs=[row(width), mix, mix, whole((4, width, w1)), whole((1, width)), whole((1, width))],
        out_specs=[row(width), row(width), row(1), pl.BlockSpec((width, block), lambda r: (0, r))],
        compiler_params=params(),
        cost_estimate=pl.CostEstimate(flops=2 * rows * width * 4 * w1, bytes_accessed=12 * rows * width, transcendentals=0),
    )(x, m0, m1, wo, gain, bias)


def qkv_grad_kernel(bits, xt, dat, dqk, dv, mixed, ga, gb, tmp):
    w1 = dv.shape[2]
    tmp[...] = dot_nn(xt[...], dqk[0]).astype(BF16)
    scatter(ga, tmp, bits, False)
    tmp[:, pl.ds(0, w1)] = dot_nn(xt[...], dv[0]).astype(BF16)
    tmp[:, pl.ds(w1, w1)] = dot_nn(dat[...], mixed[0]).astype(BF16)
    scatter(gb, tmp, bits, True)


def qkv_grads(bits, xt, dat, dqk, dv, mixed):
    width, rows = xt.shape
    w2 = dqk.shape[2]
    w1 = dv.shape[2]
    per = width // 8
    sds = jax.ShapeDtypeStruct
    pick = lambda k: k
    head = lambda w: pl.BlockSpec((1, rows, w), lambda k, *_: (k, 0, 0))
    return pl.pallas_call(
        qkv_grad_kernel,
        out_shape=(sds((2, 2, 2, 2, per, w2), BF16), sds((2, 2, 2, 2, per, w2), BF16)),
        grid_spec=pltpu.PrefetchScalarGridSpec(
            num_scalar_prefetch=1, grid=(2,),
            in_specs=[whole((width, rows)), whole((width, rows)), head(w2), head(w1), head(w1)],
            out_specs=[spec_a((per, w2), pick), spec_b((per, w2), pick)],
            scratch_shapes=[pltpu.VMEM((width, w2), BF16)],
        ),
        compiler_params=params(),
        cost_estimate=pl.CostEstimate(flops=2 * rows * width * 2 * 2 * w2, bytes_accessed=8 * rows * width, transcendentals=0),
    )(bits, xt, dat, dqk, dv, mixed)


def dinput_kernel(dfirst, dqk0, dqk1, dv0, dv1, wqk, wv, out):
    total = dfirst[...]
    for k, (a, b) in enumerate(((dqk0, dv0), (dqk0, dv0), (dqk1, dv1), (dqk1, dv1))):
        total = total + dot_nt(a[k % 2], wqk[k]) + dot_nt(b[k % 2], wv[k])
    out[...] = total


def input_backward(dfirst, dqk0, dqk1, dv0, dv1, wqk, wv, block=256):
    rows, width = dfirst.shape
    w2 = wqk.shape[2]
    w1 = wv.shape[2]
    row = pl.BlockSpec((block, width), lambda r: (r, 0))
    part = lambda w: pl.BlockSpec((2, block, w), lambda r: (0, r, 0))
    return pl.pallas_call(
        dinput_kernel,
        grid=(rows // block,),
        out_shape=jax.ShapeDtypeStruct((rows, width), F32),
        in_specs=[row, part(w2), part(w2), part(w1), part(w1), whole((4, width, w2)), whole((4, width, w1))],
        out_specs=row,
        compiler_params=params(),
        cost_estimate=pl.CostEstimate(flops=2 * rows * width * 4 * (w1 + w2), bytes_accessed=14 * rows * width, transcendentals=0),
    )(dfirst, dqk0, dqk1, dv0, dv1, wqk, wv)


GROUPS = 8


def partner_dp(value, bit):
    size = lax.axis_size("dp")
    step = (1 << bit) * (size // GROUPS)
    return lax.ppermute(value, "dp", [(i, i ^ step) for i in range(size)])


def partner_head(value, bit):
    size = lax.axis_size("head")
    return lax.ppermute(value, "head", [(i, i ^ (1 << bit)) for i in range(size)])


def over_y(value):
    return partner_dp(value, 0)


def over_near(value):
    return partner_dp(value, 1)


def over_far(value):
    return partner_dp(value, 2)


def over_pair(value):
    return partner_head(value, 0)


def over_x(value):
    return partner_head(value, 1)


def inner_groups():
    inner = lax.axis_size("dp") // GROUPS
    return inner, [[g * inner + i for i in range(inner)] for g in range(GROUPS)]


def inner_gather(value, axis):
    inner, groups = inner_groups()
    if inner == 1:
        return value
    return lax.all_gather(value, "dp", axis_index_groups=groups, axis=axis, tiled=True)


def inner_scatter(value, axis):
    inner, groups = inner_groups()
    if inner == 1:
        return value
    return lax.psum_scatter(value, "dp", axis_index_groups=groups, scatter_dimension=axis, tiled=True)


def spread(a, b):
    both = jnp.stack([a, b])
    both = jnp.stack([both, over_far(both)], axis=1)
    both = jnp.stack([both, over_near(both)], axis=1)
    a, b = both[0], both[1]
    a = jnp.stack([a, over_y(a)])
    b = jnp.stack([b, over_x(b)])
    a = jnp.stack([a, over_x(a)])
    b = jnp.stack([b, over_y(b)])
    return a, over_pair(a), b, over_pair(b)


def wide(value):
    return value.astype(F32)


def collect(a_keep, a_send, b_keep, b_send):
    ra, rb = over_pair(a_send), over_pair(b_send)
    sa = over_x((wide(a_keep[1]) + wide(ra[1])).astype(BF16))
    sb = over_y((wide(b_keep[1]) + wide(rb[1])).astype(BF16))
    ta = over_y((wide(a_keep[0, 1]) + wide(ra[0, 1]) + wide(sa[1])).astype(BF16))
    tb = over_x((wide(b_keep[0, 1]) + wide(rb[0, 1]) + wide(sb[1])).astype(BF16))
    a = wide(a_keep[0, 0]) + wide(ra[0, 0]) + wide(sa[0]) + wide(ta)
    b = wide(b_keep[0, 0]) + wide(rb[0, 0]) + wide(sb[0]) + wide(tb)
    u = over_near(jnp.stack([a[1], b[1]]).astype(BF16))
    w = over_far(jnp.stack([a[0, 1] + wide(u[0, 1]), b[0, 1] + wide(u[1, 1])]).astype(BF16))
    return a[0, 0] + wide(u[0, 0]) + wide(w[0]), b[0, 0] + wide(u[1, 0]) + wide(w[1])


def total_everywhere(value):
    for name in ("head", "dp"):
        size = lax.axis_size(name)
        step = 1
        while step < size:
            value = value + lax.ppermute(value, name, [(i, i ^ step) for i in range(size)])
            step *= 2
    return value


def per_device(layer_input, output_grad, lengths, w_qkv, w_out, w_up, w_down,
               norm_gains, norm_biases, mask_logits, mask_noise):
    micro, seq, width = layer_input.shape
    rows = micro * seq
    x = layer_input.reshape(rows, width)
    dout = output_grad.reshape(rows, width)
    place = lax.axis_index("dp") // (lax.axis_size("dp") // GROUPS)
    bits = jnp.stack([place & 1, (place >> 1) & 1, (place >> 2) & 1]).astype(jnp.int32)
    lens = lax.dynamic_slice_in_dim(lengths, lax.axis_index("head"), 1, 1).reshape(micro)

    gate_part = jax.nn.sigmoid(mask_logits + mask_noise)
    gate_all = inner_gather(gate_part.astype(BF16), 1)
    sub = gate_all.shape[1] // 2
    first = spread(
        inner_gather(jnp.concatenate([w_qkv[0], w_qkv[1]], axis=1), 0),
        inner_gather(jnp.concatenate([w_qkv[2], w_out.T], axis=1), 0),
    )
    gates = spread(gate_all[:, :sub], gate_all[:, sub:])
    ffn = spread(inner_gather(w_up, 0), inner_gather(w_down.T, 0))

    gain1, gain2 = norm_gains[0:1], norm_gains[1:2]
    bias1, bias2 = norm_biases[0:1], norm_biases[1:2]
    qk, v, wqk, wv, wo, xt = project(bits, x, *first)
    m0, lse0 = attention_forward(0, bits, lens, qk, v, gates[0], gates[2])
    m1, lse1 = attention_forward(1, bits, lens, qk, v, gates[1], gates[3])
    hid, unit, inverse, hidt = out_forward(x, m0, m1, wo, gain1, bias1)
    out, dsec, dffn, dffnt, act, gp, dgain2, dbias2 = ffn_forward(
        bits, lens, hid, *ffn, gain2, bias2, dout
    )
    up1, down1, partial = ffn_backward(False, bits, hidt, dffnt, dffn, ffn[1], ffn[3], act, gp)
    up0, down0, dfirst, dattn, dattnt, dgain1, dbias1 = ffn_backward(
        True, bits, hidt, dffnt, dffn, ffn[0], ffn[2], act, gp, (dsec, partial, unit, inverse, gain1)
    )
    up_grad, down_grad = collect(up0, up1, down0, down1)
    norms = total_everywhere(jnp.concatenate([dgain1, dgain2, dbias1, dbias2]))
    dqk1, dv1, ga1, gb1 = attention_backward(1, bits, lens, qk, v, gates[1], gates[3], lse1, dattn, wo)
    qka1, vo1 = qkv_grads(bits, xt, dattnt, dqk1, dv1, m1)
    dqk0, dv0, ga0, gb0 = attention_backward(0, bits, lens, qk, v, gates[0], gates[2], lse0, dattn, wo)
    gate_a, gate_b = collect(ga0, ga1, gb0, gb1)
    qka0, vo0 = qkv_grads(bits, xt, dattnt, dqk0, dv0, m0)
    qk_grad, vo_grad = collect(qka0, qka1, vo0, vo1)
    dinput = input_backward(dfirst, dqk0, dqk1, dv0, dv1, wqk, wv)

    qk_grad, vo_grad = inner_scatter(qk_grad, 0), inner_scatter(vo_grad, 0)
    local = vo_grad.shape[1] // 2
    gate_grad = inner_scatter(jnp.concatenate([gate_a, gate_b], axis=1), 1)
    return (
        out.reshape(micro, seq, width),
        dinput.reshape(micro, seq, width),
        jnp.stack([qk_grad[:, :local], qk_grad[:, local:], vo_grad[:, :local]]),
        vo_grad[:, local:].T,
        inner_scatter(up_grad, 0),
        inner_scatter(down_grad, 0).T,
        norms[:2],
        norms[2:],
        gate_grad * gate_part * (1.0 - gate_part),
    )


def solution(mesh):
    rows = P(None, ("dp", "head"), None)
    gates = P("head", "dp", None)
    weights = (P(None, "dp", "head"), P("head", "dp"), P("dp", "head"), P("head", "dp"))
    return jax.shard_map(
        per_device,
        mesh=mesh,
        in_specs=(rows, rows, P(None, "dp")) + weights + (P(), P(), gates, gates),
        out_specs=(rows, rows) + weights + (P(), P(), gates),
        check_vma=False,
    )
```

```python
import functools, math
import jax, jax.numpy as jnp
from jax import lax
from jax.experimental import pallas as pl
from jax.experimental.pallas import tpu as pltpu
from jax.sharding import PartitionSpec as P

HEAD_DIM = 64
EPS = 1e-05
F32 = jnp.float32
BF16 = jnp.bfloat16
SCALE = 1.0 / math.sqrt(HEAD_DIM)
LOG2E = math.log2(math.e)
NEG = -1e30
INV_SQRT2 = 1.0 / math.sqrt(2.0)
INV_SQRT2PI = 1.0 / math.sqrt(2.0 * math.pi)


def dot_nn(a, b):
    return lax.dot_general(a, b, (((1,), (0,)), ((), ())), preferred_element_type=F32)


def dot_nt(a, b):
    return lax.dot_general(a, b, (((1,), (1,)), ((), ())), preferred_element_type=F32)


def dot_tn(a, b):
    return lax.dot_general(a, b, (((0,), (0,)), ((), ())), preferred_element_type=F32)


def piece(ref, bits, d, flip):
    y = bits[0] ^ (d & 1)
    z1 = bits[1] ^ ((d >> 1) & 1)
    z2 = bits[2] ^ ((d >> 2) & 1)
    if flip:
        return ref.at[y, 0, z1, z2]
    return ref.at[0, y, z1, z2]


def assemble(dst, ref, bits, flip):
    rows = ref.shape[-2]
    for d in range(8):
        dst[pl.ds(d * rows, rows), :] = piece(ref, bits, d, flip)[...]


def scatter(ref, src, bits, flip):
    rows = ref.shape[-2]
    for d in range(8):
        piece(ref, bits, d, flip)[...] = src[pl.ds(d * rows, rows), :]


def spec_a(tail, pick):
    zeros = (0,) * len(tail)
    return pl.BlockSpec((1, 2, 2, 2) + tail, lambda k, *_: (pick(k), 0, 0, 0) + zeros)


def spec_b(tail, pick):
    zeros = (0,) * len(tail)
    return pl.BlockSpec((2, 1, 2, 2) + tail, lambda k, *_: (0, pick(k), 0, 0) + zeros)


def whole(shape):
    zeros = (0,) * len(shape)
    return pl.BlockSpec(shape, lambda *_: zeros)


def low_pick(k):
    return jnp.minimum(k, 1)


def high_pick(k):
    return jnp.maximum(k - 2, 0)


def norm_stats(z):
    mean = jnp.mean(z, axis=1, keepdims=True)
    centered = z - mean
    inverse = lax.rsqrt(jnp.mean(centered * centered, axis=1, keepdims=True) + EPS)
    return centered * inverse, inverse


def norm_back(du, unit, inverse):
    return inverse * (
        du
        - jnp.mean(du, axis=1, keepdims=True)
        - unit * jnp.mean(du * unit, axis=1, keepdims=True)
    )


def gelu_pair(up):
    cdf = 0.5 + 0.5 * lax.erf(up * INV_SQRT2)
    pdf = INV_SQRT2PI * jnp.exp(-0.5 * (up * up))
    return up * cdf, cdf + up * pdf


def params(mib=56, n=1):
    return pltpu.CompilerParams(
        dimension_semantics=("arbitrary",) * n, vmem_limit_bytes=mib * 1024 * 1024
    )


def ffn_fwd_kernel(chunk, last, bits, lens, hid, ua, db, *rest):
    if last:
        part, gain, bias, dout, act_o, gp_o, out, dsec, dffn, dffnt, dgain, dbias, wu, wd, acc = rest
    else:
        act_o, gp_o, acc, wu, wd = rest
    k = pl.program_id(0)
    rows = hid.shape[0]

    assemble(wu, ua, bits, False)
    assemble(wd, db, bits, True)

    @pl.when(k == 0)
    def _():
        if last:
            acc[...] = part[...] + hid[...].astype(F32)
        else:
            acc[...] = jnp.zeros_like(acc)

    for r in range(rows // chunk):
        at = pl.ds(r * chunk, chunk)
        act, gp = gelu_pair(dot_nn(hid[at, :], wu[...]))
        act = act.astype(BF16)
        act_o[0, at, :] = act
        gp_o[0, at, :] = gp.astype(gp_o.dtype)
        acc[at, :] += dot_nt(act, wd[...])

    if last:

        @pl.when(k == 1)
        def _():
            dgain[...] = jnp.zeros_like(dgain)
            dbias[...] = jnp.zeros_like(dbias)
            length = rows // lens.shape[0]
            small = 128

            def fin(r, c):
                start = pl.multiple_of(r * small, small)
                at = pl.ds(start, small)
                size = lens[start // length]
                pos = (start % length) + lax.broadcasted_iota(jnp.int32, (small, 1), 0)
                valid = pos < size
                unit, inverse = norm_stats(acc[at, :])
                g = gain[...]
                out[at, :] = jnp.where(valid, unit * g + bias[...], 0.0).astype(BF16)
                dy = jnp.where(valid, dout[at, :].astype(F32), 0.0)
                dgain[...] += jnp.sum(dy * unit, axis=0, keepdims=True)
                dbias[...] += jnp.sum(dy, axis=0, keepdims=True)
                dz = norm_back(dy * g, unit, inverse)
                dsec[at, :] = dz
                low = dz.astype(BF16)
                dffn[at, :] = low
                dffnt[:, at] = low.T
                return c

            lax.fori_loop(0, rows // small, fin, 0)


def ffn_forward(last, bits, lens, hid, ua, db, extra=(), chunk=512, gp_dt=F32):
    rows, width = hid.shape
    n = ua.shape[-1]
    p = ua.shape[-2]
    sds = jax.ShapeDtypeStruct
    pick = lambda k: k
    full = whole((rows, width))
    line = whole((1, width))
    unit = pl.BlockSpec((1, rows, n), lambda k, *_: (k, 0, 0))
    in_specs = [full, spec_a((p, n), pick), spec_b((p, n), pick)]
    out_shape = [sds((2, rows, n), BF16), sds((2, rows, n), gp_dt)]
    out_specs = [unit, unit]
    scratch = [pltpu.VMEM((width, n), BF16), pltpu.VMEM((width, n), BF16)]
    if last:
        in_specs += [full, line, line, full]
        out_shape += [sds((rows, width), BF16), sds((rows, width), F32), sds((rows, width), BF16),
                      sds((width, rows), BF16), sds((1, width), F32), sds((1, width), F32)]
        out_specs += [full, full, full, whole((width, rows)), line, line]
        scratch += [pltpu.VMEM((rows, width), F32)]
    else:
        out_shape += [sds((rows, width), F32)]
        out_specs += [full]
    return pl.pallas_call(
        functools.partial(ffn_fwd_kernel, chunk, last),
        out_shape=out_shape,
        grid_spec=pltpu.PrefetchScalarGridSpec(
            num_scalar_prefetch=2, grid=(2,), in_specs=in_specs, out_specs=out_specs, scratch_shapes=scratch,
        ),
        compiler_params=params(),
        cost_estimate=pl.CostEstimate(
            flops=4 * rows * width * 2 * n, bytes_accessed=24 * rows * width, transcendentals=0
        ),
    )(bits, lens, hid, ua, db, *extra)


def ffn_bwd_kernel(chunk, last, bits, ht, dt, dffn, ua, db, act, gp, *rest):
    if last:
        dsec, part, unit, inverse, gain, gu, gd, dfirst, dattn, dattnt, dgain, dbias, wu, wd, dup_s, acc, tmp = rest
    else:
        gu, gd, dh_o, wu, wd, dup_s, acc, tmp = rest
    k = pl.program_id(0)
    rows, width = dffn.shape

    assemble(wu, ua, bits, False)
    assemble(wd, db, bits, True)

    @pl.when(k == 0)
    def _():
        if last:
            acc[...] = part[...] + dsec[...]
        else:
            acc[...] = jnp.zeros_like(acc)

    def step(r, c):
        at = pl.ds(pl.multiple_of(r * chunk, chunk), chunk)
        dact = dot_nn(dffn[at, :], wd[...])
        dup = (dact * gp[0, at, :].astype(F32)).astype(BF16)
        dup_s[at, :] = dup
        acc[at, :] += dot_nt(dup, wu[...])
        return c

    lax.fori_loop(0, rows // chunk, step, 0)

    tmp[...] = dot_nn(ht[...], dup_s[...]).astype(BF16)
    scatter(gu, tmp, bits, False)
    tmp[...] = dot_nn(dt[...], act[0]).astype(BF16)
    scatter(gd, tmp, bits, True)

    @pl.when(k == 1)
    def _():
        if not last:
            dh_o[...] = acc[...]
        else:
            dgain[...] = jnp.zeros_like(dgain)
            dbias[...] = jnp.zeros_like(dbias)
            small = 128

            def fin(r, c):
                at = pl.ds(pl.multiple_of(r * small, small), small)
                dh = acc[at, :]
                u = unit[at, :]
                dgain[...] += jnp.sum(dh * u, axis=0, keepdims=True)
                dbias[...] += jnp.sum(dh, axis=0, keepdims=True)
                dz = norm_back(dh * gain[...], u, inverse[at, :])
                dfirst[at, :] = dz
                low = dz.astype(BF16)
                dattn[at, :] = low
                dattnt[:, at] = low.T
                return c

            lax.fori_loop(0, rows // small, fin, 0)


def ffn_backward(last, bits, ht, dt, dffn, ua, db, act, gp, extra=(), chunk=512):
    rows, width = dffn.shape
    n = ua.shape[-1]
    p = ua.shape[-2]
    sds = jax.ShapeDtypeStruct
    pick = lambda k: k
    out_shape = [sds((2, 2, 2, 2, p, n), BF16), sds((2, 2, 2, 2, p, n), BF16)]
    out_specs = [spec_a((p, n), pick), spec_b((p, n), pick)]
    in_specs = [
        whole((width, rows)), whole((width, rows)), whole((rows, width)),
        spec_a((p, n), pick), spec_b((p, n), pick),
        pl.BlockSpec((1, rows, n), lambda k, *_: (k, 0, 0)),
        pl.BlockSpec((1, rows, n), lambda k, *_: (k, 0, 0)),
    ]
    if last:
        in_specs += [whole((rows, width))] * 3 + [whole((rows, 1)), whole((1, width))]
        out_shape += [sds((rows, width), F32), sds((rows, width), BF16), sds((width, rows), BF16), sds((1, width), F32), sds((1, width), F32)]
        out_specs += [whole((rows, width))] * 2 + [whole((width, rows))] + [whole((1, width))] * 2
    else:
        out_shape += [sds((rows, width), F32)]
        out_specs += [whole((rows, width))]
    return pl.pallas_call(
        functools.partial(ffn_bwd_kernel, chunk, last),
        out_shape=out_shape,
        grid_spec=pltpu.PrefetchScalarGridSpec(
            num_scalar_prefetch=1, grid=(2,), in_specs=in_specs, out_specs=out_specs,
            scratch_shapes=[
                pltpu.VMEM((width, n), BF16), pltpu.VMEM((width, n), BF16),
                pltpu.VMEM((rows, n), BF16), pltpu.VMEM((rows, width), F32),
                pltpu.VMEM((width, n), BF16),
            ],
        ),
        compiler_params=params(),
        cost_estimate=pl.CostEstimate(
            flops=8 * rows * width * 2 * n, bytes_accessed=30 * rows * width, transcendentals=0
        ),
    )(bits, ht, dt, dffn, ua, db, act, gp, *extra)


def key_bias(size, length):
    pos = lax.broadcasted_iota(jnp.int32, (1, length), 1)
    return jnp.where(pos < size, 0.0, NEG).astype(F32)


def gate_rows(ga, gb, bits, i, d0, count):
    parts = []
    for j in range(count):
        d = d0 + j
        y = bits[0] ^ (d & 1)
        z1 = bits[1] ^ ((d >> 1) & 1)
        z2 = bits[2] ^ ((d >> 2) & 1)
        parts.append(ga[0, y, z1, z2, i])
        parts.append(gb[y, 0, z1, z2, i])
    return jnp.concatenate(parts, axis=0).astype(F32)


def att_fwd_kernel(bits, lens, qk, v, ga, gb, mixed, lse):
    length = qk.shape[1]
    heads = v.shape[2] // HEAD_DIM
    bias = key_bias(lens[pl.program_id(1)], length)
    count = length // (2 * ga.shape[-2])
    cols = [pl.ds(i * HEAD_DIM, HEAD_DIM) for i in range(2 * heads)]

    def score(i):
        return dot_nt(qk[0, :, cols[i]], qk[0, :, cols[heads + i]])

    ahead = score(0)
    outs = []
    stats = []
    for i in range(heads):
        s = ahead * (SCALE * LOG2E) + bias
        if i + 1 < heads:
            ahead = score(i + 1)
        top = jnp.max(s, axis=1, keepdims=True)
        e = jnp.exp2(s - top)
        total = jnp.sum(e, axis=1, keepdims=True)
        w = (e * gate_rows(ga, gb, bits, i, 0, count)).astype(BF16)
        outs.append(dot_nn(w, v[0, :, cols[i]]) * (1.0 / total))
        stats.append(top + jnp.log2(total))
    mixed[0] = jnp.concatenate(outs, axis=1).astype(BF16)
    lse[0] = jnp.concatenate(stats, axis=1)


def attention_forward(bits, lens, qk, v, ga, gb):
    _, rows, w2 = qk.shape
    w1 = v.shape[2]
    count = lens.shape[0]
    length = rows // count
    heads, sub, keys = ga.shape[-3:]
    sds = jax.ShapeDtypeStruct
    return pl.pallas_call(
        att_fwd_kernel,
        out_shape=(sds((2, rows, w1), BF16), sds((2, rows, heads), F32)),
        grid_spec=pltpu.PrefetchScalarGridSpec(
            num_scalar_prefetch=2, grid=(2, count),
            in_specs=[
                pl.BlockSpec((1, length, w2), lambda k, s, *_: (k, s, 0)),
                pl.BlockSpec((1, length, w1), lambda k, s, *_: (k, s, 0)),
                spec_a((heads, sub, keys), lambda k: k), spec_b((heads, sub, keys), lambda k: k),
            ],
            out_specs=[
                pl.BlockSpec((1, length, w1), lambda k, s, *_: (k, s, 0)),
                pl.BlockSpec((1, length, heads), lambda k, s, *_: (k, s, 0)),
            ],
        ),
        compiler_params=params(n=2),
        cost_estimate=pl.CostEstimate(
            flops=16 * 2 * rows * length * w1, bytes_accessed=16 * rows * w1, transcendentals=0
        ),
    )(bits, lens, qk, v, ga, gb)


def att_bwd_kernel(bits, lens, qk, v, ga, gb, lse, dattn, wo,
                   dqk, dv, oga, ogb, dm_s, dmt, qt, acc):
    length = qk.shape[1]
    heads = v.shape[2] // HEAD_DIM
    hw = heads * HEAD_DIM
    seq = pl.program_id(1)
    bias = key_bias(lens[seq], length)
    sub = ga.shape[-2]
    count = length // (2 * sub)
    cols = [pl.ds(i * HEAD_DIM, HEAD_DIM) for i in range(2 * heads)]

    dm = dot_nn(dattn[...], wo[0]).astype(BF16)
    dm_s[...] = dm
    dmt[...] = dm.T
    qt[...] = qk[0, :, pl.ds(0, hw)].T

    def products(i):
        return (
            dot_nt(qk[0, :, cols[i]], qk[0, :, cols[heads + i]]),
            dot_nt(dm_s[:, cols[i]], v[0, :, cols[i]]),
        )

    ahead = products(0)
    dqs, dks, dvs = [], [], []
    for i in range(heads):
        s, dw = ahead
        p = jnp.exp2(s * (SCALE * LOG2E) + bias - lse[0, :, pl.ds(i, 1)])
        if i + 1 < heads:
            ahead = products(i + 1)
        g = gate_rows(ga, gb, bits, i, 0, count)
        w = (p * g).astype(BF16)
        t = dw * p
        acc[i] = t + jnp.where(seq == 0, 0.0, acc[i])
        u = t * g
        ds = (u - p * jnp.sum(u, axis=1, keepdims=True)).astype(BF16)
        dqs.append(dot_nn(ds, qk[0, :, cols[heads + i]]) * SCALE)
        dvs.append(dot_nn(dmt[cols[i], :], w).astype(BF16).T)
        dks.append((dot_nn(qt[cols[i], :], ds) * SCALE).astype(BF16).T)
    dqk[0] = jnp.concatenate([d.astype(BF16) for d in dqs] + dks, axis=1)
    dv[0] = jnp.concatenate(dvs, axis=1)

    @pl.when(seq == pl.num_programs(1) - 1)
    def _():
        for d in range(count):
            y = bits[0] ^ (d & 1)
            z1 = bits[1] ^ ((d >> 1) & 1)
            z2 = bits[2] ^ ((d >> 2) & 1)
            for i in range(heads):
                oga[0, y, z1, z2, i] = acc[i, pl.ds(d * 2 * sub, sub), :].astype(oga.dtype)
                ogb[y, 0, z1, z2, i] = acc[i, pl.ds(d * 2 * sub + sub, sub), :].astype(ogb.dtype)


def attention_backward(bits, lens, qk, v, ga, gb, lse, dattn, wo):
    _, rows, w2 = qk.shape
    w1 = v.shape[2]
    width = dattn.shape[1]
    count = lens.shape[0]
    length = rows // count
    heads, sub, keys = ga.shape[-3:]
    sds = jax.ShapeDtypeStruct
    gates = (2, 2, 2, 2, heads, sub, keys)
    return pl.pallas_call(
        att_bwd_kernel,
        out_shape=(sds((2, rows, w2), BF16), sds((2, rows, w1), BF16), sds(gates, BF16), sds(gates, BF16)),
        grid_spec=pltpu.PrefetchScalarGridSpec(
            num_scalar_prefetch=2, grid=(2, count),
            in_specs=[
                pl.BlockSpec((1, length, w2), lambda k, s, *_: (k, s, 0)),
                pl.BlockSpec((1, length, w1), lambda k, s, *_: (k, s, 0)),
                spec_a((heads, sub, keys), lambda k: k), spec_b((heads, sub, keys), lambda k: k),
                pl.BlockSpec((1, length, heads), lambda k, s, *_: (k, s, 0)),
                pl.BlockSpec((length, width), lambda k, s, *_: (s, 0)),
                pl.BlockSpec((1, width, w1), lambda k, s, *_: (k, 0, 0)),
            ],
            out_specs=[
                pl.BlockSpec((1, length, w2), lambda k, s, *_: (k, s, 0)),
                pl.BlockSpec((1, length, w1), lambda k, s, *_: (k, s, 0)),
                spec_a((heads, sub, keys), lambda k: k), spec_b((heads, sub, keys), lambda k: k),
            ],
            scratch_shapes=[
                pltpu.VMEM((length, w1), BF16), pltpu.VMEM((w1, length), BF16),
                pltpu.VMEM((w1, length), BF16), pltpu.VMEM((heads, length, keys), F32),
            ],
        ),
        compiler_params=params(n=2),
        cost_estimate=pl.CostEstimate(
            flops=40 * 2 * rows * length * w1, bytes_accessed=30 * rows * w1, transcendentals=0
        ),
    )(bits, lens, qk, v, ga, gb, lse, dattn, wo)


def qkv_kernel(first, bits, x, wa, wb, qk, v, wqk, wv, wo, *rest):
    w1 = v.shape[2]
    wb_s = rest[-1]
    assemble(wqk.at[0], wa, bits, False)
    assemble(wb_s, wb, bits, True)

    if first:

        @pl.when(pl.program_id(0) == 0)
        def _():
            rest[0][...] = x[...].T

    wv[0] = wb_s[:, pl.ds(0, w1)]
    wo[0] = wb_s[:, pl.ds(w1, w1)]
    qk[0] = dot_nn(x[...], wqk[0]).astype(BF16)
    v[0] = dot_nn(x[...], wv[0]).astype(BF16)


def project(first, bits, x, wa, wb):
    rows, width = x.shape
    p, w2 = wa.shape[-2:]
    w1 = w2 // 2
    sds = jax.ShapeDtypeStruct
    pick = lambda k: k
    head = lambda s: pl.BlockSpec((1,) + s, lambda k, *_: (k, 0, 0))
    return pl.pallas_call(
        functools.partial(qkv_kernel, first),
        out_shape=[sds((2, rows, w2), BF16), sds((2, rows, w1), BF16), sds((2, width, w2), BF16),
                   sds((2, width, w1), BF16), sds((2, width, w1), BF16)]
        + ([sds((width, rows), BF16)] if first else []),
        grid_spec=pltpu.PrefetchScalarGridSpec(
            num_scalar_prefetch=1, grid=(2,),
            in_specs=[whole((rows, width)), spec_a((p, w2), pick), spec_b((p, w2), pick)],
            out_specs=[head((rows, w2)), head((rows, w1)), head((width, w2)), head((width, w1)), head((width, w1))]
            + ([whole((width, rows))] if first else []),
            scratch_shapes=[pltpu.VMEM((width, w2), BF16)],
        ),
        compiler_params=params(),
        cost_estimate=pl.CostEstimate(flops=2 * rows * width * 2 * (w1 + w2), bytes_accessed=8 * rows * width, transcendentals=0),
    )(bits, x, wa, wb)


def out_kernel(x, m0, m1, wo0, wo1, gain, bias, hid, unit, inverse, hidt):
    attn = dot_nt(m0[0], wo0[0]) + dot_nt(m0[1], wo0[1]) + dot_nt(m1[0], wo1[0]) + dot_nt(m1[1], wo1[1])
    u, inv = norm_stats(x[...].astype(F32) + attn)
    h = (u * gain[...] + bias[...]).astype(BF16)
    hid[...] = h
    hidt[...] = h.T
    unit[...] = u
    inverse[...] = inv


def out_forward(x, m0, m1, wo0, wo1, gain, bias, block=256):
    rows, width = x.shape
    w1 = wo0.shape[2]
    sds = jax.ShapeDtypeStruct
    row = lambda w: pl.BlockSpec((block, w), lambda r: (r, 0))
    mix = pl.BlockSpec((2, block, w1), lambda r: (0, r, 0))
    return pl.pallas_call(
        out_kernel,
        grid=(rows // block,),
        out_shape=(sds((rows, width), BF16), sds((rows, width), F32), sds((rows, 1), F32), sds((width, rows), BF16)),
        in_specs=[row(width), mix, mix, whole((2, width, w1)), whole((2, width, w1)), whole((1, width)), whole((1, width))],
        out_specs=[row(width), row(width), row(1), pl.BlockSpec((width, block), lambda r: (0, r))],
        compiler_params=params(),
        cost_estimate=pl.CostEstimate(flops=2 * rows * width * 4 * w1, bytes_accessed=12 * rows * width, transcendentals=0),
    )(x, m0, m1, wo0, wo1, gain, bias)


def qkv_grad_kernel(bits, xt, dat, dqk, dv, mixed, ga, gb, tmp):
    w1 = dv.shape[2]
    tmp[...] = dot_nn(xt[...], dqk[0]).astype(BF16)
    scatter(ga, tmp, bits, False)
    tmp[:, pl.ds(0, w1)] = dot_nn(xt[...], dv[0]).astype(BF16)
    tmp[:, pl.ds(w1, w1)] = dot_nn(dat[...], mixed[0]).astype(BF16)
    scatter(gb, tmp, bits, True)


def qkv_grads(bits, xt, dat, dqk, dv, mixed):
    width, rows = xt.shape
    w2 = dqk.shape[2]
    w1 = dv.shape[2]
    per = width // 8
    sds = jax.ShapeDtypeStruct
    pick = lambda k: k
    head = lambda w: pl.BlockSpec((1, rows, w), lambda k, *_: (k, 0, 0))
    return pl.pallas_call(
        qkv_grad_kernel,
        out_shape=(sds((2, 2, 2, 2, per, w2), BF16), sds((2, 2, 2, 2, per, w2), BF16)),
        grid_spec=pltpu.PrefetchScalarGridSpec(
            num_scalar_prefetch=1, grid=(2,),
            in_specs=[whole((width, rows)), whole((width, rows)), head(w2), head(w1), head(w1)],
            out_specs=[spec_a((per, w2), pick), spec_b((per, w2), pick)],
            scratch_shapes=[pltpu.VMEM((width, w2), BF16)],
        ),
        compiler_params=params(),
        cost_estimate=pl.CostEstimate(flops=2 * rows * width * 2 * 2 * w2, bytes_accessed=8 * rows * width, transcendentals=0),
    )(bits, xt, dat, dqk, dv, mixed)


def dinput_kernel(dfirst, dqk0, dqk1, dv0, dv1, wqk0, wqk1, wv0, wv1, out):
    total = dfirst[...]
    for a, b, wa, wb in ((dqk0, dv0, wqk0, wv0), (dqk1, dv1, wqk1, wv1)):
        for k in range(2):
            total = total + dot_nt(a[k], wa[k]) + dot_nt(b[k], wb[k])
    out[...] = total


def input_backward(dfirst, dqk0, dqk1, dv0, dv1, wqk0, wqk1, wv0, wv1, block=256):
    rows, width = dfirst.shape
    w2 = wqk0.shape[2]
    w1 = wv0.shape[2]
    row = pl.BlockSpec((block, width), lambda r: (r, 0))
    part = lambda w: pl.BlockSpec((2, block, w), lambda r: (0, r, 0))
    return pl.pallas_call(
        dinput_kernel,
        grid=(rows // block,),
        out_shape=jax.ShapeDtypeStruct((rows, width), F32),
        in_specs=[row, part(w2), part(w2), part(w1), part(w1)]
        + [whole((2, width, w2))] * 2 + [whole((2, width, w1))] * 2,
        out_specs=row,
        compiler_params=params(),
        cost_estimate=pl.CostEstimate(flops=2 * rows * width * 4 * (w1 + w2), bytes_accessed=14 * rows * width, transcendentals=0),
    )(dfirst, dqk0, dqk1, dv0, dv1, wqk0, wqk1, wv0, wv1)


GROUPS = 8


def partner_dp(value, bit):
    size = lax.axis_size("dp")
    step = (1 << bit) * (size // GROUPS)
    return lax.ppermute(value, "dp", [(i, i ^ step) for i in range(size)])


def partner_head(value, bit):
    size = lax.axis_size("head")
    return lax.ppermute(value, "head", [(i, i ^ (1 << bit)) for i in range(size)])


def over_y(value):
    return partner_dp(value, 0)


def over_near(value):
    return partner_dp(value, 1)


def over_far(value):
    return partner_dp(value, 2)


def over_pair(value):
    return partner_head(value, 0)


def over_x(value):
    return partner_head(value, 1)


def inner_groups():
    inner = lax.axis_size("dp") // GROUPS
    return inner, [[g * inner + i for i in range(inner)] for g in range(GROUPS)]


def inner_gather(value, axis):
    inner, groups = inner_groups()
    if inner == 1:
        return value
    return lax.all_gather(value, "dp", axis_index_groups=groups, axis=axis, tiled=True)


def inner_scatter(value, axis):
    inner, groups = inner_groups()
    if inner == 1:
        return value
    return lax.psum_scatter(value, "dp", axis_index_groups=groups, scatter_dimension=axis, tiled=True)


def after(values, *waits):
    return lax.optimization_barrier((tuple(values), waits))[0]


def wide(value):
    return value.astype(F32)


def first_sum(keep, got):
    return (wide(keep[1]) + wide(got[1])).astype(BF16)


def second_sum(keep, got, more):
    return (wide(keep[0, 1]) + wide(got[0, 1]) + wide(more[1])).astype(BF16)


def third_sum(keep, got, more, last):
    return wide(keep[0, 0]) + wide(got[0, 0]) + wide(more[0]) + wide(last)


def total_steps():
    steps = []
    for name in ("head", "dp"):
        size = lax.axis_size(name)
        step = 1
        while step < size:
            steps.append((name, [(i, i ^ step) for i in range(size)]))
            step *= 2
    return steps


def total_some(value, *steps):
    for name, pairs in steps:
        value = value + lax.ppermute(value, name, pairs)
    return value


def per_device(layer_input, output_grad, lengths, w_qkv, w_out, w_up, w_down,
               norm_gains, norm_biases, mask_logits, mask_noise):
    micro, seq, width = layer_input.shape
    rows = micro * seq
    x = layer_input.reshape(rows, width)
    dout = output_grad.reshape(rows, width)
    place = lax.axis_index("dp") // (lax.axis_size("dp") // GROUPS)
    bits = jnp.stack([place & 1, (place >> 1) & 1, (place >> 2) & 1]).astype(jnp.int32)
    lens = lax.dynamic_slice_in_dim(lengths, lax.axis_index("head"), 1, 1).reshape(micro)

    gate_part = jax.nn.sigmoid(mask_logits + mask_noise)
    gate_all = inner_gather(gate_part.astype(BF16), 1)
    sub = gate_all.shape[1] // 2
    gain1, gain2 = norm_gains[0:1], norm_gains[1:2]
    bias1, bias2 = norm_biases[0:1], norm_biases[1:2]

    ga = jnp.stack([
        inner_gather(jnp.concatenate([w_qkv[0], w_qkv[1]], axis=1), 0),
        inner_gather(jnp.concatenate([w_qkv[2], w_out.T], axis=1), 0),
    ])
    gb = jnp.stack([gate_all[:, :sub], gate_all[:, sub:]])
    gc = jnp.stack([inner_gather(w_up, 0), inner_gather(w_down.T, 0)])

    got = over_far(ga)
    ga = jnp.stack([ga, got], axis=1)
    got = over_near(ga)
    ga = jnp.stack([ga, got], axis=1)
    aa, ab = ga[0], ga[1]
    (gb,) = after((gb,), got)
    ra, rb = over_y(aa), over_x(ab)
    far_b = over_far(gb)
    aa, ab = jnp.stack([aa, ra]), jnp.stack([ab, rb])
    gb, = after((gb,), ra, rb)
    gb = jnp.stack([gb, far_b], axis=1)
    aa, ab = after((aa, ab), gb)
    ra, rb = over_x(aa), over_y(ab)
    near_b = over_near(gb)
    (gc,) = after((gc,), near_b)
    far_c = over_far(gc)
    gb = jnp.stack([gb, near_b], axis=1)
    ba, bb = gb[0], gb[1]
    aa, ab = jnp.stack([aa, ra]), jnp.stack([ab, rb])
    ba, bb = after((ba, bb), ra, rb)
    ca, cb = over_pair(aa), over_pair(ab)
    ra, rb = over_y(ba), over_x(bb)
    qk0, v0, wqk0, wv0, wo0, xt = project(True, bits, x, aa, ab)
    ca, cb = after((ca, cb), qk0)
    qk1, v1, wqk1, wv1, wo1 = project(False, bits, x, ca, cb)
    ba, bb = jnp.stack([ba, ra]), jnp.stack([bb, rb])
    ba, bb, gc = after((ba, bb, gc), qk1)
    ra, rb = over_x(ba), over_y(bb)
    gc = jnp.stack([gc, far_c], axis=1)
    near_c = over_near(gc)
    ba, bb = jnp.stack([ba, ra]), jnp.stack([bb, rb])
    gc = jnp.stack([gc, near_c], axis=1)
    fa, fb = gc[0], gc[1]
    fa, fb, ba, bb = after((fa, fb, ba, bb), ra, rb, near_c)
    ba1, bb1 = over_pair(ba), over_pair(bb)
    ra, rb = over_y(fa), over_x(fb)
    m0, lse0 = attention_forward(bits, lens, qk0, v0, ba, bb)
    fa, fb = jnp.stack([fa, ra]), jnp.stack([fb, rb])
    fa, fb, ba1, bb1 = after((fa, fb, ba1, bb1), m0)
    ra, rb = over_x(fa), over_y(fb)
    m1, lse1 = attention_forward(bits, lens, qk1, v1, ba1, bb1)
    hid, unit, inverse, hidt = out_forward(x, m0, m1, wo0, wo1, gain1, bias1)
    fa, fb = jnp.stack([fa, ra]), jnp.stack([fb, rb])
    fa, fb = after((fa, fb), hid)
    fa1, fb1 = over_pair(fa), over_pair(fb)
    act0, gp0, part = ffn_forward(False, bits, lens, hid, fa, fb)
    act1, gp1, out, dsec, dffn, dffnt, dgain2, dbias2 = ffn_forward(
        True, bits, lens, hid, fa1, fb1, (part, gain2, bias2, dout)
    )

    up1, down1, part = ffn_backward(False, bits, hidt, dffnt, dffn, fa1, fb1, act1, gp1)
    cu, cd = over_pair(up1), over_pair(down1)
    dffn, part = after((dffn, part), up1)
    up0, down0, dfirst, dattn, dattnt, dgain1, dbias1 = ffn_backward(
        True, bits, hidt, dffnt, dffn, fa, fb, act0, gp0, (dsec, part, unit, inverse, gain1)
    )
    up0, down0, cu, cd, norms = after(
        (up0, down0, cu, cd, jnp.concatenate([dgain1, dgain2, dbias1, dbias2])), dattn
    )
    steps = total_steps()
    xu, xd = over_x(first_sum(up0, cu)), over_y(first_sum(down0, cd))
    norms = total_some(norms, steps[0])
    dqk1, dv1, ga1, gb1 = attention_backward(bits, lens, qk1, v1, ba1, bb1, lse1, dattn, wo1)
    ga1, gb1, norms, dqk1, xu, xd = after((ga1, gb1, norms, dqk1, xu, xd), dv1)
    cga, cgb = over_pair(ga1), over_pair(gb1)
    norms = total_some(norms, steps[3])
    yu, yd = over_y(second_sum(up0, cu, xu)), over_x(second_sum(down0, cd, xd))
    qka1, vo1 = qkv_grads(bits, xt, dattnt, dqk1, dv1, m1)
    qka1, vo1, dattn, norms = after((qka1, vo1, dattn, norms), cga, cgb)
    cqk, cvo = over_pair(qka1), over_pair(vo1)
    norms = total_some(norms, steps[4])
    dqk0, dv0, ga0, gb0 = attention_backward(bits, lens, qk0, v0, ba, bb, lse0, dattn, wo0)
    ga0, gb0, cga, cgb, yu, yd, dqk0, norms = after((ga0, gb0, cga, cgb, yu, yd, dqk0, norms), dv0, cqk, cvo)
    xga, xgb = over_x(first_sum(ga0, cga)), over_y(first_sum(gb0, cgb))
    u, d = third_sum(up0, cu, xu, yu), third_sum(down0, cd, xd, yd)
    near_f = over_near(jnp.stack([u[1], d[1]]).astype(BF16))
    qka0, vo0 = qkv_grads(bits, xt, dattnt, dqk0, dv0, m0)
    qka0, vo0, near_f, xga, xgb, dqk0 = after((qka0, vo0, near_f, xga, xgb, dqk0), vo0)
    xqk, xvo = over_x(first_sum(qka0, cqk)), over_y(first_sum(vo0, cvo))
    yga, ygb = over_y(second_sum(ga0, cga, xga)), over_x(second_sum(gb0, cgb, xgb))
    far_f = over_far(jnp.stack([u[0, 1] + wide(near_f[0, 1]), d[0, 1] + wide(near_f[1, 1])]).astype(BF16))
    dinput = input_backward(dfirst, dqk0, dqk1, dv0, dv1, wqk0, wqk1, wv0, wv1)
    xqk, xvo, yga, ygb, norms = after((xqk, xvo, yga, ygb, norms), dinput)
    yqk, yvo = over_y(second_sum(qka0, cqk, xqk)), over_x(second_sum(vo0, cvo, xvo))
    g1, g2 = third_sum(ga0, cga, xga, yga), third_sum(gb0, cgb, xgb, ygb)
    near_g = over_near(jnp.stack([g1[1], g2[1]]).astype(BF16))
    norms, = after((norms,), yqk, yvo)
    norms = total_some(norms, steps[1])
    w1, w2 = third_sum(qka0, cqk, xqk, yqk), third_sum(vo0, cvo, xvo, yvo)
    near_w = over_near(jnp.stack([w1[1], w2[1]]).astype(BF16))
    far_g = over_far(jnp.stack([g1[0, 1] + wide(near_g[0, 1]), g2[0, 1] + wide(near_g[1, 1])]).astype(BF16))
    norms, = after((norms,), near_w)
    norms = total_some(norms, *steps[2:3], *steps[5:])
    far_w = over_far(jnp.stack([w1[0, 1] + wide(near_w[0, 1]), w2[0, 1] + wide(near_w[1, 1])]).astype(BF16))

    up_grad = u[0, 0] + wide(near_f[0, 0]) + wide(far_f[0])
    down_grad = d[0, 0] + wide(near_f[1, 0]) + wide(far_f[1])
    gate_a = g1[0, 0] + wide(near_g[0, 0]) + wide(far_g[0])
    gate_b = g2[0, 0] + wide(near_g[1, 0]) + wide(far_g[1])
    qk_grad = w1[0, 0] + wide(near_w[0, 0]) + wide(far_w[0])
    vo_grad = w2[0, 0] + wide(near_w[1, 0]) + wide(far_w[1])

    qk_grad, vo_grad = inner_scatter(qk_grad, 0), inner_scatter(vo_grad, 0)
    local = vo_grad.shape[1] // 2
    gate_grad = inner_scatter(jnp.concatenate([gate_a, gate_b], axis=1), 1)
    return (
        out.reshape(micro, seq, width),
        dinput.reshape(micro, seq, width),
        jnp.stack([qk_grad[:, :local], qk_grad[:, local:], vo_grad[:, :local]]),
        vo_grad[:, local:].T,
        inner_scatter(up_grad, 0),
        inner_scatter(down_grad, 0).T,
        norms[:2],
        norms[2:],
        gate_grad * gate_part * (1.0 - gate_part),
    )


def solution(mesh):
    rows = P(None, ("dp", "head"), None)
    gates = P("head", "dp", None)
    weights = (P(None, "dp", "head"), P("head", "dp"), P("dp", "head"), P("head", "dp"))
    return jax.shard_map(
        per_device,
        mesh=mesh,
        in_specs=(rows, rows, P(None, "dp")) + weights + (P(), P(), gates, gates),
        out_specs=(rows, rows) + weights + (P(), P(), gates),
        check_vma=False,
    )
```

```python
import functools, math
import jax, jax.numpy as jnp
from jax import lax
from jax.experimental import pallas as pl
from jax.experimental.pallas import tpu as pltpu
from jax.sharding import PartitionSpec as P

HEAD_DIM = 64
EPS = 1e-05
F32 = jnp.float32
BF16 = jnp.bfloat16
GP = jnp.float32
SCALE = 1.0 / math.sqrt(HEAD_DIM)
LOG2E = math.log2(math.e)
NEG = -1e30
INV_SQRT2 = 1.0 / math.sqrt(2.0)
INV_SQRT2PI = 1.0 / math.sqrt(2.0 * math.pi)


def dot_nn(a, b):
    return lax.dot_general(a, b, (((1,), (0,)), ((), ())), preferred_element_type=F32)


def dot_nt(a, b):
    return lax.dot_general(a, b, (((1,), (1,)), ((), ())), preferred_element_type=F32)


def dot_tn(a, b):
    return lax.dot_general(a, b, (((0,), (0,)), ((), ())), preferred_element_type=F32)


def piece(ref, bits, d, flip):
    y = bits[0] ^ (d & 1)
    z1 = bits[1] ^ ((d >> 1) & 1)
    z2 = bits[2] ^ ((d >> 2) & 1)
    if flip:
        return ref.at[y, 0, z1, z2]
    return ref.at[0, y, z1, z2]


def assemble(dst, ref, bits, flip, cols=None):
    rows = ref.shape[-2]
    cols = pl.ds(0, ref.shape[-1]) if cols is None else cols
    for d in range(8):
        dst[pl.ds(d * rows, rows), cols] = piece(ref, bits, d, flip)[...]


def scatter(ref, src, bits, flip):
    rows = ref.shape[-2]
    for d in range(8):
        piece(ref, bits, d, flip)[...] = src[pl.ds(d * rows, rows), :]


def own(bits, y, z1, z2):
    return (bits[0] ^ y) + 2 * (bits[1] ^ z1) + 4 * (bits[2] ^ z2)


RELATIVE = [(y, z1, z2) for y in range(2) for z1 in range(2) for z2 in range(2)]


def spec_a(tail, pick):
    zeros = (0,) * len(tail)
    return pl.BlockSpec((1, 2, 2, 2) + tail, lambda k, *_: (pick(k), 0, 0, 0) + zeros)


def spec_b(tail, pick):
    zeros = (0,) * len(tail)
    return pl.BlockSpec((2, 1, 2, 2) + tail, lambda k, *_: (0, pick(k), 0, 0) + zeros)


def whole(shape):
    zeros = (0,) * len(shape)
    return pl.BlockSpec(shape, lambda *_: zeros)


def low_pick(k):
    return jnp.minimum(k, 1)


def high_pick(k):
    return jnp.maximum(k - 2, 0)


def norm_stats(z):
    mean = jnp.mean(z, axis=1, keepdims=True)
    centered = z - mean
    inverse = lax.rsqrt(jnp.mean(centered * centered, axis=1, keepdims=True) + EPS)
    return centered * inverse, inverse


def norm_back(du, unit, inverse):
    return inverse * (
        du
        - jnp.mean(du, axis=1, keepdims=True)
        - unit * jnp.mean(du * unit, axis=1, keepdims=True)
    )


def gelu_pair(up):
    cdf = 0.5 + 0.5 * lax.erf(up * INV_SQRT2)
    pdf = INV_SQRT2PI * jnp.exp(-0.5 * (up * up))
    return up * cdf, cdf + up * pdf


SHARE = 200


def cost(flops, moved):
    return pl.CostEstimate(flops=flops // SHARE, bytes_accessed=moved // SHARE, transcendentals=0)


def params(mib=56, n=1):
    return pltpu.CompilerParams(
        dimension_semantics=("arbitrary",) * n, vmem_limit_bytes=mib * 1024 * 1024
    )


def load_pair(k, bits, wu, wd, ua0, ua1, db0, db1):
    @pl.when(k < 2)
    def _():
        assemble(wu, ua0, bits, False)
        assemble(wd, db0, bits, True)

    @pl.when(k >= 2)
    def _():
        assemble(wu, ua1, bits, False)
        assemble(wd, db1, bits, True)


def ffn_units(chunk, hid, wu, wd, act_o, gp_o, acc):
    rows = hid.shape[0]
    ats = [pl.ds(r * chunk, chunk) for r in range(rows // chunk)]
    ahead = dot_nn(hid[ats[0], :], wu[...])
    for r, at in enumerate(ats):
        act, gp = gelu_pair(ahead)
        if r + 1 < len(ats):
            ahead = dot_nn(hid[ats[r + 1], :], wu[...])
        act = act.astype(BF16)
        act_o[0, at, :] = act
        gp_o[0, at, :] = gp.astype(gp_o.dtype)
        acc[at, :] += dot_nt(act, wd[...])


def ffn_part_kernel(chunk, bits, hid, ua0, ua1, db0, db1, act_o, gp_o, acc, wu, wd):
    k = pl.program_id(0)
    load_pair(k, bits, wu, wd, ua0, ua1, db0, db1)

    @pl.when(k == 0)
    def _():
        acc[...] = hid[...].astype(F32)

    ffn_units(chunk, hid, wu, wd, act_o, gp_o, acc)


def ffn_part(bits, hid, ua0, ua1, db0, db1, units, chunk=512):
    rows, width = hid.shape
    p, n = ua0.shape[-2:]
    sds = jax.ShapeDtypeStruct
    col = pl.BlockSpec((1, rows, n), lambda k, *_: (k, 0, 0))
    return pl.pallas_call(
        functools.partial(ffn_part_kernel, chunk),
        out_shape=(sds((4, rows, units), BF16), sds((4, rows, units), GP), sds((rows, width), F32)),
        grid_spec=pltpu.PrefetchScalarGridSpec(
            num_scalar_prefetch=1, grid=(4,),
            in_specs=[whole((rows, width)), spec_a((p, n), low_pick), spec_a((p, n), high_pick),
                      spec_b((p, n), low_pick), spec_b((p, n), high_pick)],
            out_specs=[col, col, whole((rows, width))],
            scratch_shapes=[pltpu.VMEM((width, n), BF16), pltpu.VMEM((width, n), BF16)],
        ),
        compiler_params=params(48),
        cost_estimate=cost(4 * rows * width * 4 * n, 16 * rows * width),
    )(bits, hid, ua0, ua1, db0, db1)


def ffn_rest_kernel(chunk, bits, lens, hid, ua0, ua1, db0, db1, part, gain, bias, dout, act_i, gp_i,
                    act_o, gp_o, out, dsec, dffn, dffnt, dgain, dbias, wu, wd, acc):
    k = pl.program_id(0)
    rows = hid.shape[0]
    load_pair(k, bits, wu, wd, ua0, ua1, db0, db1)

    @pl.when(k == 0)
    def _():
        acc[...] = part[...]

    ffn_units(chunk, hid, wu, wd, act_o, gp_o, acc)

    @pl.when(k == 3)
    def _():
        length = rows // lens.shape[0]
        small = 256
        g = gain[...]
        b = bias[...]
        dg = jnp.zeros_like(g)
        db = jnp.zeros_like(g)
        for r in range(rows // small):
            at = pl.ds(r * small, small)
            size = lens[r * small // length]
            pos = (r * small % length) + lax.broadcasted_iota(jnp.int32, (small, 1), 0)
            valid = pos < size
            unit, inverse = norm_stats(acc[at, :])
            out[at, :] = jnp.where(valid, unit * g + b, 0.0).astype(BF16)
            dy = jnp.where(valid, dout[at, :].astype(F32), 0.0)
            dg += jnp.sum(dy * unit, axis=0, keepdims=True)
            db += jnp.sum(dy, axis=0, keepdims=True)
            dz = norm_back(dy * g, unit, inverse)
            dsec[at, :] = dz
            low = dz.astype(BF16)
            dffn[at, :] = low
            dffnt[:, at] = low.T
        dgain[...] = dg
        dbias[...] = db


def ffn_rest(bits, lens, hid, ua0, ua1, db0, db1, part, gain, bias, dout, act, gp, chunk=512):
    rows, width = hid.shape
    p, n = ua0.shape[-2:]
    last = act.shape[2] // n - 1
    sds = jax.ShapeDtypeStruct
    full = whole((rows, width))
    line = whole((1, width))
    col = pl.BlockSpec((1, rows, n), lambda k, *_: (k, 0, last))
    anywhere = pl.BlockSpec(memory_space=pl.ANY)
    return pl.pallas_call(
        functools.partial(ffn_rest_kernel, chunk),
        out_shape=(sds(act.shape, act.dtype), sds(gp.shape, gp.dtype), sds((rows, width), BF16), sds((rows, width), F32),
                   sds((rows, width), BF16), sds((width, rows), BF16), sds((1, width), F32), sds((1, width), F32)),
        grid_spec=pltpu.PrefetchScalarGridSpec(
            num_scalar_prefetch=2, grid=(4,),
            in_specs=[full, spec_a((p, n), low_pick), spec_a((p, n), high_pick),
                      spec_b((p, n), low_pick), spec_b((p, n), high_pick), full, line, line, full, anywhere, anywhere],
            out_specs=[col, col, full, full, full, whole((width, rows)), line, line],
            scratch_shapes=[pltpu.VMEM((width, n), BF16), pltpu.VMEM((width, n), BF16), pltpu.VMEM((rows, width), F32)],
        ),
        input_output_aliases={11: 0, 12: 1},
        compiler_params=params(48),
        cost_estimate=cost(4 * rows * width * 4 * n, 20 * rows * width),
    )(bits, lens, hid, ua0, ua1, db0, db1, part, gain, bias, dout, act, gp)


def down_grad_kernel(bits, dt, act, keep, send):
    k = pl.program_id(0)
    grad = dot_nn(dt[...], act[0]).astype(BF16)
    rows = keep.shape[-2]

    def put(ref):
        for d in range(8):
            piece(ref, bits, d, True)[...] = grad[d * rows : (d + 1) * rows]

    @pl.when(k < 2)
    def _():
        put(keep)

    @pl.when(k >= 2)
    def _():
        put(send)


def down_grads(bits, dt, act):
    width, rows = dt.shape
    n = act.shape[2]
    p = width // 8
    sds = jax.ShapeDtypeStruct
    return pl.pallas_call(
        down_grad_kernel,
        out_shape=(sds((2, 2, 2, 2, p, n), BF16), sds((2, 2, 2, 2, p, n), BF16)),
        grid_spec=pltpu.PrefetchScalarGridSpec(
            num_scalar_prefetch=1, grid=(4,),
            in_specs=[whole((width, rows)), pl.BlockSpec((1, rows, n), lambda k, *_: (k, 0, 0))],
            out_specs=[spec_b((p, n), low_pick), spec_b((p, n), high_pick)],
        ),
        compiler_params=params(40),
        cost_estimate=cost(2 * rows * width * 4 * n, 14 * rows * width),
    )(bits, dt, act)


def ffn_bwd_kernel(chunk, last, bits, ht, dffn, uap, uaq, dbp, dbq, gp, *rest):
    if last:
        dsec, part, unit, inverse, gain, gu, dfirst, dattn, dattnt, dgain, dbias, wu, wd, dup_s, acc = rest
    else:
        gu, acc, wu, wd, dup_s = rest
    k = pl.program_id(0)
    rows, width = dffn.shape
    np = uap.shape[-1]
    left, right = pl.ds(0, np), pl.ds(np, uaq.shape[-1])

    assemble(wu, uap, bits, False, left)
    assemble(wu, uaq, bits, False, right)
    assemble(wd, dbp, bits, True, left)
    assemble(wd, dbq, bits, True, right)

    @pl.when(k == 0)
    def _():
        if last:
            acc[...] = part[...] + dsec[...]
        else:
            acc[...] = jnp.zeros_like(acc)

    ats = [pl.ds(r * chunk, chunk) for r in range(rows // chunk)]
    ahead = dot_nn(dffn[ats[0], :], wd[...])
    for r, at in enumerate(ats):
        dup = (ahead * gp[0, at, :].astype(F32)).astype(BF16)
        if r + 1 < len(ats):
            ahead = dot_nn(dffn[ats[r + 1], :], wd[...])
        dup_s[at, :] = dup
        acc[at, :] += dot_nt(dup, wu[...])

    grad = dot_nn(ht[...], dup_s[...]).astype(BF16)
    p = gu.shape[-2]
    for d in range(8):
        piece(gu, bits, d, False)[...] = grad[d * p : (d + 1) * p]

    if last:

        @pl.when(k == 1)
        def _():
            small = 256
            g = gain[...]
            dg = jnp.zeros_like(g)
            db = jnp.zeros_like(g)
            for r in range(rows // small):
                at = pl.ds(r * small, small)
                dh = acc[at, :]
                u = unit[at, :]
                dg += jnp.sum(dh * u, axis=0, keepdims=True)
                db += jnp.sum(dh, axis=0, keepdims=True)
                dz = norm_back(dh * g, u, inverse[at, :])
                dfirst[at, :] = dz
                low = dz.astype(BF16)
                dattn[at, :] = low
                dattnt[:, at] = low.T
            dgain[...] = dg
            dbias[...] = db


def ffn_backward(last, bits, ht, dffn, uap, uaq, dbp, dbq, gp, extra=(), chunk=512):
    rows, width = dffn.shape
    p, np = uap.shape[-2:]
    nq = uaq.shape[-1]
    n = np + nq
    sds = jax.ShapeDtypeStruct
    off = 0 if last else 2
    pick = lambda k: k
    full = whole((rows, width))
    line = whole((1, width))
    out_shape = [sds((2, 2, 2, 2, p, n), BF16)]
    out_specs = [spec_a((p, n), pick)]
    in_specs = [
        whole((width, rows)), full,
        spec_a((p, np), pick), spec_a((p, nq), pick), spec_b((p, np), pick), spec_b((p, nq), pick),
        pl.BlockSpec((1, rows, n), lambda k, *_: (k + off, 0, 0)),
    ]
    scratch = [pltpu.VMEM((width, n), BF16), pltpu.VMEM((width, n), BF16), pltpu.VMEM((rows, n), BF16)]
    if last:
        in_specs += [full] * 3 + [whole((rows, 1)), line]
        out_shape += [sds((rows, width), F32), sds((rows, width), BF16), sds((width, rows), BF16), sds((1, width), F32), sds((1, width), F32)]
        out_specs += [full, full, whole((width, rows)), line, line]
        scratch += [pltpu.VMEM((rows, width), F32)]
    else:
        out_shape += [sds((rows, width), F32)]
        out_specs += [full]
    return pl.pallas_call(
        functools.partial(ffn_bwd_kernel, chunk, last),
        out_shape=out_shape,
        grid_spec=pltpu.PrefetchScalarGridSpec(
            num_scalar_prefetch=1, grid=(2,), in_specs=in_specs, out_specs=out_specs, scratch_shapes=scratch,
        ),
        compiler_params=params(56),
        cost_estimate=cost(6 * rows * width * 2 * n, 30 * rows * width),
    )(bits, ht, dffn, uap, uaq, dbp, dbq, gp, *extra)


def key_bias(size, length):
    pos = lax.broadcasted_iota(jnp.int32, (1, length), 1)
    return jnp.where(pos < size, 0.0, NEG).astype(F32)


def gate_rows(ga, gb, bits, i, d0, count):
    parts = []
    for j in range(count):
        d = d0 + j
        y = bits[0] ^ (d & 1)
        z1 = bits[1] ^ ((d >> 1) & 1)
        z2 = bits[2] ^ ((d >> 2) & 1)
        parts.append(ga[0, y, z1, z2, i])
        parts.append(gb[y, 0, z1, z2, i])
    return jnp.concatenate(parts, axis=0).astype(F32)


def att_fwd_kernel(bits, lens, qk, v, ga, gb, mixed, lse):
    length = qk.shape[1]
    heads = v.shape[2] // HEAD_DIM
    bias = key_bias(lens[pl.program_id(1)], length)
    count = length // (2 * ga.shape[-2])
    cols = [pl.ds(i * HEAD_DIM, HEAD_DIM) for i in range(2 * heads)]

    def score(i):
        return dot_nt(qk[0, :, cols[i]], qk[0, :, cols[heads + i]])

    ahead = score(0)
    outs = []
    stats = []
    for i in range(heads):
        s = ahead * (SCALE * LOG2E) + bias
        if i + 1 < heads:
            ahead = score(i + 1)
        top = jnp.max(s, axis=1, keepdims=True)
        e = jnp.exp2(s - top)
        total = jnp.sum(e, axis=1, keepdims=True)
        w = (e * gate_rows(ga, gb, bits, i, 0, count)).astype(BF16)
        outs.append(dot_nn(w, v[0, :, cols[i]]) * (1.0 / total))
        stats.append(top + jnp.log2(total))
    mixed[0] = jnp.concatenate(outs, axis=1).astype(BF16)
    lse[0] = jnp.concatenate(stats, axis=1)


def attention_forward(bits, lens, qk, v, ga, gb):
    _, rows, w2 = qk.shape
    w1 = v.shape[2]
    count = lens.shape[0]
    length = rows // count
    heads, sub, keys = ga.shape[-3:]
    sds = jax.ShapeDtypeStruct
    return pl.pallas_call(
        att_fwd_kernel,
        out_shape=(sds((2, rows, w1), BF16), sds((2, rows, heads), F32)),
        grid_spec=pltpu.PrefetchScalarGridSpec(
            num_scalar_prefetch=2, grid=(2, count),
            in_specs=[
                pl.BlockSpec((1, length, w2), lambda k, s, *_: (k, s, 0)),
                pl.BlockSpec((1, length, w1), lambda k, s, *_: (k, s, 0)),
                spec_a((heads, sub, keys), lambda k: k), spec_b((heads, sub, keys), lambda k: k),
            ],
            out_specs=[
                pl.BlockSpec((1, length, w1), lambda k, s, *_: (k, s, 0)),
                pl.BlockSpec((1, length, heads), lambda k, s, *_: (k, s, 0)),
            ],
        ),
        compiler_params=params(n=2),
        cost_estimate=cost(16 * 2 * rows * length * w1, 16 * rows * w1),
    )(bits, lens, qk, v, ga, gb)


def att_bwd_kernel(last, bits, lens, qk, v, ga, gb, lse, dattn, wo, *rest):
    if last:
        ra, rb, dqk, dv, a_keep, a_send, b_keep, b_send, dm_s, dmt, qt, acc = rest
    else:
        dqk, dv, oga, ogb, dm_s, dmt, qt, acc = rest
    length = qk.shape[1]
    heads = v.shape[2] // HEAD_DIM
    hw = heads * HEAD_DIM
    k = pl.program_id(0)
    seq = pl.program_id(1)
    bias = key_bias(lens[seq], length)
    sub = ga.shape[-2]
    count = length // (2 * sub)
    cols = [pl.ds(i * HEAD_DIM, HEAD_DIM) for i in range(2 * heads)]

    dm = dot_nn(dattn[...], wo[0]).astype(BF16)
    dm_s[...] = dm
    dmt[...] = dm.T
    qt[...] = qk[0, :, pl.ds(0, hw)].T

    def products(i):
        return (
            dot_nt(qk[0, :, cols[i]], qk[0, :, cols[heads + i]]),
            dot_nt(dm_s[:, cols[i]], v[0, :, cols[i]]),
        )

    ahead = products(0)
    dqs, dks, dvs = [], [], []
    for i in range(heads):
        s, dw = ahead
        p = jnp.exp2(s * (SCALE * LOG2E) + bias - lse[0, :, pl.ds(i, 1)])
        if i + 1 < heads:
            ahead = products(i + 1)
        g = gate_rows(ga, gb, bits, i, 0, count)
        w = (p * g).astype(BF16)
        t = dw * p
        acc[i] = t + jnp.where(seq == 0, 0.0, acc[i])
        u = t * g
        ds = (u - p * jnp.sum(u, axis=1, keepdims=True)).astype(BF16)
        dqs.append(dot_nn(ds, qk[0, :, cols[heads + i]]) * SCALE)
        dvs.append(dot_nn(dmt[cols[i], :], w).astype(BF16).T)
        dks.append((dot_nn(qt[cols[i], :], ds) * SCALE).astype(BF16).T)
    dqk[0] = jnp.concatenate([d.astype(BF16) for d in dqs] + dks, axis=1)
    dv[0] = jnp.concatenate(dvs, axis=1)

    def first_rows(y, z1, z2):
        return pl.ds(pl.multiple_of(own(bits, y, z1, z2) * 2 * sub, sub), sub)

    def second_rows(y, z1, z2):
        return pl.ds(pl.multiple_of(own(bits, y, z1, z2) * 2 * sub + sub, sub), sub)

    @pl.when(seq == pl.num_programs(1) - 1)
    def _():
        if not last:
            for r in RELATIVE:
                for i in range(heads):
                    oga[(0,) + r + (i,)] = acc[i, first_rows(*r), :].astype(BF16)
                    ogb[(r[0], 0) + r[1:] + (i,)] = acc[i, second_rows(*r), :].astype(BF16)
            return

        def put_a(ref):
            for r in RELATIVE:
                for i in range(heads):
                    ref[r + (i,)] = (acc[i, first_rows(*r), :] + ra[(0,) + r + (i,)].astype(F32)).astype(BF16)

        @pl.when(k == 0)
        def _():
            put_a(a_keep)

        @pl.when(k == 1)
        def _():
            put_a(a_send)

        for r in RELATIVE:
            ref = b_send if r[0] else b_keep
            for i in range(heads):
                ref[(0,) + r[1:] + (i,)] = (
                    acc[i, second_rows(*r), :] + rb[(r[0], 0) + r[1:] + (i,)].astype(F32)
                ).astype(BF16)


def attention_backward(last, bits, lens, qk, v, ga, gb, lse, dattn, wo, got=()):
    _, rows, w2 = qk.shape
    w1 = v.shape[2]
    width = dattn.shape[1]
    count = lens.shape[0]
    length = rows // count
    tail = ga.shape[-3:]
    heads, sub, keys = tail
    sds = jax.ShapeDtypeStruct
    pick = lambda k: k
    in_specs = [
        pl.BlockSpec((1, length, w2), lambda k, s, *_: (k, s, 0)),
        pl.BlockSpec((1, length, w1), lambda k, s, *_: (k, s, 0)),
        spec_a(tail, pick), spec_b(tail, pick),
        pl.BlockSpec((1, length, heads), lambda k, s, *_: (k, s, 0)),
        pl.BlockSpec((length, width), lambda k, s, *_: (s, 0)),
        pl.BlockSpec((1, width, w1), lambda k, s, *_: (k, 0, 0)),
    ]
    out_shape = [sds((2, rows, w2), BF16), sds((2, rows, w1), BF16)]
    out_specs = [
        pl.BlockSpec((1, length, w2), lambda k, s, *_: (k, s, 0)),
        pl.BlockSpec((1, length, w1), lambda k, s, *_: (k, s, 0)),
    ]
    if last:
        in_specs += [spec_a(tail, pick), spec_b(tail, pick)]
        out_shape += [sds((2, 2, 2) + tail, BF16)] * 4
        out_specs += [whole((2, 2, 2) + tail)] * 2 + [
            pl.BlockSpec((1, 2, 2) + tail, lambda k, *_: (k, 0, 0, 0, 0, 0))
        ] * 2
    else:
        out_shape += [sds((2, 2, 2, 2) + tail, BF16)] * 2
        out_specs += [spec_a(tail, pick), spec_b(tail, pick)]
    return pl.pallas_call(
        functools.partial(att_bwd_kernel, last),
        out_shape=out_shape,
        grid_spec=pltpu.PrefetchScalarGridSpec(
            num_scalar_prefetch=2, grid=(2, count), in_specs=in_specs, out_specs=out_specs,
            scratch_shapes=[
                pltpu.VMEM((length, w1), BF16), pltpu.VMEM((w1, length), BF16),
                pltpu.VMEM((w1, length), BF16), pltpu.VMEM((heads, length, keys), F32),
            ],
        ),
        compiler_params=params(n=2),
        cost_estimate=cost(40 * 2 * rows * length * w1, 30 * rows * w1),
    )(bits, lens, qk, v, ga, gb, lse, dattn, wo, *got)


def qkv_kernel(first, bits, x, wa, wb, qk, v, wqk, wv, wo, *rest):
    w1 = v.shape[2]
    wb_s = rest[-1]
    assemble(wqk.at[0], wa, bits, False)
    assemble(wb_s, wb, bits, True)

    if first:

        @pl.when(pl.program_id(0) == 0)
        def _():
            rest[0][...] = x[...].T

    wv[0] = wb_s[:, pl.ds(0, w1)]
    wo[0] = wb_s[:, pl.ds(w1, w1)]
    qk[0] = dot_nn(x[...], wqk[0]).astype(BF16)
    v[0] = dot_nn(x[...], wv[0]).astype(BF16)


def project(first, bits, x, wa, wb):
    rows, width = x.shape
    p, w2 = wa.shape[-2:]
    w1 = w2 // 2
    sds = jax.ShapeDtypeStruct
    pick = lambda k: k
    head = lambda s: pl.BlockSpec((1,) + s, lambda k, *_: (k, 0, 0))
    return pl.pallas_call(
        functools.partial(qkv_kernel, first),
        out_shape=[sds((2, rows, w2), BF16), sds((2, rows, w1), BF16), sds((2, width, w2), BF16),
                   sds((2, width, w1), BF16), sds((2, width, w1), BF16)]
        + ([sds((width, rows), BF16)] if first else []),
        grid_spec=pltpu.PrefetchScalarGridSpec(
            num_scalar_prefetch=1, grid=(2,),
            in_specs=[whole((rows, width)), spec_a((p, w2), pick), spec_b((p, w2), pick)],
            out_specs=[head((rows, w2)), head((rows, w1)), head((width, w2)), head((width, w1)), head((width, w1))]
            + ([whole((width, rows))] if first else []),
            scratch_shapes=[pltpu.VMEM((width, w2), BF16)],
        ),
        compiler_params=params(),
        cost_estimate=cost(2 * rows * width * 2 * (w1 + w2), 8 * rows * width),
    )(bits, x, wa, wb)


def out_kernel(x, m0, m1, wo0, wo1, gain, bias, hid, unit, inverse, hidt):
    attn = dot_nt(m0[0], wo0[0]) + dot_nt(m0[1], wo0[1]) + dot_nt(m1[0], wo1[0]) + dot_nt(m1[1], wo1[1])
    u, inv = norm_stats(x[...].astype(F32) + attn)
    h = (u * gain[...] + bias[...]).astype(BF16)
    hid[...] = h
    hidt[...] = h.T
    unit[...] = u
    inverse[...] = inv


def out_forward(x, m0, m1, wo0, wo1, gain, bias, block=256):
    rows, width = x.shape
    w1 = wo0.shape[2]
    sds = jax.ShapeDtypeStruct
    row = lambda w: pl.BlockSpec((block, w), lambda r: (r, 0))
    mix = pl.BlockSpec((2, block, w1), lambda r: (0, r, 0))
    return pl.pallas_call(
        out_kernel,
        grid=(rows // block,),
        out_shape=(sds((rows, width), BF16), sds((rows, width), F32), sds((rows, 1), F32), sds((width, rows), BF16)),
        in_specs=[row(width), mix, mix, whole((2, width, w1)), whole((2, width, w1)), whole((1, width)), whole((1, width))],
        out_specs=[row(width), row(width), row(1), pl.BlockSpec((width, block), lambda r: (0, r))],
        compiler_params=params(),
        cost_estimate=cost(2 * rows * width * 4 * w1, 12 * rows * width),
    )(x, m0, m1, wo0, wo1, gain, bias)


def qkv_grad_kernel(last, bits, xt, dat, dqk, dv, mixed, *rest):
    if last:
        ra, rb, a_keep, a_send, b_keep, b_send, ta, tb = rest
    else:
        ga, gb, ta, tb = rest
    w1 = dv.shape[2]
    k = pl.program_id(0)
    ta[...] = dot_nn(xt[...], dqk[0]).astype(ta.dtype)
    tb[:, pl.ds(0, w1)] = dot_nn(xt[...], dv[0]).astype(tb.dtype)
    tb[:, pl.ds(w1, w1)] = dot_nn(dat[...], mixed[0]).astype(tb.dtype)
    if not last:
        scatter(ga, ta, bits, False)
        scatter(gb, tb, bits, True)
        return
    p = ra.shape[-2]

    def rows(r):
        return pl.ds(pl.multiple_of(own(bits, *r) * p, 16), p)

    def put_a(ref):
        for r in RELATIVE:
            ref[r] = (ta[rows(r), :] + ra[(0,) + r].astype(F32)).astype(BF16)

    @pl.when(k == 0)
    def _():
        put_a(a_keep)

    @pl.when(k == 1)
    def _():
        put_a(a_send)

    for r in RELATIVE:
        ref = b_send if r[0] else b_keep
        ref[(0,) + r[1:]] = (tb[rows(r), :] + rb[(r[0], 0) + r[1:]].astype(F32)).astype(BF16)


def qkv_grads(last, bits, xt, dat, dqk, dv, mixed, got=()):
    width, rows = xt.shape
    w2 = dqk.shape[2]
    w1 = dv.shape[2]
    per = width // 8
    sds = jax.ShapeDtypeStruct
    pick = lambda k: k
    head = lambda w: pl.BlockSpec((1, rows, w), lambda k, *_: (k, 0, 0))
    in_specs = [whole((width, rows)), whole((width, rows)), head(w2), head(w1), head(w1)]
    if last:
        in_specs += [spec_a((per, w2), pick), spec_b((per, w2), pick)]
        out_shape = [sds((2, 2, 2, per, w2), BF16)] * 4
        out_specs = [whole((2, 2, 2, per, w2))] * 2 + [
            pl.BlockSpec((1, 2, 2, per, w2), lambda k, *_: (k, 0, 0, 0, 0))
        ] * 2
    else:
        out_shape = [sds((2, 2, 2, 2, per, w2), BF16)] * 2
        out_specs = [spec_a((per, w2), pick), spec_b((per, w2), pick)]
    kind = F32 if last else BF16
    return pl.pallas_call(
        functools.partial(qkv_grad_kernel, last),
        out_shape=out_shape,
        grid_spec=pltpu.PrefetchScalarGridSpec(
            num_scalar_prefetch=1, grid=(2,), in_specs=in_specs, out_specs=out_specs,
            scratch_shapes=[pltpu.VMEM((width, w2), kind), pltpu.VMEM((width, w2), kind)],
        ),
        compiler_params=params(40),
        cost_estimate=cost(2 * rows * width * 2 * 2 * w2, 8 * rows * width),
    )(bits, xt, dat, dqk, dv, mixed, *got)


def dinput_kernel(dfirst, dqk0, dqk1, dv0, dv1, wqk0, wqk1, wv0, wv1, out):
    total = dfirst[...]
    for a, b, wa, wb in ((dqk0, dv0, wqk0, wv0), (dqk1, dv1, wqk1, wv1)):
        for k in range(2):
            total = total + dot_nt(a[k], wa[k]) + dot_nt(b[k], wb[k])
    out[...] = total


def input_backward(dfirst, dqk0, dqk1, dv0, dv1, wqk0, wqk1, wv0, wv1, block=256):
    rows, width = dfirst.shape
    w2 = wqk0.shape[2]
    w1 = wv0.shape[2]
    row = pl.BlockSpec((block, width), lambda r: (r, 0))
    part = lambda w: pl.BlockSpec((2, block, w), lambda r: (0, r, 0))
    return pl.pallas_call(
        dinput_kernel,
        grid=(rows // block,),
        out_shape=jax.ShapeDtypeStruct((rows, width), F32),
        in_specs=[row, part(w2), part(w2), part(w1), part(w1)]
        + [whole((2, width, w2))] * 2 + [whole((2, width, w1))] * 2,
        out_specs=row,
        compiler_params=params(),
        cost_estimate=cost(2 * rows * width * 4 * (w1 + w2), 14 * rows * width),
    )(dfirst, dqk0, dqk1, dv0, dv1, wqk0, wqk1, wv0, wv1)


GROUPS = 8


def partner_dp(value, bit):
    size = lax.axis_size("dp")
    step = (1 << bit) * (size // GROUPS)
    return lax.ppermute(value, "dp", [(i, i ^ step) for i in range(size)])


def partner_head(value, bit):
    size = lax.axis_size("head")
    return lax.ppermute(value, "head", [(i, i ^ (1 << bit)) for i in range(size)])


def over_y(value):
    return partner_dp(value, 0)


def over_near(value):
    return partner_dp(value, 1)


def over_far(value):
    return partner_dp(value, 2)


def over_pair(value):
    return partner_head(value, 0)


def over_x(value):
    return partner_head(value, 1)


def inner_groups():
    inner = lax.axis_size("dp") // GROUPS
    return inner, [[g * inner + i for i in range(inner)] for g in range(GROUPS)]


def inner_gather(value, axis):
    inner, groups = inner_groups()
    if inner == 1:
        return value
    return lax.all_gather(value, "dp", axis_index_groups=groups, axis=axis, tiled=True)


def inner_scatter(value, axis):
    inner, groups = inner_groups()
    if inner == 1:
        return value
    return lax.psum_scatter(value, "dp", axis_index_groups=groups, scatter_dimension=axis, tiled=True)


def after(values, *waits):
    return lax.optimization_barrier((tuple(values), waits))[0]


def wide(value):
    return value.astype(F32)


def first_sum(keep, got):
    return (wide(keep[1]) + wide(got[1])).astype(BF16)


def second_sum(keep, got, more):
    return (wide(keep[0, 1]) + wide(got[0, 1]) + wide(more[1])).astype(BF16)


def third_sum(keep, got, more, last):
    return wide(keep[0, 0]) + wide(got[0, 0]) + wide(more[0]) + wide(last)


def low_sum(keep, got):
    return (wide(keep[1]) + wide(got[1])).astype(BF16)


def high_sum(keep, got, more):
    return wide(keep[0]) + wide(got[0]) + wide(more)


def total_steps():
    steps = []
    for name in ("head", "dp"):
        size = lax.axis_size(name)
        step = 1
        while step < size:
            steps.append((name, [(i, i ^ step) for i in range(size)]))
            step *= 2
    return steps


def total_some(value, *steps):
    for name, pairs in steps:
        value = value + lax.ppermute(value, name, pairs)
    return value


def per_device(layer_input, output_grad, lengths, w_qkv, w_out, w_up, w_down,
               norm_gains, norm_biases, mask_logits, mask_noise):
    micro, seq, width = layer_input.shape
    rows = micro * seq
    x = layer_input.reshape(rows, width)
    dout = output_grad.reshape(rows, width)
    place = lax.axis_index("dp") // (lax.axis_size("dp") // GROUPS)
    bits = jnp.stack([place & 1, (place >> 1) & 1, (place >> 2) & 1]).astype(jnp.int32)
    lens = lax.dynamic_slice_in_dim(lengths, lax.axis_index("head"), 1, 1).reshape(micro)

    gate_part = jax.nn.sigmoid(mask_logits + mask_noise)
    gate_all = inner_gather(gate_part.astype(BF16), 1)
    sub = gate_all.shape[1] // 2
    gain1, gain2 = norm_gains[0:1], norm_gains[1:2]
    bias1, bias2 = norm_biases[0:1], norm_biases[1:2]

    ga = jnp.stack([
        inner_gather(jnp.concatenate([w_qkv[0], w_qkv[1]], axis=1), 0),
        inner_gather(jnp.concatenate([w_qkv[2], w_out.T], axis=1), 0),
    ])
    gb = jnp.stack([gate_all[:, :sub], gate_all[:, sub:]])
    up_all, down_all = inner_gather(w_up, 0), inner_gather(w_down.T, 0)
    units = up_all.shape[1]
    most = units * 2 // 3
    gc = jnp.stack([up_all[:, :most], down_all[:, :most]])
    ge = jnp.stack([up_all[:, most:], down_all[:, most:]])

    got = over_far(ga)
    ga = jnp.stack([ga, got], axis=1)
    got = over_near(ga)
    ga = jnp.stack([ga, got], axis=1)
    aa, ab = ga[0], ga[1]
    (gb,) = after((gb,), got)
    ra, rb = over_y(aa), over_x(ab)
    far_b = over_far(gb)
    aa, ab = jnp.stack([aa, ra]), jnp.stack([ab, rb])
    gb, = after((gb,), ra, rb)
    gb = jnp.stack([gb, far_b], axis=1)
    aa, ab = after((aa, ab), gb)
    ra, rb = over_x(aa), over_y(ab)
    near_b = over_near(gb)
    (gc,) = after((gc,), near_b)
    far_c = over_far(gc)
    gb = jnp.stack([gb, near_b], axis=1)
    ba, bb = gb[0], gb[1]
    aa, ab = jnp.stack([aa, ra]), jnp.stack([ab, rb])
    ba, bb = after((ba, bb), ra, rb)
    ca, cb = over_pair(aa), over_pair(ab)
    ra, rb = over_y(ba), over_x(bb)
    qk0, v0, wqk0, wv0, wo0, xt = project(True, bits, x, aa, ab)
    ba, bb = jnp.stack([ba, ra]), jnp.stack([bb, rb])
    ba, bb, gc, ca, cb = after((ba, bb, gc, ca, cb), qk0, ra, rb)
    ra, rb = over_x(ba), over_y(bb)
    gc = jnp.stack([gc, far_c], axis=1)
    near_c = over_near(gc)
    qk1, v1, wqk1, wv1, wo1 = project(False, bits, x, ca, cb)
    ba, bb = jnp.stack([ba, ra]), jnp.stack([bb, rb])
    gc = jnp.stack([gc, near_c], axis=1)
    fa, fb = gc[0], gc[1]
    fa, fb, ba, bb, ge = after((fa, fb, ba, bb, ge), ra, rb, near_c, qk1)
    ba1, bb1 = over_pair(ba), over_pair(bb)
    ra, rb = over_y(fa), over_x(fb)
    far_e = over_far(ge)
    m0, lse0 = attention_forward(bits, lens, qk0, v0, ba, bb)
    fa, fb = jnp.stack([fa, ra]), jnp.stack([fb, rb])
    ge = jnp.stack([ge, far_e], axis=1)
    fa, fb, ge, ba1, bb1 = after((fa, fb, ge, ba1, bb1), m0)
    ra, rb = over_x(fa), over_y(fb)
    near_e = over_near(ge)
    ge = jnp.stack([ge, near_e], axis=1)
    m1, lse1 = attention_forward(bits, lens, qk1, v1, ba1, bb1)
    hid, unit, inverse, hidt = out_forward(x, m0, m1, wo0, wo1, gain1, bias1)
    fa, fb = jnp.stack([fa, ra]), jnp.stack([fb, rb])
    ea, eb = ge[0], ge[1]
    fa, fb, ea, eb = after((fa, fb, ea, eb), hid, ra, rb)
    fa1, fb1 = over_pair(fa), over_pair(fb)
    ra, rb = over_y(ea), over_x(eb)
    ea, eb = jnp.stack([ea, ra]), jnp.stack([eb, rb])
    ea, eb, hid = after((ea, eb, hid), fa1, fb1)
    ra, rb = over_x(ea), over_y(eb)
    act, gp, part = ffn_part(bits, hid, fa, fa1, fb, fb1, units)
    ea, eb = jnp.stack([ea, ra]), jnp.stack([eb, rb])
    ea, eb = after((ea, eb), part)
    ea1, eb1 = over_pair(ea), over_pair(eb)
    act, gp, out, dsec, dffn, dffnt, dgain2, dbias2 = ffn_rest(
        bits, lens, hid, ea, ea1, eb, eb1, part, gain2, bias2, dout, act, gp
    )

    steps = total_steps()
    down0, down1 = down_grads(bits, dffnt, act)
    cd = over_pair(down1)
    dffn, = after((dffn,), down1)
    up1, part = ffn_backward(False, bits, hidt, dffn, fa1, ea1, fb1, eb1, gp)
    down0, cd, up1, dffn = after((down0, cd, up1, dffn), part)
    xd = over_y(first_sum(down0, cd))
    cu = over_pair(up1)
    up0, dfirst, dattn, dattnt, dgain1, dbias1 = ffn_backward(
        True, bits, hidt, dffn, fa, ea, fb, eb, gp, (dsec, part, unit, inverse, gain1)
    )
    up0, cu, norms, dattn = after((up0, cu, jnp.concatenate([dgain1, dgain2, dbias1, dbias2]), dattn), up0)
    xu = over_x(first_sum(up0, cu))
    norms = total_some(norms, steps[0])
    dqk1, dv1, ga1, gb1 = attention_backward(False, bits, lens, qk1, v1, ba1, bb1, lse1, dattn, wo1)
    ga1, gb1, norms, dqk1, xd, xu = after((ga1, gb1, norms, dqk1, xd, xu), dv1)
    cga, cgb = over_pair(ga1), over_pair(gb1)
    norms = total_some(norms, steps[3])
    yd, yu = over_x(second_sum(down0, cd, xd)), over_y(second_sum(up0, cu, xu))
    qka1, vo1 = qkv_grads(False, bits, xt, dattnt, dqk1, dv1, m1)
    qka1, vo1, dattn, norms, cga, cgb, yd, yu = after((qka1, vo1, dattn, norms, cga, cgb, yd, yu), vo1)
    cqk, cvo = over_pair(qka1), over_pair(vo1)
    u, d = third_sum(up0, cu, xu, yu), third_sum(down0, cd, xd, yd)
    near_f = over_near(jnp.stack([u[1], d[1]]).astype(BF16))
    norms = total_some(norms, steps[4])
    dqk0, dv0, ga0, ga_out, gb0, gb_out = attention_backward(
        True, bits, lens, qk0, v0, ba, bb, lse0, dattn, wo0, (cga, cgb)
    )
    ga_out, gb_out, dqk0, norms, cqk, cvo, near_f = after((ga_out, gb_out, dqk0, norms, cqk, cvo, near_f), dv0)
    xga, xgb = over_x(ga_out), over_y(gb_out)
    far_f = over_far(jnp.stack([u[0, 1] + wide(near_f[0, 1]), d[0, 1] + wide(near_f[1, 1])]).astype(BF16))
    qka0, qka_out, vo0, vo_out = qkv_grads(True, bits, xt, dattnt, dqk0, dv0, m0, (cqk, cvo))
    qka_out, vo_out, far_f, xga, xgb, dqk0 = after((qka_out, vo_out, far_f, xga, xgb, dqk0), vo0)
    xqk, xvo = over_x(qka_out), over_y(vo_out)
    yga, ygb = over_y(low_sum(ga0, xga)), over_x(low_sum(gb0, xgb))
    dinput = input_backward(dfirst, dqk0, dqk1, dv0, dv1, wqk0, wqk1, wv0, wv1)
    xqk, xvo, yga, ygb, norms = after((xqk, xvo, yga, ygb, norms), dinput)
    yqk, yvo = over_y(low_sum(qka0, xqk)), over_x(low_sum(vo0, xvo))
    g1, g2 = high_sum(ga0, xga, yga), high_sum(gb0, xgb, ygb)
    near_g = over_near(jnp.stack([g1[1], g2[1]]).astype(BF16))
    norms, = after((norms,), yqk, yvo)
    norms = total_some(norms, steps[1])
    w1, w2 = high_sum(qka0, xqk, yqk), high_sum(vo0, xvo, yvo)
    near_w = over_near(jnp.stack([w1[1], w2[1]]).astype(BF16))
    far_g = over_far(jnp.stack([g1[0, 1] + wide(near_g[0, 1]), g2[0, 1] + wide(near_g[1, 1])]).astype(BF16))
    norms, = after((norms,), near_w)
    norms = total_some(norms, *steps[2:3], *steps[5:])
    far_w = over_far(jnp.stack([w1[0, 1] + wide(near_w[0, 1]), w2[0, 1] + wide(near_w[1, 1])]).astype(BF16))

    up_grad = u[0, 0] + wide(near_f[0, 0]) + wide(far_f[0])
    down_grad = d[0, 0] + wide(near_f[1, 0]) + wide(far_f[1])
    gate_a = g1[0, 0] + wide(near_g[0, 0]) + wide(far_g[0])
    gate_b = g2[0, 0] + wide(near_g[1, 0]) + wide(far_g[1])
    qk_grad = w1[0, 0] + wide(near_w[0, 0]) + wide(far_w[0])
    vo_grad = w2[0, 0] + wide(near_w[1, 0]) + wide(far_w[1])

    qk_grad, vo_grad = inner_scatter(qk_grad, 0), inner_scatter(vo_grad, 0)
    local = vo_grad.shape[1] // 2
    gate_grad = inner_scatter(jnp.concatenate([gate_a, gate_b], axis=1), 1)
    return (
        out.reshape(micro, seq, width),
        dinput.reshape(micro, seq, width),
        jnp.stack([qk_grad[:, :local], qk_grad[:, local:], vo_grad[:, :local]]),
        vo_grad[:, local:].T,
        inner_scatter(up_grad, 0),
        inner_scatter(down_grad, 0).T,
        norms[:2],
        norms[2:],
        gate_grad * gate_part * (1.0 - gate_part),
    )


def solution(mesh):
    rows = P(None, ("dp", "head"), None)
    gates = P("head", "dp", None)
    weights = (P(None, "dp", "head"), P("head", "dp"), P("dp", "head"), P("head", "dp"))
    return jax.shard_map(
        per_device,
        mesh=mesh,
        in_specs=(rows, rows, P(None, "dp")) + weights + (P(), P(), gates, gates),
        out_specs=(rows, rows) + weights + (P(), P(), gates),
        check_vma=False,
    )
```

```python
import functools, math
import jax, jax.numpy as jnp
from jax import lax
from jax.experimental import pallas as pl
from jax.experimental.pallas import tpu as pltpu
from jax.sharding import PartitionSpec as P

HEAD_DIM = 64
EPS = 1e-05
F32 = jnp.float32
BF16 = jnp.bfloat16
GP = jnp.float32
SCALE = 1.0 / math.sqrt(HEAD_DIM)
LOG2E = math.log2(math.e)
NEG = -1e30
INV_SQRT2 = 1.0 / math.sqrt(2.0)
INV_SQRT2PI = 1.0 / math.sqrt(2.0 * math.pi)


def dot_nn(a, b):
    return lax.dot_general(a, b, (((1,), (0,)), ((), ())), preferred_element_type=F32)


def dot_nt(a, b):
    return lax.dot_general(a, b, (((1,), (1,)), ((), ())), preferred_element_type=F32)


def dot_tn(a, b):
    return lax.dot_general(a, b, (((0,), (0,)), ((), ())), preferred_element_type=F32)


def piece(ref, bits, d, flip):
    y = bits[0] ^ (d & 1)
    z1 = bits[1] ^ ((d >> 1) & 1)
    z2 = bits[2] ^ ((d >> 2) & 1)
    if flip:
        return ref.at[y, 0, z1, z2]
    return ref.at[0, y, z1, z2]


def assemble(dst, ref, bits, flip, cols=None):
    rows = ref.shape[-2]
    cols = pl.ds(0, ref.shape[-1]) if cols is None else cols
    for d in range(8):
        dst[pl.ds(d * rows, rows), cols] = piece(ref, bits, d, flip)[...]


def scatter(ref, src, bits, flip):
    rows = ref.shape[-2]
    for d in range(8):
        piece(ref, bits, d, flip)[...] = src[pl.ds(d * rows, rows), :]


def own(bits, y, z1, z2):
    return (bits[0] ^ y) + 2 * (bits[1] ^ z1) + 4 * (bits[2] ^ z2)


RELATIVE = [(y, z1, z2) for y in range(2) for z1 in range(2) for z2 in range(2)]


def spec_a(tail, pick):
    zeros = (0,) * len(tail)
    return pl.BlockSpec((1, 2, 2, 2) + tail, lambda k, *_: (pick(k), 0, 0, 0) + zeros)


def spec_b(tail, pick):
    zeros = (0,) * len(tail)
    return pl.BlockSpec((2, 1, 2, 2) + tail, lambda k, *_: (0, pick(k), 0, 0) + zeros)


def whole(shape):
    zeros = (0,) * len(shape)
    return pl.BlockSpec(shape, lambda *_: zeros)


def low_pick(k):
    return jnp.minimum(k, 1)


def high_pick(k):
    return jnp.maximum(k - 2, 0)


def norm_stats(z):
    mean = jnp.mean(z, axis=1, keepdims=True)
    centered = z - mean
    inverse = lax.rsqrt(jnp.mean(centered * centered, axis=1, keepdims=True) + EPS)
    return centered * inverse, inverse


def norm_back(du, unit, inverse):
    return inverse * (
        du
        - jnp.mean(du, axis=1, keepdims=True)
        - unit * jnp.mean(du * unit, axis=1, keepdims=True)
    )


def gelu_pair(up):
    cdf = 0.5 + 0.5 * lax.erf(up * INV_SQRT2)
    pdf = INV_SQRT2PI * jnp.exp(-0.5 * (up * up))
    return up * cdf, cdf + up * pdf


SHARE = 10


def cost(flops, moved):
    return pl.CostEstimate(flops=flops * SHARE, bytes_accessed=moved * SHARE, transcendentals=0)


def params(mib=60, n=1):
    return pltpu.CompilerParams(
        dimension_semantics=("arbitrary",) * n, vmem_limit_bytes=mib * 1024 * 1024
    )


def load_pair(k, bits, wu, wd, ua0, ua1, db0, db1):
    @pl.when(k < 2)
    def _():
        assemble(wu, ua0, bits, False)
        assemble(wd, db0, bits, True)

    @pl.when(k >= 2)
    def _():
        assemble(wu, ua1, bits, False)
        assemble(wd, db1, bits, True)


def ffn_units(chunk, hid, wu, wd, act_o, gp_o, acc):
    rows = hid.shape[0]
    ats = [pl.ds(r * chunk, chunk) for r in range(rows // chunk)]
    ahead = dot_nn(hid[ats[0], :], wu[...])
    for r, at in enumerate(ats):
        act, gp = gelu_pair(ahead)
        if r + 1 < len(ats):
            ahead = dot_nn(hid[ats[r + 1], :], wu[...])
        act = act.astype(BF16)
        act_o[0, at, :] = act
        gp_o[0, at, :] = gp.astype(gp_o.dtype)
        acc[at, :] += dot_nt(act, wd[...])


def ffn_part_kernel(chunk, bits, hid, ua0, ua1, db0, db1, act_o, gp_o, acc, wu, wd):
    k = pl.program_id(0)
    load_pair(k, bits, wu, wd, ua0, ua1, db0, db1)

    @pl.when(k == 0)
    def _():
        acc[...] = hid[...].astype(F32)

    ffn_units(chunk, hid, wu, wd, act_o, gp_o, acc)


def ffn_part(bits, hid, ua0, ua1, db0, db1, units, chunk=512):
    rows, width = hid.shape
    p, n = ua0.shape[-2:]
    sds = jax.ShapeDtypeStruct
    col = pl.BlockSpec((1, rows, n), lambda k, *_: (k, 0, 0))
    return pl.pallas_call(
        functools.partial(ffn_part_kernel, chunk),
        out_shape=(sds((4, rows, units), BF16), sds((4, rows, units), GP), sds((rows, width), F32)),
        grid_spec=pltpu.PrefetchScalarGridSpec(
            num_scalar_prefetch=1, grid=(4,),
            in_specs=[whole((rows, width)), spec_a((p, n), low_pick), spec_a((p, n), high_pick),
                      spec_b((p, n), low_pick), spec_b((p, n), high_pick)],
            out_specs=[col, col, whole((rows, width))],
            scratch_shapes=[pltpu.VMEM((width, n), BF16), pltpu.VMEM((width, n), BF16)],
        ),
        compiler_params=params(32),
        cost_estimate=cost(4 * rows * width * 4 * n, 16 * rows * width),
    )(bits, hid, ua0, ua1, db0, db1)


def ffn_rest_kernel(chunk, bits, lens, hid, ua0, ua1, db0, db1, part, gain, bias, dout, act_i, gp_i,
                    act_o, gp_o, out, dsec, dffn, dffnt, dgain, dbias, wu, wd, acc):
    k = pl.program_id(0)
    rows = hid.shape[0]
    load_pair(k, bits, wu, wd, ua0, ua1, db0, db1)

    @pl.when(k == 0)
    def _():
        acc[...] = part[...]

    ffn_units(chunk, hid, wu, wd, act_o, gp_o, acc)

    @pl.when(k == 3)
    def _():
        length = rows // lens.shape[0]
        small = 256
        g = gain[...]
        b = bias[...]
        dg = jnp.zeros_like(g)
        db = jnp.zeros_like(g)
        for r in range(rows // small):
            at = pl.ds(r * small, small)
            size = lens[r * small // length]
            pos = (r * small % length) + lax.broadcasted_iota(jnp.int32, (small, 1), 0)
            valid = pos < size
            unit, inverse = norm_stats(acc[at, :])
            out[at, :] = jnp.where(valid, unit * g + b, 0.0).astype(BF16)
            dy = jnp.where(valid, dout[at, :].astype(F32), 0.0)
            dg += jnp.sum(dy * unit, axis=0, keepdims=True)
            db += jnp.sum(dy, axis=0, keepdims=True)
            dz = norm_back(dy * g, unit, inverse)
            dsec[at, :] = dz
            low = dz.astype(BF16)
            dffn[at, :] = low
            dffnt[:, at] = low.T
        dgain[...] = dg
        dbias[...] = db


def ffn_rest(bits, lens, hid, ua0, ua1, db0, db1, part, gain, bias, dout, act, gp, chunk=512):
    rows, width = hid.shape
    p, n = ua0.shape[-2:]
    last = act.shape[2] // n - 1
    sds = jax.ShapeDtypeStruct
    full = whole((rows, width))
    line = whole((1, width))
    col = pl.BlockSpec((1, rows, n), lambda k, *_: (k, 0, last))
    anywhere = pl.BlockSpec(memory_space=pl.ANY)
    return pl.pallas_call(
        functools.partial(ffn_rest_kernel, chunk),
        out_shape=(sds(act.shape, act.dtype), sds(gp.shape, gp.dtype), sds((rows, width), BF16), sds((rows, width), F32),
                   sds((rows, width), BF16), sds((width, rows), BF16), sds((1, width), F32), sds((1, width), F32)),
        grid_spec=pltpu.PrefetchScalarGridSpec(
            num_scalar_prefetch=2, grid=(4,),
            in_specs=[full, spec_a((p, n), low_pick), spec_a((p, n), high_pick),
                      spec_b((p, n), low_pick), spec_b((p, n), high_pick), full, line, line, full, anywhere, anywhere],
            out_specs=[col, col, full, full, full, whole((width, rows)), line, line],
            scratch_shapes=[pltpu.VMEM((width, n), BF16), pltpu.VMEM((width, n), BF16), pltpu.VMEM((rows, width), F32)],
        ),
        input_output_aliases={11: 0, 12: 1},
        compiler_params=params(46),
        cost_estimate=cost(4 * rows * width * 4 * n, 20 * rows * width),
    )(bits, lens, hid, ua0, ua1, db0, db1, part, gain, bias, dout, act, gp)


def down_grad_kernel(bits, dt, act, keep, send):
    k = pl.program_id(0)
    grad = dot_nn(dt[...], act[0]).astype(BF16)
    rows = keep.shape[-2]

    def put(ref):
        for d in range(8):
            piece(ref, bits, d, True)[...] = grad[d * rows : (d + 1) * rows]

    @pl.when(k < 2)
    def _():
        put(keep)

    @pl.when(k >= 2)
    def _():
        put(send)


def down_grads(bits, dt, act):
    width, rows = dt.shape
    n = act.shape[2]
    p = width // 8
    sds = jax.ShapeDtypeStruct
    return pl.pallas_call(
        down_grad_kernel,
        out_shape=(sds((2, 2, 2, 2, p, n), BF16), sds((2, 2, 2, 2, p, n), BF16)),
        grid_spec=pltpu.PrefetchScalarGridSpec(
            num_scalar_prefetch=1, grid=(4,),
            in_specs=[whole((width, rows)), pl.BlockSpec((1, rows, n), lambda k, *_: (k, 0, 0))],
            out_specs=[spec_b((p, n), low_pick), spec_b((p, n), high_pick)],
        ),
        compiler_params=params(22),
        cost_estimate=cost(2 * rows * width * 4 * n, 14 * rows * width),
    )(bits, dt, act)


def ffn_bwd_kernel(chunk, last, bits, ht, dffn, uap, uaq, dbp, dbq, gp, *rest):
    if last:
        dsec, part, unit, inverse, gain, gu, dfirst, dattn, dattnt, dgain, dbias, wu, wd, dup_s, acc = rest
    else:
        gu, acc, wu, wd, dup_s = rest
    k = pl.program_id(0)
    rows, width = dffn.shape
    np = uap.shape[-1]
    left, right = pl.ds(0, np), pl.ds(np, uaq.shape[-1])

    assemble(wu, uap, bits, False, left)
    assemble(wu, uaq, bits, False, right)
    assemble(wd, dbp, bits, True, left)
    assemble(wd, dbq, bits, True, right)

    @pl.when(k == 0)
    def _():
        if last:
            acc[...] = part[...] + dsec[...]
        else:
            acc[...] = jnp.zeros_like(acc)

    ats = [pl.ds(r * chunk, chunk) for r in range(rows // chunk)]
    ahead = dot_nn(dffn[ats[0], :], wd[...])
    for r, at in enumerate(ats):
        dup = (ahead * gp[0, at, :].astype(F32)).astype(BF16)
        if r + 1 < len(ats):
            ahead = dot_nn(dffn[ats[r + 1], :], wd[...])
        dup_s[at, :] = dup
        acc[at, :] += dot_nt(dup, wu[...])

    grad = dot_nn(ht[...], dup_s[...]).astype(BF16)
    p = gu.shape[-2]
    for d in range(8):
        piece(gu, bits, d, False)[...] = grad[d * p : (d + 1) * p]

    if last:

        @pl.when(k == 1)
        def _():
            small = 256
            g = gain[...]
            dg = jnp.zeros_like(g)
            db = jnp.zeros_like(g)
            for r in range(rows // small):
                at = pl.ds(r * small, small)
                dh = acc[at, :]
                u = unit[at, :]
                dg += jnp.sum(dh * u, axis=0, keepdims=True)
                db += jnp.sum(dh, axis=0, keepdims=True)
                dz = norm_back(dh * g, u, inverse[at, :])
                dfirst[at, :] = dz
                low = dz.astype(BF16)
                dattn[at, :] = low
                dattnt[:, at] = low.T
            dgain[...] = dg
            dbias[...] = db


def ffn_backward(last, bits, ht, dffn, uap, uaq, dbp, dbq, gp, extra=(), chunk=512):
    rows, width = dffn.shape
    p, np = uap.shape[-2:]
    nq = uaq.shape[-1]
    n = np + nq
    sds = jax.ShapeDtypeStruct
    off = 0 if last else 2
    pick = lambda k: k
    full = whole((rows, width))
    line = whole((1, width))
    out_shape = [sds((2, 2, 2, 2, p, n), BF16)]
    out_specs = [spec_a((p, n), pick)]
    in_specs = [
        whole((width, rows)), full,
        spec_a((p, np), pick), spec_a((p, nq), pick), spec_b((p, np), pick), spec_b((p, nq), pick),
        pl.BlockSpec((1, rows, n), lambda k, *_: (k + off, 0, 0)),
    ]
    scratch = [pltpu.VMEM((width, n), BF16), pltpu.VMEM((width, n), BF16), pltpu.VMEM((rows, n), BF16)]
    if last:
        in_specs += [full] * 3 + [whole((rows, 1)), line]
        out_shape += [sds((rows, width), F32), sds((rows, width), BF16), sds((width, rows), BF16), sds((1, width), F32), sds((1, width), F32)]
        out_specs += [full, full, whole((width, rows)), line, line]
        scratch += [pltpu.VMEM((rows, width), F32)]
    else:
        out_shape += [sds((rows, width), F32)]
        out_specs += [full]
    return pl.pallas_call(
        functools.partial(ffn_bwd_kernel, chunk, last),
        out_shape=out_shape,
        grid_spec=pltpu.PrefetchScalarGridSpec(
            num_scalar_prefetch=1, grid=(2,), in_specs=in_specs, out_specs=out_specs, scratch_shapes=scratch,
        ),
        compiler_params=params(56),
        cost_estimate=cost(6 * rows * width * 2 * n, 30 * rows * width),
    )(bits, ht, dffn, uap, uaq, dbp, dbq, gp, *extra)


def key_bias(size, length):
    pos = lax.broadcasted_iota(jnp.int32, (1, length), 1)
    return jnp.where(pos < size, 0.0, NEG).astype(F32)


def gate_rows(ga, gb, bits, i, d0, count):
    parts = []
    for j in range(count):
        d = d0 + j
        y = bits[0] ^ (d & 1)
        z1 = bits[1] ^ ((d >> 1) & 1)
        z2 = bits[2] ^ ((d >> 2) & 1)
        parts.append(ga[0, y, z1, z2, i])
        parts.append(gb[y, 0, z1, z2, i])
    return jnp.concatenate(parts, axis=0).astype(F32)


def att_fwd_kernel(bits, lens, qk, v, ga, gb, mixed, lse):
    length = qk.shape[1]
    heads = v.shape[2] // HEAD_DIM
    bias = key_bias(lens[pl.program_id(1)], length)
    count = length // (2 * ga.shape[-2])
    cols = [pl.ds(i * HEAD_DIM, HEAD_DIM) for i in range(2 * heads)]

    def score(i):
        return dot_nt(qk[0, :, cols[i]], qk[0, :, cols[heads + i]])

    ahead = score(0)
    outs = []
    stats = []
    for i in range(heads):
        s = ahead * (SCALE * LOG2E) + bias
        if i + 1 < heads:
            ahead = score(i + 1)
        top = jnp.max(s, axis=1, keepdims=True)
        e = jnp.exp2(s - top)
        total = jnp.sum(e, axis=1, keepdims=True)
        w = (e * gate_rows(ga, gb, bits, i, 0, count)).astype(BF16)
        outs.append(dot_nn(w, v[0, :, cols[i]]) * (1.0 / total))
        stats.append(top + jnp.log2(total))
    mixed[0] = jnp.concatenate(outs, axis=1).astype(BF16)
    lse[0] = jnp.concatenate(stats, axis=1)


def attention_forward(bits, lens, qk, v, ga, gb):
    _, rows, w2 = qk.shape
    w1 = v.shape[2]
    count = lens.shape[0]
    length = rows // count
    heads, sub, keys = ga.shape[-3:]
    sds = jax.ShapeDtypeStruct
    return pl.pallas_call(
        att_fwd_kernel,
        out_shape=(sds((2, rows, w1), BF16), sds((2, rows, heads), F32)),
        grid_spec=pltpu.PrefetchScalarGridSpec(
            num_scalar_prefetch=2, grid=(2, count),
            in_specs=[
                pl.BlockSpec((1, length, w2), lambda k, s, *_: (k, s, 0)),
                pl.BlockSpec((1, length, w1), lambda k, s, *_: (k, s, 0)),
                spec_a((heads, sub, keys), lambda k: k), spec_b((heads, sub, keys), lambda k: k),
            ],
            out_specs=[
                pl.BlockSpec((1, length, w1), lambda k, s, *_: (k, s, 0)),
                pl.BlockSpec((1, length, heads), lambda k, s, *_: (k, s, 0)),
            ],
        ),
        compiler_params=params(30, 2),
        cost_estimate=cost(16 * 2 * rows * length * w1, 16 * rows * w1),
    )(bits, lens, qk, v, ga, gb)


def att_bwd_kernel(last, bits, lens, qk, v, ga, gb, lse, dattn, wo, *rest):
    if last:
        ra, rb, dqk, dv, a_keep, a_send, b_keep, b_send, dm_s, dmt, qt, acc = rest
    else:
        dqk, dv, oga, ogb, dm_s, dmt, qt, acc = rest
    length = qk.shape[1]
    heads = v.shape[2] // HEAD_DIM
    hw = heads * HEAD_DIM
    k = pl.program_id(0)
    seq = pl.program_id(1)
    bias = key_bias(lens[seq], length)
    sub = ga.shape[-2]
    count = length // (2 * sub)
    cols = [pl.ds(i * HEAD_DIM, HEAD_DIM) for i in range(2 * heads)]

    dm = dot_nn(dattn[...], wo[0]).astype(BF16)
    dm_s[...] = dm
    dmt[...] = dm.T
    qt[...] = qk[0, :, pl.ds(0, hw)].T

    def products(i):
        return (
            dot_nt(qk[0, :, cols[i]], qk[0, :, cols[heads + i]]),
            dot_nt(dm_s[:, cols[i]], v[0, :, cols[i]]),
        )

    ahead = products(0)
    dqs, dks, dvs = [], [], []
    for i in range(heads):
        s, dw = ahead
        p = jnp.exp2(s * (SCALE * LOG2E) + bias - lse[0, :, pl.ds(i, 1)])
        if i + 1 < heads:
            ahead = products(i + 1)
        g = gate_rows(ga, gb, bits, i, 0, count)
        w = (p * g).astype(BF16)
        t = dw * p
        acc[i] = t + jnp.where(seq == 0, 0.0, acc[i])
        u = t * g
        ds = (u - p * jnp.sum(u, axis=1, keepdims=True)).astype(BF16)
        dqs.append(dot_nn(ds, qk[0, :, cols[heads + i]]) * SCALE)
        dvs.append(dot_nn(dmt[cols[i], :], w).astype(BF16).T)
        dks.append((dot_nn(qt[cols[i], :], ds) * SCALE).astype(BF16).T)
    dqk[0] = jnp.concatenate([d.astype(BF16) for d in dqs] + dks, axis=1)
    dv[0] = jnp.concatenate(dvs, axis=1)

    def first_rows(y, z1, z2):
        return pl.ds(pl.multiple_of(own(bits, y, z1, z2) * 2 * sub, sub), sub)

    def second_rows(y, z1, z2):
        return pl.ds(pl.multiple_of(own(bits, y, z1, z2) * 2 * sub + sub, sub), sub)

    @pl.when(seq == pl.num_programs(1) - 1)
    def _():
        if not last:
            for r in RELATIVE:
                for i in range(heads):
                    oga[(0,) + r + (i,)] = acc[i, first_rows(*r), :].astype(BF16)
                    ogb[(r[0], 0) + r[1:] + (i,)] = acc[i, second_rows(*r), :].astype(BF16)
            return

        def put_a(ref):
            for r in RELATIVE:
                for i in range(heads):
                    ref[r + (i,)] = (acc[i, first_rows(*r), :] + ra[(0,) + r + (i,)].astype(F32)).astype(BF16)

        @pl.when(k == 0)
        def _():
            put_a(a_keep)

        @pl.when(k == 1)
        def _():
            put_a(a_send)

        for r in RELATIVE:
            ref = b_send if r[0] else b_keep
            for i in range(heads):
                ref[(0,) + r[1:] + (i,)] = (
                    acc[i, second_rows(*r), :] + rb[(r[0], 0) + r[1:] + (i,)].astype(F32)
                ).astype(BF16)


def attention_backward(last, bits, lens, qk, v, ga, gb, lse, dattn, wo, got=()):
    _, rows, w2 = qk.shape
    w1 = v.shape[2]
    width = dattn.shape[1]
    count = lens.shape[0]
    length = rows // count
    tail = ga.shape[-3:]
    heads, sub, keys = tail
    sds = jax.ShapeDtypeStruct
    pick = lambda k: k
    in_specs = [
        pl.BlockSpec((1, length, w2), lambda k, s, *_: (k, s, 0)),
        pl.BlockSpec((1, length, w1), lambda k, s, *_: (k, s, 0)),
        spec_a(tail, pick), spec_b(tail, pick),
        pl.BlockSpec((1, length, heads), lambda k, s, *_: (k, s, 0)),
        pl.BlockSpec((length, width), lambda k, s, *_: (s, 0)),
        pl.BlockSpec((1, width, w1), lambda k, s, *_: (k, 0, 0)),
    ]
    out_shape = [sds((2, rows, w2), BF16), sds((2, rows, w1), BF16)]
    out_specs = [
        pl.BlockSpec((1, length, w2), lambda k, s, *_: (k, s, 0)),
        pl.BlockSpec((1, length, w1), lambda k, s, *_: (k, s, 0)),
    ]
    if last:
        in_specs += [spec_a(tail, pick), spec_b(tail, pick)]
        out_shape += [sds((2, 2, 2) + tail, BF16)] * 4
        out_specs += [whole((2, 2, 2) + tail)] * 2 + [
            pl.BlockSpec((1, 2, 2) + tail, lambda k, *_: (k, 0, 0, 0, 0, 0))
        ] * 2
    else:
        out_shape += [sds((2, 2, 2, 2) + tail, BF16)] * 2
        out_specs += [spec_a(tail, pick), spec_b(tail, pick)]
    return pl.pallas_call(
        functools.partial(att_bwd_kernel, last),
        out_shape=out_shape,
        grid_spec=pltpu.PrefetchScalarGridSpec(
            num_scalar_prefetch=2, grid=(2, count), in_specs=in_specs, out_specs=out_specs,
            scratch_shapes=[
                pltpu.VMEM((length, w1), BF16), pltpu.VMEM((w1, length), BF16),
                pltpu.VMEM((w1, length), BF16), pltpu.VMEM((heads, length, keys), F32),
            ],
        ),
        compiler_params=params(36, 2),
        cost_estimate=cost(40 * 2 * rows * length * w1, 30 * rows * w1),
    )(bits, lens, qk, v, ga, gb, lse, dattn, wo, *got)


def qkv_kernel(first, bits, x, wa, wb, qk, v, wqk, wv, wo, *rest):
    w1 = v.shape[2]
    wb_s = rest[-1]
    assemble(wqk.at[0], wa, bits, False)
    assemble(wb_s, wb, bits, True)

    if first:

        @pl.when(pl.program_id(0) == 0)
        def _():
            rest[0][...] = x[...].T

    wv[0] = wb_s[:, pl.ds(0, w1)]
    wo[0] = wb_s[:, pl.ds(w1, w1)]
    qk[0] = dot_nn(x[...], wqk[0]).astype(BF16)
    v[0] = dot_nn(x[...], wv[0]).astype(BF16)


def project(first, bits, x, wa, wb):
    rows, width = x.shape
    p, w2 = wa.shape[-2:]
    w1 = w2 // 2
    sds = jax.ShapeDtypeStruct
    pick = lambda k: k
    head = lambda s: pl.BlockSpec((1,) + s, lambda k, *_: (k, 0, 0))
    return pl.pallas_call(
        functools.partial(qkv_kernel, first),
        out_shape=[sds((2, rows, w2), BF16), sds((2, rows, w1), BF16), sds((2, width, w2), BF16),
                   sds((2, width, w1), BF16), sds((2, width, w1), BF16)]
        + ([sds((width, rows), BF16)] if first else []),
        grid_spec=pltpu.PrefetchScalarGridSpec(
            num_scalar_prefetch=1, grid=(2,),
            in_specs=[whole((rows, width)), spec_a((p, w2), pick), spec_b((p, w2), pick)],
            out_specs=[head((rows, w2)), head((rows, w1)), head((width, w2)), head((width, w1)), head((width, w1))]
            + ([whole((width, rows))] if first else []),
            scratch_shapes=[pltpu.VMEM((width, w2), BF16)],
        ),
        compiler_params=params(24),
        cost_estimate=cost(2 * rows * width * 2 * (w1 + w2), 8 * rows * width),
    )(bits, x, wa, wb)


def out_kernel(x, m0, m1, wo0, wo1, gain, bias, hid, unit, inverse, hidt):
    attn = dot_nt(m0[0], wo0[0]) + dot_nt(m0[1], wo0[1]) + dot_nt(m1[0], wo1[0]) + dot_nt(m1[1], wo1[1])
    u, inv = norm_stats(x[...].astype(F32) + attn)
    h = (u * gain[...] + bias[...]).astype(BF16)
    hid[...] = h
    hidt[...] = h.T
    unit[...] = u
    inverse[...] = inv


def out_forward(x, m0, m1, wo0, wo1, gain, bias, block=256):
    rows, width = x.shape
    w1 = wo0.shape[2]
    sds = jax.ShapeDtypeStruct
    row = lambda w: pl.BlockSpec((block, w), lambda r: (r, 0))
    mix = pl.BlockSpec((2, block, w1), lambda r: (0, r, 0))
    return pl.pallas_call(
        out_kernel,
        grid=(rows // block,),
        out_shape=(sds((rows, width), BF16), sds((rows, width), F32), sds((rows, 1), F32), sds((width, rows), BF16)),
        in_specs=[row(width), mix, mix, whole((2, width, w1)), whole((2, width, w1)), whole((1, width)), whole((1, width))],
        out_specs=[row(width), row(width), row(1), pl.BlockSpec((width, block), lambda r: (0, r))],
        compiler_params=params(20),
        cost_estimate=cost(2 * rows * width * 4 * w1, 12 * rows * width),
    )(x, m0, m1, wo0, wo1, gain, bias)


def qkv_grad_kernel(last, bits, xt, dat, dqk, dv, mixed, *rest):
    if last:
        ra, rb, a_keep, a_send, b_keep, b_send, ta, tb = rest
    else:
        ga, gb, ta, tb = rest
    w1 = dv.shape[2]
    k = pl.program_id(0)
    ta[...] = dot_nn(xt[...], dqk[0]).astype(ta.dtype)
    tb[:, pl.ds(0, w1)] = dot_nn(xt[...], dv[0]).astype(tb.dtype)
    tb[:, pl.ds(w1, w1)] = dot_nn(dat[...], mixed[0]).astype(tb.dtype)
    if not last:
        scatter(ga, ta, bits, False)
        scatter(gb, tb, bits, True)
        return
    p = ra.shape[-2]

    def rows(r):
        return pl.ds(pl.multiple_of(own(bits, *r) * p, 16), p)

    def put_a(ref):
        for r in RELATIVE:
            ref[r] = (ta[rows(r), :] + ra[(0,) + r].astype(F32)).astype(BF16)

    @pl.when(k == 0)
    def _():
        put_a(a_keep)

    @pl.when(k == 1)
    def _():
        put_a(a_send)

    for r in RELATIVE:
        ref = b_send if r[0] else b_keep
        ref[(0,) + r[1:]] = (tb[rows(r), :] + rb[(r[0], 0) + r[1:]].astype(F32)).astype(BF16)


def qkv_grads(last, bits, xt, dat, dqk, dv, mixed, got=()):
    width, rows = xt.shape
    w2 = dqk.shape[2]
    w1 = dv.shape[2]
    per = width // 8
    sds = jax.ShapeDtypeStruct
    pick = lambda k: k
    head = lambda w: pl.BlockSpec((1, rows, w), lambda k, *_: (k, 0, 0))
    in_specs = [whole((width, rows)), whole((width, rows)), head(w2), head(w1), head(w1)]
    if last:
        in_specs += [spec_a((per, w2), pick), spec_b((per, w2), pick)]
        out_shape = [sds((2, 2, 2, per, w2), BF16)] * 4
        out_specs = [whole((2, 2, 2, per, w2))] * 2 + [
            pl.BlockSpec((1, 2, 2, per, w2), lambda k, *_: (k, 0, 0, 0, 0))
        ] * 2
    else:
        out_shape = [sds((2, 2, 2, 2, per, w2), BF16)] * 2
        out_specs = [spec_a((per, w2), pick), spec_b((per, w2), pick)]
    kind = F32 if last else BF16
    return pl.pallas_call(
        functools.partial(qkv_grad_kernel, last),
        out_shape=out_shape,
        grid_spec=pltpu.PrefetchScalarGridSpec(
            num_scalar_prefetch=1, grid=(2,), in_specs=in_specs, out_specs=out_specs,
            scratch_shapes=[pltpu.VMEM((width, w2), kind), pltpu.VMEM((width, w2), kind)],
        ),
        compiler_params=params(26),
        cost_estimate=cost(2 * rows * width * 2 * 2 * w2, 8 * rows * width),
    )(bits, xt, dat, dqk, dv, mixed, *got)


def dinput_kernel(dfirst, dqk0, dqk1, dv0, dv1, wqk0, wqk1, wv0, wv1, out):
    total = dfirst[...]
    for a, b, wa, wb in ((dqk0, dv0, wqk0, wv0), (dqk1, dv1, wqk1, wv1)):
        for k in range(2):
            total = total + dot_nt(a[k], wa[k]) + dot_nt(b[k], wb[k])
    out[...] = total


def input_backward(dfirst, dqk0, dqk1, dv0, dv1, wqk0, wqk1, wv0, wv1, block=256):
    rows, width = dfirst.shape
    w2 = wqk0.shape[2]
    w1 = wv0.shape[2]
    row = pl.BlockSpec((block, width), lambda r: (r, 0))
    part = lambda w: pl.BlockSpec((2, block, w), lambda r: (0, r, 0))
    return pl.pallas_call(
        dinput_kernel,
        grid=(rows // block,),
        out_shape=jax.ShapeDtypeStruct((rows, width), F32),
        in_specs=[row, part(w2), part(w2), part(w1), part(w1)]
        + [whole((2, width, w2))] * 2 + [whole((2, width, w1))] * 2,
        out_specs=row,
        compiler_params=params(24),
        cost_estimate=cost(2 * rows * width * 4 * (w1 + w2), 14 * rows * width),
    )(dfirst, dqk0, dqk1, dv0, dv1, wqk0, wqk1, wv0, wv1)


GROUPS = 8


def partner_dp(value, bit):
    size = lax.axis_size("dp")
    step = (1 << bit) * (size // GROUPS)
    return lax.ppermute(value, "dp", [(i, i ^ step) for i in range(size)])


def partner_head(value, bit):
    size = lax.axis_size("head")
    return lax.ppermute(value, "head", [(i, i ^ (1 << bit)) for i in range(size)])


def over_y(value):
    return partner_dp(value, 0)


def over_near(value):
    return partner_dp(value, 1)


def over_far(value):
    return partner_dp(value, 2)


def over_pair(value):
    return partner_head(value, 0)


def over_x(value):
    return partner_head(value, 1)


def inner_groups():
    inner = lax.axis_size("dp") // GROUPS
    return inner, [[g * inner + i for i in range(inner)] for g in range(GROUPS)]


def inner_gather(value, axis):
    inner, groups = inner_groups()
    if inner == 1:
        return value
    return lax.all_gather(value, "dp", axis_index_groups=groups, axis=axis, tiled=True)


def inner_scatter(value, axis):
    inner, groups = inner_groups()
    if inner == 1:
        return value
    return lax.psum_scatter(value, "dp", axis_index_groups=groups, scatter_dimension=axis, tiled=True)


def after(values, *waits):
    return lax.optimization_barrier((tuple(values), waits))[0]


def wide(value):
    return value.astype(F32)


def first_sum(keep, got):
    return (wide(keep[1]) + wide(got[1])).astype(BF16)


def second_sum(keep, got, more):
    return (wide(keep[0, 1]) + wide(got[0, 1]) + wide(more[1])).astype(BF16)


def third_sum(keep, got, more, last):
    return wide(keep[0, 0]) + wide(got[0, 0]) + wide(more[0]) + wide(last)


def low_sum(keep, got):
    return (wide(keep[1]) + wide(got[1])).astype(BF16)


def high_sum(keep, got, more):
    return wide(keep[0]) + wide(got[0]) + wide(more)


def total_steps():
    steps = []
    for name in ("head", "dp"):
        size = lax.axis_size(name)
        step = 1
        while step < size:
            steps.append((name, [(i, i ^ step) for i in range(size)]))
            step *= 2
    return steps


def total_some(value, *steps):
    for name, pairs in steps:
        value = value + lax.ppermute(value, name, pairs)
    return value


def per_device(layer_input, output_grad, lengths, w_qkv, w_out, w_up, w_down,
               norm_gains, norm_biases, mask_logits, mask_noise):
    micro, seq, width = layer_input.shape
    rows = micro * seq
    x = layer_input.reshape(rows, width)
    dout = output_grad.reshape(rows, width)
    place = lax.axis_index("dp") // (lax.axis_size("dp") // GROUPS)
    bits = jnp.stack([place & 1, (place >> 1) & 1, (place >> 2) & 1]).astype(jnp.int32)
    lens = lax.dynamic_slice_in_dim(lengths, lax.axis_index("head"), 1, 1).reshape(micro)

    gate_part = jax.nn.sigmoid(mask_logits + mask_noise)
    gate_all = inner_gather(gate_part.astype(BF16), 1)
    sub = gate_all.shape[1] // 2
    gain1, gain2 = norm_gains[0:1], norm_gains[1:2]
    bias1, bias2 = norm_biases[0:1], norm_biases[1:2]

    ga = jnp.stack([
        inner_gather(jnp.concatenate([w_qkv[0], w_qkv[1]], axis=1), 0),
        inner_gather(jnp.concatenate([w_qkv[2], w_out.T], axis=1), 0),
    ])
    gb = jnp.stack([gate_all[:, :sub], gate_all[:, sub:]])
    up_all, down_all = inner_gather(w_up, 0), inner_gather(w_down.T, 0)
    units = up_all.shape[1]
    most = units * 2 // 3
    gc = jnp.stack([up_all[:, :most], down_all[:, :most]])
    ge = jnp.stack([up_all[:, most:], down_all[:, most:]])

    got = over_far(ga)
    ga = jnp.stack([ga, got], axis=1)
    got = over_near(ga)
    ga = jnp.stack([ga, got], axis=1)
    aa, ab = ga[0], ga[1]
    (gb,) = after((gb,), got)
    ra, rb = over_y(aa), over_x(ab)
    far_b = over_far(gb)
    aa, ab = jnp.stack([aa, ra]), jnp.stack([ab, rb])
    gb, = after((gb,), ra, rb)
    gb = jnp.stack([gb, far_b], axis=1)
    aa, ab = after((aa, ab), gb)
    ra, rb = over_x(aa), over_y(ab)
    near_b = over_near(gb)
    (gc,) = after((gc,), near_b)
    far_c = over_far(gc)
    gb = jnp.stack([gb, near_b], axis=1)
    ba, bb = gb[0], gb[1]
    aa, ab = jnp.stack([aa, ra]), jnp.stack([ab, rb])
    ba, bb = after((ba, bb), ra, rb)
    ca, cb = over_pair(aa), over_pair(ab)
    ra, rb = over_y(ba), over_x(bb)
    qk0, v0, wqk0, wv0, wo0, xt = project(True, bits, x, aa, ab)
    ba, bb = jnp.stack([ba, ra]), jnp.stack([bb, rb])
    ba, bb, gc, ca, cb = after((ba, bb, gc, ca, cb), qk0, ra, rb)
    ra, rb = over_x(ba), over_y(bb)
    gc = jnp.stack([gc, far_c], axis=1)
    near_c = over_near(gc)
    qk1, v1, wqk1, wv1, wo1 = project(False, bits, x, ca, cb)
    ba, bb = jnp.stack([ba, ra]), jnp.stack([bb, rb])
    gc = jnp.stack([gc, near_c], axis=1)
    fa, fb = gc[0], gc[1]
    fa, fb, ba, bb, ge = after((fa, fb, ba, bb, ge), ra, rb, near_c, qk1)
    ba1, bb1 = over_pair(ba), over_pair(bb)
    ra, rb = over_y(fa), over_x(fb)
    far_e = over_far(ge)
    m0, lse0 = attention_forward(bits, lens, qk0, v0, ba, bb)
    fa, fb = jnp.stack([fa, ra]), jnp.stack([fb, rb])
    ge = jnp.stack([ge, far_e], axis=1)
    fa, fb, ge, ba1, bb1 = after((fa, fb, ge, ba1, bb1), m0)
    ra, rb = over_x(fa), over_y(fb)
    near_e = over_near(ge)
    ge = jnp.stack([ge, near_e], axis=1)
    m1, lse1 = attention_forward(bits, lens, qk1, v1, ba1, bb1)
    hid, unit, inverse, hidt = out_forward(x, m0, m1, wo0, wo1, gain1, bias1)
    fa, fb = jnp.stack([fa, ra]), jnp.stack([fb, rb])
    ea, eb = ge[0], ge[1]
    fa, fb, ea, eb = after((fa, fb, ea, eb), hid, ra, rb)
    fa1, fb1 = over_pair(fa), over_pair(fb)
    ra, rb = over_y(ea), over_x(eb)
    ea, eb = jnp.stack([ea, ra]), jnp.stack([eb, rb])
    ea, eb, hid = after((ea, eb, hid), fa1, fb1)
    ra, rb = over_x(ea), over_y(eb)
    act, gp, part = ffn_part(bits, hid, fa, fa1, fb, fb1, units)
    ea, eb = jnp.stack([ea, ra]), jnp.stack([eb, rb])
    ea, eb = after((ea, eb), part)
    ea1, eb1 = over_pair(ea), over_pair(eb)
    act, gp, out, dsec, dffn, dffnt, dgain2, dbias2 = ffn_rest(
        bits, lens, hid, ea, ea1, eb, eb1, part, gain2, bias2, dout, act, gp
    )

    steps = total_steps()
    down0, down1 = down_grads(bits, dffnt, act)
    cd = over_pair(down1)
    dffn, = after((dffn,), down1)
    up1, part = ffn_backward(False, bits, hidt, dffn, fa1, ea1, fb1, eb1, gp)
    down0, cd, up1, dffn = after((down0, cd, up1, dffn), part)
    xd = over_y(first_sum(down0, cd))
    cu = over_pair(up1)
    up0, dfirst, dattn, dattnt, dgain1, dbias1 = ffn_backward(
        True, bits, hidt, dffn, fa, ea, fb, eb, gp, (dsec, part, unit, inverse, gain1)
    )
    up0, cu, norms, dattn = after((up0, cu, jnp.concatenate([dgain1, dgain2, dbias1, dbias2]), dattn), up0)
    xu = over_x(first_sum(up0, cu))
    norms = total_some(norms, steps[0])
    dqk1, dv1, ga1, gb1 = attention_backward(False, bits, lens, qk1, v1, ba1, bb1, lse1, dattn, wo1)
    ga1, gb1, norms, dqk1, xd = after((ga1, gb1, norms, dqk1, xd), dv1)
    cga, cgb = over_pair(ga1), over_pair(gb1)
    norms = total_some(norms, steps[3])
    qka1, vo1 = qkv_grads(False, bits, xt, dattnt, dqk1, dv1, m1)
    qka1, vo1, dattn, norms, cga, cgb, xu, xd = after((qka1, vo1, dattn, norms, cga, cgb, xu, xd), vo1)
    cqk, cvo = over_pair(qka1), over_pair(vo1)
    norms = total_some(norms, steps[4])
    yd, yu = over_x(second_sum(down0, cd, xd)), over_y(second_sum(up0, cu, xu))
    dqk0, dv0, ga0, ga_out, gb0, gb_out = attention_backward(
        True, bits, lens, qk0, v0, ba, bb, lse0, dattn, wo0, (cga, cgb)
    )
    ga_out, gb_out, dqk0, norms, cqk, cvo, yd, yu = after((ga_out, gb_out, dqk0, norms, cqk, cvo, yd, yu), dv0)
    xga, xgb = over_x(ga_out), over_y(gb_out)
    u, d = third_sum(up0, cu, xu, yu), third_sum(down0, cd, xd, yd)
    near_f = over_near(jnp.stack([u[1], d[1]]).astype(BF16))
    qka0, qka_out, vo0, vo_out = qkv_grads(True, bits, xt, dattnt, dqk0, dv0, m0, (cqk, cvo))
    qka_out, vo_out, near_f, xga, xgb, dqk0 = after((qka_out, vo_out, near_f, xga, xgb, dqk0), vo0)
    xqk, xvo = over_x(qka_out), over_y(vo_out)
    yga, ygb = over_y(low_sum(ga0, xga)), over_x(low_sum(gb0, xgb))
    far_f = over_far(jnp.stack([u[0, 1] + wide(near_f[0, 1]), d[0, 1] + wide(near_f[1, 1])]).astype(BF16))
    dinput = input_backward(dfirst, dqk0, dqk1, dv0, dv1, wqk0, wqk1, wv0, wv1)
    xqk, xvo, yga, ygb, norms, far_f = after((xqk, xvo, yga, ygb, norms, far_f), dinput)
    norms = total_some(norms, steps[1])
    send_qk, send_vo = low_sum(qka0, xqk), low_sum(vo0, xvo)
    g1, g2 = high_sum(ga0, xga, yga), high_sum(gb0, xgb, ygb)
    send_g = jnp.stack([g1[1], g2[1]]).astype(BF16)
    send_qk, send_vo, send_g, norms = after((send_qk, send_vo, send_g, norms), norms)
    yqk, yvo = over_y(send_qk), over_x(send_vo)
    near_g = over_near(send_g)
    norms, = after((norms,), yqk, yvo)
    norms = total_some(norms, *steps[2:3], *steps[5:])
    w1, w2 = high_sum(qka0, xqk, yqk), high_sum(vo0, xvo, yvo)
    send_w = jnp.stack([w1[1], w2[1]]).astype(BF16)
    send_g = jnp.stack([g1[0, 1] + wide(near_g[0, 1]), g2[0, 1] + wide(near_g[1, 1])]).astype(BF16)
    near_w = over_near(send_w)
    far_g = over_far(send_g)
    far_w = over_far(jnp.stack([w1[0, 1] + wide(near_w[0, 1]), w2[0, 1] + wide(near_w[1, 1])]).astype(BF16))

    up_grad = u[0, 0] + wide(near_f[0, 0]) + wide(far_f[0])
    down_grad = d[0, 0] + wide(near_f[1, 0]) + wide(far_f[1])
    gate_a = g1[0, 0] + wide(near_g[0, 0]) + wide(far_g[0])
    gate_b = g2[0, 0] + wide(near_g[1, 0]) + wide(far_g[1])
    qk_grad = w1[0, 0] + wide(near_w[0, 0]) + wide(far_w[0])
    vo_grad = w2[0, 0] + wide(near_w[1, 0]) + wide(far_w[1])

    qk_grad, vo_grad = inner_scatter(qk_grad, 0), inner_scatter(vo_grad, 0)
    local = vo_grad.shape[1] // 2
    gate_grad = inner_scatter(jnp.concatenate([gate_a, gate_b], axis=1), 1)
    return (
        out.reshape(micro, seq, width),
        dinput.reshape(micro, seq, width),
        jnp.stack([qk_grad[:, :local], qk_grad[:, local:], vo_grad[:, :local]]),
        vo_grad[:, local:].T,
        inner_scatter(up_grad, 0),
        inner_scatter(down_grad, 0).T,
        norms[:2],
        norms[2:],
        gate_grad * gate_part * (1.0 - gate_part),
    )


def solution(mesh):
    rows = P(None, ("dp", "head"), None)
    gates = P("head", "dp", None)
    weights = (P(None, "dp", "head"), P("head", "dp"), P("dp", "head"), P("head", "dp"))
    return jax.shard_map(
        per_device,
        mesh=mesh,
        in_specs=(rows, rows, P(None, "dp")) + weights + (P(), P(), gates, gates),
        out_specs=(rows, rows) + weights + (P(), P(), gates),
        check_vma=False,
    )
```

```python
import functools, math
import jax, jax.numpy as jnp
from jax import lax
from jax.experimental import pallas as pl
from jax.experimental.pallas import tpu as pltpu
from jax.sharding import PartitionSpec as P

HEAD_DIM = 64
EPS = 1e-05
F32 = jnp.float32
BF16 = jnp.bfloat16
GP = jnp.bfloat16
SCALE = 1.0 / math.sqrt(HEAD_DIM)
LOG2E = math.log2(math.e)
NEG = -1e30
INV_SQRT2 = 1.0 / math.sqrt(2.0)
INV_SQRT2PI = 1.0 / math.sqrt(2.0 * math.pi)


def dot_nn(a, b):
    return lax.dot_general(a, b, (((1,), (0,)), ((), ())), preferred_element_type=F32)


def dot_nt(a, b):
    return lax.dot_general(a, b, (((1,), (1,)), ((), ())), preferred_element_type=F32)


def dot_tn(a, b):
    return lax.dot_general(a, b, (((0,), (0,)), ((), ())), preferred_element_type=F32)


def piece(ref, bits, d, flip):
    y = bits[0] ^ (d & 1)
    z1 = bits[1] ^ ((d >> 1) & 1)
    z2 = bits[2] ^ ((d >> 2) & 1)
    if flip:
        return ref.at[y, 0, z1, z2]
    return ref.at[0, y, z1, z2]


def assemble(dst, ref, bits, flip, cols=None):
    rows = ref.shape[-2]
    cols = pl.ds(0, ref.shape[-1]) if cols is None else cols
    for d in range(8):
        dst[pl.ds(d * rows, rows), cols] = piece(ref, bits, d, flip)[...]


def scatter(ref, src, bits, flip):
    rows = ref.shape[-2]
    for d in range(8):
        piece(ref, bits, d, flip)[...] = src[pl.ds(d * rows, rows), :]


def own(bits, y, z1, z2):
    return (bits[0] ^ y) + 2 * (bits[1] ^ z1) + 4 * (bits[2] ^ z2)


RELATIVE = [(y, z1, z2) for y in range(2) for z1 in range(2) for z2 in range(2)]


def spec_a(tail, pick):
    zeros = (0,) * len(tail)
    return pl.BlockSpec((1, 2, 2, 2) + tail, lambda k, *_: (pick(k), 0, 0, 0) + zeros)


def spec_b(tail, pick):
    zeros = (0,) * len(tail)
    return pl.BlockSpec((2, 1, 2, 2) + tail, lambda k, *_: (0, pick(k), 0, 0) + zeros)


def whole(shape):
    zeros = (0,) * len(shape)
    return pl.BlockSpec(shape, lambda *_: zeros, pipeline_mode=pl.Buffered(1))


def low_pick(k):
    return jnp.minimum(k, 1)


def high_pick(k):
    return jnp.maximum(k - 2, 0)


def norm_stats(z):
    mean = jnp.mean(z, axis=1, keepdims=True)
    centered = z - mean
    inverse = lax.rsqrt(jnp.mean(centered * centered, axis=1, keepdims=True) + EPS)
    return centered * inverse, inverse


def norm_back(du, unit, inverse):
    return inverse * (
        du
        - jnp.mean(du, axis=1, keepdims=True)
        - unit * jnp.mean(du * unit, axis=1, keepdims=True)
    )


def gelu_pair(up):
    cdf = 0.5 + 0.5 * lax.erf(up * INV_SQRT2)
    pdf = INV_SQRT2PI * jnp.exp(-0.5 * (up * up))
    return up * cdf, cdf + up * pdf


SHARE = 10


def cost(flops, moved):
    return pl.CostEstimate(flops=flops * SHARE, bytes_accessed=moved * SHARE, transcendentals=0)


def params(mib=60, n=1):
    return pltpu.CompilerParams(
        dimension_semantics=("arbitrary",) * n, vmem_limit_bytes=mib * 1024 * 1024
    )


def load_pair(k, bits, wu, wd, ua0, ua1, db0, db1):
    @pl.when(k < 2)
    def _():
        assemble(wu, ua0, bits, False)
        assemble(wd, db0, bits, True)

    @pl.when(k >= 2)
    def _():
        assemble(wu, ua1, bits, False)
        assemble(wd, db1, bits, True)


def ffn_units(chunk, hid, wu, wd, act_o, gp_o, acc):
    rows = hid.shape[0]
    ats = [pl.ds(r * chunk, chunk) for r in range(rows // chunk)]
    ahead = dot_nn(hid[ats[0], :], wu[...])
    for r, at in enumerate(ats):
        act, gp = gelu_pair(ahead)
        if r + 1 < len(ats):
            ahead = dot_nn(hid[ats[r + 1], :], wu[...])
        act = act.astype(BF16)
        act_o[0, at, :] = act
        gp_o[0, at, :] = gp.astype(gp_o.dtype)
        acc[at, :] += dot_nt(act, wd[...])


def ffn_part_kernel(chunk, bits, hid, ua0, ua1, db0, db1, act_o, gp_o, acc, wu, wd):
    k = pl.program_id(0)
    load_pair(k, bits, wu, wd, ua0, ua1, db0, db1)

    @pl.when(k == 0)
    def _():
        acc[...] = hid[...].astype(F32)

    ffn_units(chunk, hid, wu, wd, act_o, gp_o, acc)


def ffn_part(bits, hid, ua0, ua1, db0, db1, chunk=512):
    rows, width = hid.shape
    p, n = ua0.shape[-2:]
    sds = jax.ShapeDtypeStruct
    col = pl.BlockSpec((1, rows, n), lambda k, *_: (k, 0, 0))
    return pl.pallas_call(
        functools.partial(ffn_part_kernel, chunk),
        out_shape=(sds((4, rows, n), BF16), sds((4, rows, n), GP), sds((rows, width), F32)),
        grid_spec=pltpu.PrefetchScalarGridSpec(
            num_scalar_prefetch=1, grid=(4,),
            in_specs=[whole((rows, width)), spec_a((p, n), low_pick), spec_a((p, n), high_pick),
                      spec_b((p, n), low_pick), spec_b((p, n), high_pick)],
            out_specs=[col, col, whole((rows, width))],
            scratch_shapes=[pltpu.VMEM((width, n), BF16), pltpu.VMEM((width, n), BF16)],
        ),
        compiler_params=params(26),
        cost_estimate=cost(4 * rows * width * 4 * n, 16 * rows * width),
    )(bits, hid, ua0, ua1, db0, db1)


def ffn_rest_kernel(chunk, bits, lens, hid, ua0, ua1, db0, db1, part, gain, bias, dout,
                    act_o, gp_o, out, acc, dffn, dffnt, dgain, dbias, wu, wd):
    k = pl.program_id(0)
    rows = hid.shape[0]
    load_pair(k, bits, wu, wd, ua0, ua1, db0, db1)

    @pl.when(k == 0)
    def _():
        acc[...] = part[...]

    ffn_units(chunk, hid, wu, wd, act_o, gp_o, acc)

    @pl.when(k == 3)
    def _():
        length = rows // lens.shape[0]
        small = 256
        g = gain[...]
        b = bias[...]
        dg = jnp.zeros_like(g)
        db = jnp.zeros_like(g)
        for r in range(rows // small):
            at = pl.ds(r * small, small)
            size = lens[r * small // length]
            pos = (r * small % length) + lax.broadcasted_iota(jnp.int32, (small, 1), 0)
            valid = pos < size
            unit, inverse = norm_stats(acc[at, :])
            out[at, :] = jnp.where(valid, unit * g + b, 0.0).astype(BF16)
            dy = jnp.where(valid, dout[at, :].astype(F32), 0.0)
            dg += jnp.sum(dy * unit, axis=0, keepdims=True)
            db += jnp.sum(dy, axis=0, keepdims=True)
            dz = norm_back(dy * g, unit, inverse)
            acc[at, :] = dz
            low = dz.astype(BF16)
            dffn[at, :] = low
            dffnt[:, at] = low.T
        dgain[...] = dg
        dbias[...] = db


def ffn_rest(bits, lens, hid, ua0, ua1, db0, db1, part, gain, bias, dout, chunk=512):
    rows, width = hid.shape
    p, n = ua0.shape[-2:]
    sds = jax.ShapeDtypeStruct
    full = whole((rows, width))
    line = whole((1, width))
    col = pl.BlockSpec((1, rows, n), lambda k, *_: (k, 0, 0))
    return pl.pallas_call(
        functools.partial(ffn_rest_kernel, chunk),
        out_shape=(sds((4, rows, n), BF16), sds((4, rows, n), GP), sds((rows, width), BF16), sds((rows, width), F32),
                   sds((rows, width), BF16), sds((width, rows), BF16), sds((1, width), F32), sds((1, width), F32)),
        grid_spec=pltpu.PrefetchScalarGridSpec(
            num_scalar_prefetch=2, grid=(4,),
            in_specs=[full, spec_a((p, n), low_pick), spec_a((p, n), high_pick),
                      spec_b((p, n), low_pick), spec_b((p, n), high_pick), full, line, line, full],
            out_specs=[col, col, full, full, full, whole((width, rows)), line, line],
            scratch_shapes=[pltpu.VMEM((width, n), BF16), pltpu.VMEM((width, n), BF16)],
        ),
        compiler_params=params(30),
        cost_estimate=cost(4 * rows * width * 4 * n, 20 * rows * width),
    )(bits, lens, hid, ua0, ua1, db0, db1, part, gain, bias, dout)


def down_grad_kernel(bits, dt, actp, actq, keep, send):
    k = pl.program_id(0)
    first = dot_nn(dt[...], actp[0]).astype(BF16)
    second = dot_nn(dt[...], actq[0]).astype(BF16)
    rows = keep.shape[-2]
    n = actp.shape[2]

    def put(ref):
        for d in range(8):
            at = piece(ref, bits, d, True)
            at[:, pl.ds(0, n)] = first[d * rows : (d + 1) * rows]
            at[:, pl.ds(n, actq.shape[2])] = second[d * rows : (d + 1) * rows]

    @pl.when(k < 2)
    def _():
        put(keep)

    @pl.when(k >= 2)
    def _():
        put(send)


def down_grads(bits, dt, actp, actq):
    width, rows = dt.shape
    col = lambda a: pl.BlockSpec((1, rows, a.shape[2]), lambda k, *_: (k, 0, 0))
    n = actp.shape[2] + actq.shape[2]
    p = width // 8
    sds = jax.ShapeDtypeStruct
    return pl.pallas_call(
        down_grad_kernel,
        out_shape=(sds((2, 2, 2, 2, p, n), BF16), sds((2, 2, 2, 2, p, n), BF16)),
        grid_spec=pltpu.PrefetchScalarGridSpec(
            num_scalar_prefetch=1, grid=(4,),
            in_specs=[whole((width, rows)), col(actp), col(actq)],
            out_specs=[spec_b((p, n), low_pick), spec_b((p, n), high_pick)],
        ),
        compiler_params=params(22),
        cost_estimate=cost(2 * rows * width * 4 * n, 14 * rows * width),
    )(bits, dt, actp, actq)


def ffn_bwd_kernel(chunk, last, bits, ht, dffn, uap, uaq, dbp, dbq, gpp, gpq, *rest):
    if last:
        dsec, part, unit, inverse, gain, gu, acc, dattn, dattnt, dgain, dbias, wu, wd, dup_s = rest
    else:
        gu, acc, wu, wd, dup_s = rest
    k = pl.program_id(0)
    rows, width = dffn.shape
    np = uap.shape[-1]
    left, right = pl.ds(0, np), pl.ds(np, uaq.shape[-1])

    assemble(wu, uap, bits, False, left)
    assemble(wu, uaq, bits, False, right)
    assemble(wd, dbp, bits, True, left)
    assemble(wd, dbq, bits, True, right)

    @pl.when(k == 0)
    def _():
        if last:
            acc[...] = part[...] + dsec[...]
        else:
            acc[...] = jnp.zeros_like(acc)

    ats = [pl.ds(r * chunk, chunk) for r in range(rows // chunk)]
    ahead = dot_nn(dffn[ats[0], :], wd[...])
    for r, at in enumerate(ats):
        dup_s[at, left] = (ahead[:, :np] * gpp[0, at, :].astype(F32)).astype(BF16)
        dup_s[at, right] = (ahead[:, np:] * gpq[0, at, :].astype(F32)).astype(BF16)
        if r + 1 < len(ats):
            ahead = dot_nn(dffn[ats[r + 1], :], wd[...])
        acc[at, :] += dot_nt(dup_s[at, :], wu[...])

    grad = dot_nn(ht[...], dup_s[...]).astype(BF16)
    p = gu.shape[-2]
    for d in range(8):
        piece(gu, bits, d, False)[...] = grad[d * p : (d + 1) * p]

    if last:

        @pl.when(k == 1)
        def _():
            small = 256
            g = gain[...]
            dg = jnp.zeros_like(g)
            db = jnp.zeros_like(g)
            for r in range(rows // small):
                at = pl.ds(r * small, small)
                dh = acc[at, :]
                u = unit[at, :]
                dg += jnp.sum(dh * u, axis=0, keepdims=True)
                db += jnp.sum(dh, axis=0, keepdims=True)
                dz = norm_back(dh * g, u, inverse[at, :])
                acc[at, :] = dz
                low = dz.astype(BF16)
                dattn[at, :] = low
                dattnt[:, at] = low.T
            dgain[...] = dg
            dbias[...] = db


def ffn_backward(last, bits, ht, dffn, uap, uaq, dbp, dbq, gpp, gpq, extra=(), chunk=512):
    rows, width = dffn.shape
    p, np = uap.shape[-2:]
    nq = uaq.shape[-1]
    n = np + nq
    sds = jax.ShapeDtypeStruct
    off = 0 if last else 2
    pick = lambda k: k
    full = whole((rows, width))
    line = whole((1, width))
    out_shape = [sds((2, 2, 2, 2, p, n), BF16)]
    out_specs = [spec_a((p, n), pick)]
    in_specs = [
        whole((width, rows)), full,
        spec_a((p, np), pick), spec_a((p, nq), pick), spec_b((p, np), pick), spec_b((p, nq), pick),
        pl.BlockSpec((1, rows, np), lambda k, *_: (k + off, 0, 0)),
        pl.BlockSpec((1, rows, nq), lambda k, *_: (k + off, 0, 0)),
    ]
    scratch = [pltpu.VMEM((width, n), BF16), pltpu.VMEM((width, n), BF16), pltpu.VMEM((rows, n), BF16)]
    if last:
        in_specs += [full] * 3 + [whole((rows, 1)), line]
        out_shape += [sds((rows, width), F32), sds((rows, width), BF16), sds((width, rows), BF16), sds((1, width), F32), sds((1, width), F32)]
        out_specs += [full, full, whole((width, rows)), line, line]
    else:
        out_shape += [sds((rows, width), F32)]
        out_specs += [full]
    return pl.pallas_call(
        functools.partial(ffn_bwd_kernel, chunk, last),
        out_shape=out_shape,
        grid_spec=pltpu.PrefetchScalarGridSpec(
            num_scalar_prefetch=1, grid=(2,), in_specs=in_specs, out_specs=out_specs, scratch_shapes=scratch,
        ),
        compiler_params=params(36),
        cost_estimate=cost(6 * rows * width * 2 * n, 30 * rows * width),
    )(bits, ht, dffn, uap, uaq, dbp, dbq, gpp, gpq, *extra)


def key_bias(size, length):
    pos = lax.broadcasted_iota(jnp.int32, (1, length), 1)
    return jnp.where(pos < size, 0.0, NEG).astype(F32)


def gate_rows(ga, gb, bits, i, d0, count):
    parts = []
    for j in range(count):
        d = d0 + j
        y = bits[0] ^ (d & 1)
        z1 = bits[1] ^ ((d >> 1) & 1)
        z2 = bits[2] ^ ((d >> 2) & 1)
        parts.append(ga[0, y, z1, z2, i])
        parts.append(gb[y, 0, z1, z2, i])
    return jnp.concatenate(parts, axis=0).astype(F32)


def att_fwd_kernel(bits, lens, qk, v, ga, gb, mixed, lse):
    length = qk.shape[1]
    heads = v.shape[2] // HEAD_DIM
    bias = key_bias(lens[pl.program_id(1)], length)
    count = length // (2 * ga.shape[-2])
    cols = [pl.ds(i * HEAD_DIM, HEAD_DIM) for i in range(2 * heads)]

    def score(i):
        return dot_nt(qk[0, :, cols[i]], qk[0, :, cols[heads + i]])

    ahead = score(0)
    outs = []
    stats = []
    for i in range(heads):
        s = ahead * (SCALE * LOG2E) + bias
        if i + 1 < heads:
            ahead = score(i + 1)
        top = jnp.max(s, axis=1, keepdims=True)
        e = jnp.exp2(s - top)
        total = jnp.sum(e, axis=1, keepdims=True)
        w = (e * gate_rows(ga, gb, bits, i, 0, count)).astype(BF16)
        outs.append(dot_nn(w, v[0, :, cols[i]]) * (1.0 / total))
        stats.append(top + jnp.log2(total))
    mixed[0] = jnp.concatenate(outs, axis=1).astype(BF16)
    lse[0] = jnp.concatenate(stats, axis=1)


def attention_forward(bits, lens, qk, v, ga, gb):
    _, rows, w2 = qk.shape
    w1 = v.shape[2]
    count = lens.shape[0]
    length = rows // count
    heads, sub, keys = ga.shape[-3:]
    sds = jax.ShapeDtypeStruct
    return pl.pallas_call(
        att_fwd_kernel,
        out_shape=(sds((2, rows, w1), BF16), sds((2, rows, heads), F32)),
        grid_spec=pltpu.PrefetchScalarGridSpec(
            num_scalar_prefetch=2, grid=(2, count),
            in_specs=[
                pl.BlockSpec((1, length, w2), lambda k, s, *_: (k, s, 0)),
                pl.BlockSpec((1, length, w1), lambda k, s, *_: (k, s, 0)),
                spec_a((heads, sub, keys), lambda k: k), spec_b((heads, sub, keys), lambda k: k),
            ],
            out_specs=[
                pl.BlockSpec((1, length, w1), lambda k, s, *_: (k, s, 0)),
                pl.BlockSpec((1, length, heads), lambda k, s, *_: (k, s, 0)),
            ],
        ),
        compiler_params=params(30, 2),
        cost_estimate=cost(16 * 2 * rows * length * w1, 16 * rows * w1),
    )(bits, lens, qk, v, ga, gb)


def att_bwd_kernel(last, bits, lens, qk, v, ga, gb, lse, dattn, wo, *rest):
    if last:
        ra, rb, dqk, dv, a_keep, a_send, b_keep, b_send, dm_s, dmt, qt, acc = rest
    else:
        dqk, dv, oga, ogb, dm_s, dmt, qt, acc = rest
    length = qk.shape[1]
    heads = v.shape[2] // HEAD_DIM
    hw = heads * HEAD_DIM
    k = pl.program_id(0)
    seq = pl.program_id(1)
    bias = key_bias(lens[seq], length)
    sub = ga.shape[-2]
    count = length // (2 * sub)
    cols = [pl.ds(i * HEAD_DIM, HEAD_DIM) for i in range(2 * heads)]

    dm = dot_nn(dattn[...], wo[0]).astype(BF16)
    dm_s[...] = dm
    dmt[...] = dm.T
    qt[...] = qk[0, :, pl.ds(0, hw)].T

    def products(i):
        return (
            dot_nt(qk[0, :, cols[i]], qk[0, :, cols[heads + i]]),
            dot_nt(dm_s[:, cols[i]], v[0, :, cols[i]]),
        )

    ahead = products(0)
    dqs, dks, dvs = [], [], []
    for i in range(heads):
        s, dw = ahead
        p = jnp.exp2(s * (SCALE * LOG2E) + bias - lse[0, :, pl.ds(i, 1)])
        if i + 1 < heads:
            ahead = products(i + 1)
        g = gate_rows(ga, gb, bits, i, 0, count)
        w = (p * g).astype(BF16)
        t = dw * p
        acc[i] = t + jnp.where(seq == 0, 0.0, acc[i])
        u = t * g
        ds = (u - p * jnp.sum(u, axis=1, keepdims=True)).astype(BF16)
        dqs.append(dot_nn(ds, qk[0, :, cols[heads + i]]) * SCALE)
        dvs.append(dot_nn(dmt[cols[i], :], w).astype(BF16).T)
        dks.append((dot_nn(qt[cols[i], :], ds) * SCALE).astype(BF16).T)
    dqk[0] = jnp.concatenate([d.astype(BF16) for d in dqs] + dks, axis=1)
    dv[0] = jnp.concatenate(dvs, axis=1)

    def first_rows(y, z1, z2):
        return pl.ds(pl.multiple_of(own(bits, y, z1, z2) * 2 * sub, sub), sub)

    def second_rows(y, z1, z2):
        return pl.ds(pl.multiple_of(own(bits, y, z1, z2) * 2 * sub + sub, sub), sub)

    @pl.when(seq == pl.num_programs(1) - 1)
    def _():
        if not last:
            for r in RELATIVE:
                for i in range(heads):
                    oga[(0,) + r + (i,)] = acc[i, first_rows(*r), :].astype(BF16)
                    ogb[(r[0], 0) + r[1:] + (i,)] = acc[i, second_rows(*r), :].astype(BF16)
            return

        def put_a(ref):
            for r in RELATIVE:
                for i in range(heads):
                    ref[r + (i,)] = (acc[i, first_rows(*r), :] + ra[(0,) + r + (i,)].astype(F32)).astype(BF16)

        @pl.when(k == 0)
        def _():
            put_a(a_keep)

        @pl.when(k == 1)
        def _():
            put_a(a_send)

        for r in RELATIVE:
            ref = b_send if r[0] else b_keep
            for i in range(heads):
                ref[(0,) + r[1:] + (i,)] = (
                    acc[i, second_rows(*r), :] + rb[(r[0], 0) + r[1:] + (i,)].astype(F32)
                ).astype(BF16)


def attention_backward(last, bits, lens, qk, v, ga, gb, lse, dattn, wo, got=()):
    _, rows, w2 = qk.shape
    w1 = v.shape[2]
    width = dattn.shape[1]
    count = lens.shape[0]
    length = rows // count
    tail = ga.shape[-3:]
    heads, sub, keys = tail
    sds = jax.ShapeDtypeStruct
    pick = lambda k: k
    in_specs = [
        pl.BlockSpec((1, length, w2), lambda k, s, *_: (k, s, 0)),
        pl.BlockSpec((1, length, w1), lambda k, s, *_: (k, s, 0)),
        spec_a(tail, pick), spec_b(tail, pick),
        pl.BlockSpec((1, length, heads), lambda k, s, *_: (k, s, 0)),
        pl.BlockSpec((length, width), lambda k, s, *_: (s, 0)),
        pl.BlockSpec((1, width, w1), lambda k, s, *_: (k, 0, 0)),
    ]
    out_shape = [sds((2, rows, w2), BF16), sds((2, rows, w1), BF16)]
    out_specs = [
        pl.BlockSpec((1, length, w2), lambda k, s, *_: (k, s, 0)),
        pl.BlockSpec((1, length, w1), lambda k, s, *_: (k, s, 0)),
    ]
    if last:
        in_specs += [spec_a(tail, pick), spec_b(tail, pick)]
        out_shape += [sds((2, 2, 2) + tail, BF16)] * 4
        out_specs += [whole((2, 2, 2) + tail)] * 2 + [
            pl.BlockSpec((1, 2, 2) + tail, lambda k, *_: (k, 0, 0, 0, 0, 0))
        ] * 2
    else:
        out_shape += [sds((2, 2, 2, 2) + tail, BF16)] * 2
        out_specs += [spec_a(tail, pick), spec_b(tail, pick)]
    return pl.pallas_call(
        functools.partial(att_bwd_kernel, last),
        out_shape=out_shape,
        grid_spec=pltpu.PrefetchScalarGridSpec(
            num_scalar_prefetch=2, grid=(2, count), in_specs=in_specs, out_specs=out_specs,
            scratch_shapes=[
                pltpu.VMEM((length, w1), BF16), pltpu.VMEM((w1, length), BF16),
                pltpu.VMEM((w1, length), BF16), pltpu.VMEM((heads, length, keys), F32),
            ],
        ),
        compiler_params=params(36, 2),
        cost_estimate=cost(40 * 2 * rows * length * w1, 30 * rows * w1),
    )(bits, lens, qk, v, ga, gb, lse, dattn, wo, *got)


def qkv_kernel(first, bits, x, wa, wb, qk, v, wqk, wv, wo, *rest):
    w1 = v.shape[2]
    wb_s = rest[-1]
    assemble(wqk.at[0], wa, bits, False)
    assemble(wb_s, wb, bits, True)

    if first:

        @pl.when(pl.program_id(0) == 0)
        def _():
            rest[0][...] = x[...].T

    wv[0] = wb_s[:, pl.ds(0, w1)]
    wo[0] = wb_s[:, pl.ds(w1, w1)]
    qk[0] = dot_nn(x[...], wqk[0]).astype(BF16)
    v[0] = dot_nn(x[...], wv[0]).astype(BF16)


def project(first, bits, x, wa, wb):
    rows, width = x.shape
    p, w2 = wa.shape[-2:]
    w1 = w2 // 2
    sds = jax.ShapeDtypeStruct
    pick = lambda k: k
    head = lambda s: pl.BlockSpec((1,) + s, lambda k, *_: (k, 0, 0))
    return pl.pallas_call(
        functools.partial(qkv_kernel, first),
        out_shape=[sds((2, rows, w2), BF16), sds((2, rows, w1), BF16), sds((2, width, w2), BF16),
                   sds((2, width, w1), BF16), sds((2, width, w1), BF16)]
        + ([sds((width, rows), BF16)] if first else []),
        grid_spec=pltpu.PrefetchScalarGridSpec(
            num_scalar_prefetch=1, grid=(2,),
            in_specs=[whole((rows, width)), spec_a((p, w2), pick), spec_b((p, w2), pick)],
            out_specs=[head((rows, w2)), head((rows, w1)), head((width, w2)), head((width, w1)), head((width, w1))]
            + ([whole((width, rows))] if first else []),
            scratch_shapes=[pltpu.VMEM((width, w2), BF16)],
        ),
        compiler_params=params(24),
        cost_estimate=cost(2 * rows * width * 2 * (w1 + w2), 8 * rows * width),
    )(bits, x, wa, wb)


def out_kernel(x, m0, m1, wo0, wo1, gain, bias, hid, unit, inverse, hidt):
    attn = dot_nt(m0[0], wo0[0]) + dot_nt(m0[1], wo0[1]) + dot_nt(m1[0], wo1[0]) + dot_nt(m1[1], wo1[1])
    u, inv = norm_stats(x[...].astype(F32) + attn)
    h = (u * gain[...] + bias[...]).astype(BF16)
    hid[...] = h
    hidt[...] = h.T
    unit[...] = u
    inverse[...] = inv


def out_forward(x, m0, m1, wo0, wo1, gain, bias, block=256):
    rows, width = x.shape
    w1 = wo0.shape[2]
    sds = jax.ShapeDtypeStruct
    row = lambda w: pl.BlockSpec((block, w), lambda r: (r, 0))
    mix = pl.BlockSpec((2, block, w1), lambda r: (0, r, 0))
    return pl.pallas_call(
        out_kernel,
        grid=(rows // block,),
        out_shape=(sds((rows, width), BF16), sds((rows, width), F32), sds((rows, 1), F32), sds((width, rows), BF16)),
        in_specs=[row(width), mix, mix, whole((2, width, w1)), whole((2, width, w1)), whole((1, width)), whole((1, width))],
        out_specs=[row(width), row(width), row(1), pl.BlockSpec((width, block), lambda r: (0, r))],
        compiler_params=params(20),
        cost_estimate=cost(2 * rows * width * 4 * w1, 12 * rows * width),
    )(x, m0, m1, wo0, wo1, gain, bias)


def qkv_grad_kernel(last, bits, xt, dat, dqk, dv, mixed, *rest):
    if last:
        ra, rb, a_keep, a_send, b_keep, b_send, ta, tb = rest
    else:
        ga, gb, ta, tb = rest
    w1 = dv.shape[2]
    k = pl.program_id(0)
    ta[...] = dot_nn(xt[...], dqk[0]).astype(ta.dtype)
    tb[:, pl.ds(0, w1)] = dot_nn(xt[...], dv[0]).astype(tb.dtype)
    tb[:, pl.ds(w1, w1)] = dot_nn(dat[...], mixed[0]).astype(tb.dtype)
    if not last:
        scatter(ga, ta, bits, False)
        scatter(gb, tb, bits, True)
        return
    p = ra.shape[-2]

    def rows(r):
        return pl.ds(pl.multiple_of(own(bits, *r) * p, 16), p)

    def put_a(ref):
        for r in RELATIVE:
            ref[r] = (ta[rows(r), :] + ra[(0,) + r].astype(F32)).astype(BF16)

    @pl.when(k == 0)
    def _():
        put_a(a_keep)

    @pl.when(k == 1)
    def _():
        put_a(a_send)

    for r in RELATIVE:
        ref = b_send if r[0] else b_keep
        ref[(0,) + r[1:]] = (tb[rows(r), :] + rb[(r[0], 0) + r[1:]].astype(F32)).astype(BF16)


def qkv_grads(last, bits, xt, dat, dqk, dv, mixed, got=()):
    width, rows = xt.shape
    w2 = dqk.shape[2]
    w1 = dv.shape[2]
    per = width // 8
    sds = jax.ShapeDtypeStruct
    pick = lambda k: k
    head = lambda w: pl.BlockSpec((1, rows, w), lambda k, *_: (k, 0, 0))
    in_specs = [whole((width, rows)), whole((width, rows)), head(w2), head(w1), head(w1)]
    if last:
        in_specs += [spec_a((per, w2), pick), spec_b((per, w2), pick)]
        out_shape = [sds((2, 2, 2, per, w2), BF16)] * 4
        out_specs = [whole((2, 2, 2, per, w2))] * 2 + [
            pl.BlockSpec((1, 2, 2, per, w2), lambda k, *_: (k, 0, 0, 0, 0))
        ] * 2
    else:
        out_shape = [sds((2, 2, 2, 2, per, w2), BF16)] * 2
        out_specs = [spec_a((per, w2), pick), spec_b((per, w2), pick)]
    kind = F32 if last else BF16
    return pl.pallas_call(
        functools.partial(qkv_grad_kernel, last),
        out_shape=out_shape,
        grid_spec=pltpu.PrefetchScalarGridSpec(
            num_scalar_prefetch=1, grid=(2,), in_specs=in_specs, out_specs=out_specs,
            scratch_shapes=[pltpu.VMEM((width, w2), kind), pltpu.VMEM((width, w2), kind)],
        ),
        compiler_params=params(26),
        cost_estimate=cost(2 * rows * width * 2 * 2 * w2, 8 * rows * width),
    )(bits, xt, dat, dqk, dv, mixed, *got)


def dinput_kernel(dfirst, dqk0, dqk1, dv0, dv1, wqk0, wqk1, wv0, wv1, out):
    total = dfirst[...]
    for a, b, wa, wb in ((dqk0, dv0, wqk0, wv0), (dqk1, dv1, wqk1, wv1)):
        for k in range(2):
            total = total + dot_nt(a[k], wa[k]) + dot_nt(b[k], wb[k])
    out[...] = total


def input_backward(dfirst, dqk0, dqk1, dv0, dv1, wqk0, wqk1, wv0, wv1, block=256):
    rows, width = dfirst.shape
    w2 = wqk0.shape[2]
    w1 = wv0.shape[2]
    row = pl.BlockSpec((block, width), lambda r: (r, 0))
    part = lambda w: pl.BlockSpec((2, block, w), lambda r: (0, r, 0))
    return pl.pallas_call(
        dinput_kernel,
        grid=(rows // block,),
        out_shape=jax.ShapeDtypeStruct((rows, width), F32),
        in_specs=[row, part(w2), part(w2), part(w1), part(w1)]
        + [whole((2, width, w2))] * 2 + [whole((2, width, w1))] * 2,
        out_specs=row,
        compiler_params=params(24),
        cost_estimate=cost(2 * rows * width * 4 * (w1 + w2), 14 * rows * width),
    )(dfirst, dqk0, dqk1, dv0, dv1, wqk0, wqk1, wv0, wv1)


GROUPS = 8


def partner_dp(value, bit):
    size = lax.axis_size("dp")
    step = (1 << bit) * (size // GROUPS)
    return lax.ppermute(value, "dp", [(i, i ^ step) for i in range(size)])


def partner_head(value, bit):
    size = lax.axis_size("head")
    return lax.ppermute(value, "head", [(i, i ^ (1 << bit)) for i in range(size)])


def over_y(value):
    return partner_dp(value, 0)


def over_near(value):
    return partner_dp(value, 1)


def over_far(value):
    return partner_dp(value, 2)


def over_pair(value):
    return partner_head(value, 0)


def over_x(value):
    return partner_head(value, 1)


def inner_groups():
    inner = lax.axis_size("dp") // GROUPS
    return inner, [[g * inner + i for i in range(inner)] for g in range(GROUPS)]


def inner_gather(value, axis):
    inner, groups = inner_groups()
    if inner == 1:
        return value
    return lax.all_gather(value, "dp", axis_index_groups=groups, axis=axis, tiled=True)


def inner_scatter(value, axis):
    inner, groups = inner_groups()
    if inner == 1:
        return value
    return lax.psum_scatter(value, "dp", axis_index_groups=groups, scatter_dimension=axis, tiled=True)


def after(values, *waits):
    return lax.optimization_barrier((tuple(values), waits))[0]


def wide(value):
    return value.astype(F32)


def first_sum(keep, got):
    return (wide(keep[1]) + wide(got[1])).astype(BF16)


def second_sum(keep, got, more):
    return (wide(keep[0, 1]) + wide(got[0, 1]) + wide(more[1])).astype(BF16)


def third_sum(keep, got, more, last):
    return wide(keep[0, 0]) + wide(got[0, 0]) + wide(more[0]) + wide(last)


def low_sum(keep, got):
    return (wide(keep[1]) + wide(got[1])).astype(BF16)


def high_sum(keep, got, more):
    return wide(keep[0]) + wide(got[0]) + wide(more)


def total_steps():
    steps = []
    for name in ("head", "dp"):
        size = lax.axis_size(name)
        step = 1
        while step < size:
            steps.append((name, [(i, i ^ step) for i in range(size)]))
            step *= 2
    return steps


def total_some(value, *steps):
    for name, pairs in steps:
        value = value + lax.ppermute(value, name, pairs)
    return value


def per_device(layer_input, output_grad, lengths, w_qkv, w_out, w_up, w_down,
               norm_gains, norm_biases, mask_logits, mask_noise):
    micro, seq, width = layer_input.shape
    rows = micro * seq
    x = layer_input.reshape(rows, width)
    dout = output_grad.reshape(rows, width)
    place = lax.axis_index("dp") // (lax.axis_size("dp") // GROUPS)
    bits = jnp.stack([place & 1, (place >> 1) & 1, (place >> 2) & 1]).astype(jnp.int32)
    lens = lax.dynamic_slice_in_dim(lengths, lax.axis_index("head"), 1, 1).reshape(micro)

    gate_part = jax.nn.sigmoid(mask_logits + mask_noise)
    gate_all = inner_gather(gate_part.astype(BF16), 1)
    sub = gate_all.shape[1] // 2
    gain1, gain2 = norm_gains[0:1], norm_gains[1:2]
    bias1, bias2 = norm_biases[0:1], norm_biases[1:2]

    ga = jnp.stack([
        inner_gather(jnp.concatenate([w_qkv[0], w_qkv[1]], axis=1), 0),
        inner_gather(jnp.concatenate([w_qkv[2], w_out.T], axis=1), 0),
    ])
    gb = jnp.stack([gate_all[:, :sub], gate_all[:, sub:]])
    up_all, down_all = inner_gather(w_up, 0), inner_gather(w_down.T, 0)
    units = up_all.shape[1]
    most = units * 2 // 3
    gc = jnp.stack([up_all[:, :most], down_all[:, :most]])
    ge = jnp.stack([up_all[:, most:], down_all[:, most:]])

    got = over_far(ga)
    ga = jnp.stack([ga, got], axis=1)
    got = over_near(ga)
    ga = jnp.stack([ga, got], axis=1)
    aa, ab = ga[0], ga[1]
    (gb,) = after((gb,), got)
    ra, rb = over_y(aa), over_x(ab)
    far_b = over_far(gb)
    aa, ab = jnp.stack([aa, ra]), jnp.stack([ab, rb])
    gb, = after((gb,), ra, rb)
    gb = jnp.stack([gb, far_b], axis=1)
    aa, ab = after((aa, ab), gb)
    ra, rb = over_x(aa), over_y(ab)
    near_b = over_near(gb)
    (gc,) = after((gc,), near_b)
    far_c = over_far(gc)
    gb = jnp.stack([gb, near_b], axis=1)
    ba, bb = gb[0], gb[1]
    aa, ab = jnp.stack([aa, ra]), jnp.stack([ab, rb])
    ba, bb = after((ba, bb), ra, rb)
    ca, cb = over_pair(aa), over_pair(ab)
    ra, rb = over_y(ba), over_x(bb)
    qk0, v0, wqk0, wv0, wo0, xt = project(True, bits, x, aa, ab)
    ba, bb = jnp.stack([ba, ra]), jnp.stack([bb, rb])
    ba, bb, gc, ca, cb = after((ba, bb, gc, ca, cb), qk0, ra, rb)
    ra, rb = over_x(ba), over_y(bb)
    gc = jnp.stack([gc, far_c], axis=1)
    near_c = over_near(gc)
    qk1, v1, wqk1, wv1, wo1 = project(False, bits, x, ca, cb)
    ba, bb = jnp.stack([ba, ra]), jnp.stack([bb, rb])
    gc = jnp.stack([gc, near_c], axis=1)
    fa, fb = gc[0], gc[1]
    fa, fb, ba, bb, ge = after((fa, fb, ba, bb, ge), ra, rb, near_c, qk1)
    ba1, bb1 = over_pair(ba), over_pair(bb)
    ra, rb = over_y(fa), over_x(fb)
    far_e = over_far(ge)
    m0, lse0 = attention_forward(bits, lens, qk0, v0, ba, bb)
    fa, fb = jnp.stack([fa, ra]), jnp.stack([fb, rb])
    ge = jnp.stack([ge, far_e], axis=1)
    fa, fb, ge, ba1, bb1 = after((fa, fb, ge, ba1, bb1), m0)
    ra, rb = over_x(fa), over_y(fb)
    near_e = over_near(ge)
    ge = jnp.stack([ge, near_e], axis=1)
    m1, lse1 = attention_forward(bits, lens, qk1, v1, ba1, bb1)
    hid, unit, inverse, hidt = out_forward(x, m0, m1, wo0, wo1, gain1, bias1)
    fa, fb = jnp.stack([fa, ra]), jnp.stack([fb, rb])
    ea, eb = ge[0], ge[1]
    fa, fb, ea, eb = after((fa, fb, ea, eb), hid, ra, rb)
    fa1, fb1 = over_pair(fa), over_pair(fb)
    ra, rb = over_y(ea), over_x(eb)
    ea, eb = jnp.stack([ea, ra]), jnp.stack([eb, rb])
    ea, eb, hid = after((ea, eb, hid), fa1, fb1)
    ra, rb = over_x(ea), over_y(eb)
    actp, gpp, part = ffn_part(bits, hid, fa, fa1, fb, fb1)
    ea, eb = jnp.stack([ea, ra]), jnp.stack([eb, rb])
    ea, eb = after((ea, eb), part)
    ea1, eb1 = over_pair(ea), over_pair(eb)
    actq, gpq, out, dsec, dffn, dffnt, dgain2, dbias2 = ffn_rest(
        bits, lens, hid, ea, ea1, eb, eb1, part, gain2, bias2, dout
    )

    steps = total_steps()
    down0, down1 = down_grads(bits, dffnt, actp, actq)
    cd = over_pair(down1)
    dffn, = after((dffn,), down1)
    up1, part = ffn_backward(False, bits, hidt, dffn, fa1, ea1, fb1, eb1, gpp, gpq)
    down0, cd, up1, dffn = after((down0, cd, up1, dffn), part)
    xd = over_y(first_sum(down0, cd))
    cu = over_pair(up1)
    up0, dfirst, dattn, dattnt, dgain1, dbias1 = ffn_backward(
        True, bits, hidt, dffn, fa, ea, fb, eb, gpp, gpq, (dsec, part, unit, inverse, gain1)
    )
    up0, cu, norms, dattn = after((up0, cu, jnp.concatenate([dgain1, dgain2, dbias1, dbias2]), dattn), up0)
    xu = over_x(first_sum(up0, cu))
    norms = total_some(norms, steps[0])
    dqk1, dv1, ga1, gb1 = attention_backward(False, bits, lens, qk1, v1, ba1, bb1, lse1, dattn, wo1)
    ga1, gb1, norms, dqk1, xd = after((ga1, gb1, norms, dqk1, xd), dv1)
    cga, cgb = over_pair(ga1), over_pair(gb1)
    norms = total_some(norms, steps[3])
    qka1, vo1 = qkv_grads(False, bits, xt, dattnt, dqk1, dv1, m1)
    qka1, vo1, dattn, norms, cga, cgb, xu, xd = after((qka1, vo1, dattn, norms, cga, cgb, xu, xd), vo1)
    cqk, cvo = over_pair(qka1), over_pair(vo1)
    norms, = after((norms,), xu, xd)
    norms = total_some(norms, steps[1])
    send_d, send_u = second_sum(down0, cd, xd), second_sum(up0, cu, xu)
    send_d, send_u, norms = after((send_d, send_u, norms), norms)
    yd, yu = over_x(send_d), over_y(send_u)
    norms = total_some(norms, steps[4])
    dqk0, dv0, ga0, ga_out, gb0, gb_out = attention_backward(
        True, bits, lens, qk0, v0, ba, bb, lse0, dattn, wo0, (cga, cgb)
    )
    ga_out, gb_out, dqk0, norms, cqk, cvo, yd, yu = after((ga_out, gb_out, dqk0, norms, cqk, cvo, yd, yu), dv0)
    xga = over_x(ga_out)
    norms = total_some(norms, *steps[2:3], *steps[5:])
    u, d = third_sum(up0, cu, xu, yu), third_sum(down0, cd, xd, yd)
    send_f = jnp.stack([u[1], d[1]]).astype(BF16)
    send_f, gb_out, norms = after((send_f, gb_out, norms), norms)
    xgb = over_y(gb_out)
    near_f = over_near(send_f)
    qka0, qka_out, vo0, vo_out = qkv_grads(True, bits, xt, dattnt, dqk0, dv0, m0, (cqk, cvo))
    xqk, xvo = over_x(qka_out), over_y(vo_out)
    near_f, xga, xgb, dqk0 = after((near_f, xga, xgb, dqk0), vo0)
    yga, ygb = over_y(low_sum(ga0, xga)), over_x(low_sum(gb0, xgb))
    far_f = over_far(jnp.stack([u[0, 1] + wide(near_f[0, 1]), d[0, 1] + wide(near_f[1, 1])]).astype(BF16))
    dinput = input_backward(dfirst, dqk0, dqk1, dv0, dv1, wqk0, wqk1, wv0, wv1)
    xqk, xvo, yga, ygb, far_f = after((xqk, xvo, yga, ygb, far_f), dinput)
    send_qk, send_vo = low_sum(qka0, xqk), low_sum(vo0, xvo)
    g1, g2 = high_sum(ga0, xga, yga), high_sum(gb0, xgb, ygb)
    send_g = jnp.stack([g1[1], g2[1]]).astype(BF16)
    yqk, yvo = over_y(send_qk), over_x(send_vo)
    near_g = over_near(send_g)
    w1, w2 = high_sum(qka0, xqk, yqk), high_sum(vo0, xvo, yvo)
    send_w = jnp.stack([w1[1], w2[1]]).astype(BF16)
    send_g = jnp.stack([g1[0, 1] + wide(near_g[0, 1]), g2[0, 1] + wide(near_g[1, 1])]).astype(BF16)
    near_w = over_near(send_w)
    far_g = over_far(send_g)
    far_w = over_far(jnp.stack([w1[0, 1] + wide(near_w[0, 1]), w2[0, 1] + wide(near_w[1, 1])]).astype(BF16))

    up_grad = u[0, 0] + wide(near_f[0, 0]) + wide(far_f[0])
    down_grad = d[0, 0] + wide(near_f[1, 0]) + wide(far_f[1])
    gate_a = g1[0, 0] + wide(near_g[0, 0]) + wide(far_g[0])
    gate_b = g2[0, 0] + wide(near_g[1, 0]) + wide(far_g[1])
    qk_grad = w1[0, 0] + wide(near_w[0, 0]) + wide(far_w[0])
    vo_grad = w2[0, 0] + wide(near_w[1, 0]) + wide(far_w[1])

    qk_grad, vo_grad = inner_scatter(qk_grad, 0), inner_scatter(vo_grad, 0)
    local = vo_grad.shape[1] // 2
    gate_grad = inner_scatter(jnp.concatenate([gate_a, gate_b], axis=1), 1)
    return (
        out.reshape(micro, seq, width),
        dinput.reshape(micro, seq, width),
        jnp.stack([qk_grad[:, :local], qk_grad[:, local:], vo_grad[:, :local]]),
        vo_grad[:, local:].T,
        inner_scatter(up_grad, 0),
        inner_scatter(down_grad, 0).T,
        norms[:2],
        norms[2:],
        gate_grad * gate_part * (1.0 - gate_part),
    )


def solution(mesh):
    rows = P(None, ("dp", "head"), None)
    gates = P("head", "dp", None)
    weights = (P(None, "dp", "head"), P("head", "dp"), P("dp", "head"), P("head", "dp"))
    return jax.shard_map(
        per_device,
        mesh=mesh,
        in_specs=(rows, rows, P(None, "dp")) + weights + (P(), P(), gates, gates),
        out_specs=(rows, rows) + weights + (P(), P(), gates),
        check_vma=False,
    )
```

```python
import functools, math
import jax, jax.numpy as jnp
from jax import lax
from jax.experimental import pallas as pl
from jax.experimental.pallas import tpu as pltpu
from jax.sharding import PartitionSpec as P

HEAD_DIM = 64
EPS = 1e-05
F32 = jnp.float32
BF16 = jnp.bfloat16
GP = jnp.bfloat16
SCALE = 1.0 / math.sqrt(HEAD_DIM)
LOG2E = math.log2(math.e)
NEG = -1e30
INV_SQRT2 = 1.0 / math.sqrt(2.0)
INV_SQRT2PI = 1.0 / math.sqrt(2.0 * math.pi)


def dot_nn(a, b):
    return lax.dot_general(a, b, (((1,), (0,)), ((), ())), preferred_element_type=F32)


def dot_nt(a, b):
    return lax.dot_general(a, b, (((1,), (1,)), ((), ())), preferred_element_type=F32)


def dot_tn(a, b):
    return lax.dot_general(a, b, (((0,), (0,)), ((), ())), preferred_element_type=F32)


def piece(ref, bits, d, flip):
    y = bits[0] ^ (d & 1)
    z1 = bits[1] ^ ((d >> 1) & 1)
    z2 = bits[2] ^ ((d >> 2) & 1)
    if flip:
        return ref.at[y, 0, z1, z2]
    return ref.at[0, y, z1, z2]


def assemble(dst, ref, bits, flip, cols=None):
    rows = ref.shape[-2]
    cols = pl.ds(0, ref.shape[-1]) if cols is None else cols
    for d in range(8):
        dst[pl.ds(d * rows, rows), cols] = piece(ref, bits, d, flip)[...]


def scatter(ref, src, bits, flip):
    rows = ref.shape[-2]
    for d in range(8):
        piece(ref, bits, d, flip)[...] = src[pl.ds(d * rows, rows), :]


def own(bits, y, z1, z2):
    return (bits[0] ^ y) + 2 * (bits[1] ^ z1) + 4 * (bits[2] ^ z2)


RELATIVE = [(y, z1, z2) for y in range(2) for z1 in range(2) for z2 in range(2)]


def spec_a(tail, pick):
    zeros = (0,) * len(tail)
    return pl.BlockSpec((1, 2, 2, 2) + tail, lambda k, *_: (pick(k), 0, 0, 0) + zeros)


def spec_b(tail, pick):
    zeros = (0,) * len(tail)
    return pl.BlockSpec((2, 1, 2, 2) + tail, lambda k, *_: (0, pick(k), 0, 0) + zeros)


def whole(shape):
    zeros = (0,) * len(shape)
    return pl.BlockSpec(shape, lambda *_: zeros, pipeline_mode=pl.Buffered(1))


def low_pick(k):
    return jnp.minimum(k, 1)


def high_pick(k):
    return jnp.maximum(k - 2, 0)


def norm_stats(z):
    mean = jnp.mean(z, axis=1, keepdims=True)
    centered = z - mean
    inverse = lax.rsqrt(jnp.mean(centered * centered, axis=1, keepdims=True) + EPS)
    return centered * inverse, inverse


def norm_back(du, unit, inverse):
    return inverse * (
        du
        - jnp.mean(du, axis=1, keepdims=True)
        - unit * jnp.mean(du * unit, axis=1, keepdims=True)
    )


def gelu_pair(up):
    cdf = 0.5 + 0.5 * lax.erf(up * INV_SQRT2)
    pdf = INV_SQRT2PI * jnp.exp(-0.5 * (up * up))
    return up * cdf, cdf + up * pdf


SHARE = 10


def cost(flops, moved):
    return pl.CostEstimate(flops=flops * SHARE, bytes_accessed=moved * SHARE, transcendentals=0)


def params(mib=60, n=1):
    return pltpu.CompilerParams(
        dimension_semantics=("arbitrary",) * n, vmem_limit_bytes=mib * 1024 * 1024
    )


def load_pair(k, bits, wu, wd, ua0, ua1, db0, db1):
    @pl.when(k < 2)
    def _():
        assemble(wu, ua0, bits, False)
        assemble(wd, db0, bits, True)

    @pl.when(k >= 2)
    def _():
        assemble(wu, ua1, bits, False)
        assemble(wd, db1, bits, True)


def ffn_units(chunk, hid, wu, wd, act_o, gp_o, acc, finish=None):
    rows = hid.shape[0]
    ats = [pl.ds(r * chunk, chunk) for r in range(rows // chunk)]
    ahead = dot_nn(hid[ats[0], :], wu[...])
    for r, at in enumerate(ats):
        act, gp = gelu_pair(ahead)
        if r + 1 < len(ats):
            ahead = dot_nn(hid[ats[r + 1], :], wu[...])
        act = act.astype(BF16)
        act_o[0, at, :] = act
        gp_o[0, at, :] = gp.astype(gp_o.dtype)
        acc[at, :] += dot_nt(act, wd[...])
        if finish is not None:
            finish(r * chunk, chunk)


def ffn_part_kernel(chunk, bits, hid, ua0, ua1, db0, db1, act_o, gp_o, acc, wu, wd):
    k = pl.program_id(0)
    load_pair(k, bits, wu, wd, ua0, ua1, db0, db1)

    @pl.when(k == 0)
    def _():
        acc[...] = hid[...].astype(F32)

    ffn_units(chunk, hid, wu, wd, act_o, gp_o, acc)


def ffn_part(bits, hid, ua0, ua1, db0, db1, chunk=512):
    rows, width = hid.shape
    p, n = ua0.shape[-2:]
    sds = jax.ShapeDtypeStruct
    col = pl.BlockSpec((1, rows, n), lambda k, *_: (k, 0, 0))
    return pl.pallas_call(
        functools.partial(ffn_part_kernel, chunk),
        out_shape=(pltpu.HBM((4, rows, n), BF16), pltpu.HBM((4, rows, n), GP), sds((rows, width), F32)),
        grid_spec=pltpu.PrefetchScalarGridSpec(
            num_scalar_prefetch=1, grid=(4,),
            in_specs=[whole((rows, width)), spec_a((p, n), low_pick), spec_a((p, n), high_pick),
                      spec_b((p, n), low_pick), spec_b((p, n), high_pick)],
            out_specs=[col, col, whole((rows, width))],
            scratch_shapes=[pltpu.VMEM((width, n), BF16), pltpu.VMEM((width, n), BF16)],
        ),
        compiler_params=params(26),
        cost_estimate=cost(4 * rows * width * 4 * n, 16 * rows * width),
    )(bits, hid, ua0, ua1, db0, db1)


def ffn_rest_kernel(chunk, bits, lens, hid, ua0, ua1, db0, db1, part, gain, bias, dout,
                    act_o, gp_o, out, acc, dffn, dffnt, dgain, dbias, wu, wd):
    k = pl.program_id(0)
    rows = hid.shape[0]
    load_pair(k, bits, wu, wd, ua0, ua1, db0, db1)

    @pl.when(k == 0)
    def _():
        acc[...] = part[...]

    @pl.when(k < 3)
    def _():
        ffn_units(chunk, hid, wu, wd, act_o, gp_o, acc)

    @pl.when(k == 3)
    def _():
        length = rows // lens.shape[0]
        small = 256
        g = gain[...]
        b = bias[...]
        sums = [jnp.zeros_like(g), jnp.zeros_like(g)]

        def finish(start, count):
            for at0 in range(start, start + count, small):
                at = pl.ds(at0, small)
                size = lens[at0 // length]
                pos = (at0 % length) + lax.broadcasted_iota(jnp.int32, (small, 1), 0)
                valid = pos < size
                unit, inverse = norm_stats(acc[at, :])
                out[at, :] = jnp.where(valid, unit * g + b, 0.0).astype(BF16)
                dy = jnp.where(valid, dout[at, :].astype(F32), 0.0)
                sums[0] = sums[0] + jnp.sum(dy * unit, axis=0, keepdims=True)
                sums[1] = sums[1] + jnp.sum(dy, axis=0, keepdims=True)
                dz = norm_back(dy * g, unit, inverse)
                acc[at, :] = dz
                low = dz.astype(BF16)
                dffn[at, :] = low
                dffnt[:, at] = low.T

        ffn_units(chunk, hid, wu, wd, act_o, gp_o, acc, finish)
        dgain[...] = sums[0]
        dbias[...] = sums[1]


def ffn_rest(bits, lens, hid, ua0, ua1, db0, db1, part, gain, bias, dout, chunk=512):
    rows, width = hid.shape
    p, n = ua0.shape[-2:]
    sds = jax.ShapeDtypeStruct
    full = whole((rows, width))
    line = whole((1, width))
    col = pl.BlockSpec((1, rows, n), lambda k, *_: (k, 0, 0))
    return pl.pallas_call(
        functools.partial(ffn_rest_kernel, chunk),
        out_shape=(sds((4, rows, n), BF16), sds((4, rows, n), GP), sds((rows, width), BF16), sds((rows, width), F32),
                   sds((rows, width), BF16), sds((width, rows), BF16), sds((1, width), F32), sds((1, width), F32)),
        grid_spec=pltpu.PrefetchScalarGridSpec(
            num_scalar_prefetch=2, grid=(4,),
            in_specs=[full, spec_a((p, n), low_pick), spec_a((p, n), high_pick),
                      spec_b((p, n), low_pick), spec_b((p, n), high_pick), full, line, line, full],
            out_specs=[col, col, full, full, full, whole((width, rows)), line, line],
            scratch_shapes=[pltpu.VMEM((width, n), BF16), pltpu.VMEM((width, n), BF16)],
        ),
        compiler_params=params(30),
        cost_estimate=cost(4 * rows * width * 4 * n, 20 * rows * width),
    )(bits, lens, hid, ua0, ua1, db0, db1, part, gain, bias, dout)


def down_grad_kernel(bits, dt, actp, actq, keep, send):
    k = pl.program_id(0)
    first = dot_nn(dt[...], actp[0]).astype(BF16)
    second = dot_nn(dt[...], actq[0]).astype(BF16)
    rows = keep.shape[-2]
    n = actp.shape[2]

    def put(ref):
        for d in range(8):
            at = piece(ref, bits, d, True)
            at[:, pl.ds(0, n)] = first[d * rows : (d + 1) * rows]
            at[:, pl.ds(n, actq.shape[2])] = second[d * rows : (d + 1) * rows]

    @pl.when(k < 2)
    def _():
        put(keep)

    @pl.when(k >= 2)
    def _():
        put(send)


def down_grads(bits, dt, actp, actq):
    width, rows = dt.shape
    col = lambda a: pl.BlockSpec((1, rows, a.shape[2]), lambda k, *_: (k, 0, 0))
    n = actp.shape[2] + actq.shape[2]
    p = width // 8
    sds = jax.ShapeDtypeStruct
    return pl.pallas_call(
        down_grad_kernel,
        out_shape=(sds((2, 2, 2, 2, p, n), BF16), sds((2, 2, 2, 2, p, n), BF16)),
        grid_spec=pltpu.PrefetchScalarGridSpec(
            num_scalar_prefetch=1, grid=(4,),
            in_specs=[whole((width, rows)), col(actp), col(actq)],
            out_specs=[spec_b((p, n), low_pick), spec_b((p, n), high_pick)],
        ),
        compiler_params=params(22),
        cost_estimate=cost(2 * rows * width * 4 * n, 14 * rows * width),
    )(bits, dt, actp, actq)


def ffn_bwd_kernel(chunk, last, bits, ht, dffn, uap, uaq, dbp, dbq, gpp, gpq, *rest):
    if last:
        dsec, part, unit, inverse, gain, gu, acc, dattn, dattnt, dgain, dbias, wu, wd, dup_s = rest
    else:
        gu, acc, wu, wd, dup_s = rest
    k = pl.program_id(0)
    rows, width = dffn.shape
    np = uap.shape[-1]
    left, right = pl.ds(0, np), pl.ds(np, uaq.shape[-1])

    assemble(wu, uap, bits, False, left)
    assemble(wu, uaq, bits, False, right)
    assemble(wd, dbp, bits, True, left)
    assemble(wd, dbq, bits, True, right)

    @pl.when(k == 0)
    def _():
        if last:
            acc[...] = part[...] + dsec[...]
        else:
            acc[...] = jnp.zeros_like(acc)

    def run(finish=None):
        ats = [pl.ds(r * chunk, chunk) for r in range(rows // chunk)]
        ahead = dot_nn(dffn[ats[0], :], wd[...])
        for r, at in enumerate(ats):
            dup_s[at, left] = (ahead[:, :np] * gpp[0, at, :].astype(F32)).astype(BF16)
            dup_s[at, right] = (ahead[:, np:] * gpq[0, at, :].astype(F32)).astype(BF16)
            if r + 1 < len(ats):
                ahead = dot_nn(dffn[ats[r + 1], :], wd[...])
            acc[at, :] += dot_nt(dup_s[at, :], wu[...])
            if finish is not None:
                finish(r * chunk, chunk)
        grad = dot_nn(ht[...], dup_s[...]).astype(BF16)
        p = gu.shape[-2]
        for d in range(8):
            piece(gu, bits, d, False)[...] = grad[d * p : (d + 1) * p]

    if not last:
        run()
        return

    @pl.when(k == 0)
    def _():
        run()

    @pl.when(k == 1)
    def _():
        small = 256
        g = gain[...]
        sums = [jnp.zeros_like(g), jnp.zeros_like(g)]

        def finish(start, count):
            for at0 in range(start, start + count, small):
                at = pl.ds(at0, small)
                dh = acc[at, :]
                u = unit[at, :]
                sums[0] = sums[0] + jnp.sum(dh * u, axis=0, keepdims=True)
                sums[1] = sums[1] + jnp.sum(dh, axis=0, keepdims=True)
                dz = norm_back(dh * g, u, inverse[at, :])
                acc[at, :] = dz
                low = dz.astype(BF16)
                dattn[at, :] = low
                dattnt[:, at] = low.T

        run(finish)
        dgain[...] = sums[0]
        dbias[...] = sums[1]


def ffn_backward(last, bits, ht, dffn, uap, uaq, dbp, dbq, gpp, gpq, extra=(), chunk=512):
    rows, width = dffn.shape
    p, np = uap.shape[-2:]
    nq = uaq.shape[-1]
    n = np + nq
    sds = jax.ShapeDtypeStruct
    off = 0 if last else 2
    pick = lambda k: k
    full = whole((rows, width))
    line = whole((1, width))
    out_shape = [sds((2, 2, 2, 2, p, n), BF16)]
    out_specs = [spec_a((p, n), pick)]
    in_specs = [
        whole((width, rows)), full,
        spec_a((p, np), pick), spec_a((p, nq), pick), spec_b((p, np), pick), spec_b((p, nq), pick),
        pl.BlockSpec((1, rows, np), lambda k, *_: (k + off, 0, 0)),
        pl.BlockSpec((1, rows, nq), lambda k, *_: (k + off, 0, 0)),
    ]
    scratch = [pltpu.VMEM((width, n), BF16), pltpu.VMEM((width, n), BF16), pltpu.VMEM((rows, n), BF16)]
    if last:
        in_specs += [full] * 3 + [whole((rows, 1)), line]
        out_shape += [sds((rows, width), F32), sds((rows, width), BF16), sds((width, rows), BF16), sds((1, width), F32), sds((1, width), F32)]
        out_specs += [full, full, whole((width, rows)), line, line]
    else:
        out_shape += [sds((rows, width), F32)]
        out_specs += [full]
    return pl.pallas_call(
        functools.partial(ffn_bwd_kernel, chunk, last),
        out_shape=out_shape,
        grid_spec=pltpu.PrefetchScalarGridSpec(
            num_scalar_prefetch=1, grid=(2,), in_specs=in_specs, out_specs=out_specs, scratch_shapes=scratch,
        ),
        compiler_params=params(36),
        cost_estimate=cost(6 * rows * width * 2 * n, 30 * rows * width),
    )(bits, ht, dffn, uap, uaq, dbp, dbq, gpp, gpq, *extra)


def key_bias(size, length):
    pos = lax.broadcasted_iota(jnp.int32, (1, length), 1)
    return jnp.where(pos < size, 0.0, NEG).astype(F32)


def gate_rows(ga, gb, bits, i, d0, count):
    parts = []
    for j in range(count):
        d = d0 + j
        y = bits[0] ^ (d & 1)
        z1 = bits[1] ^ ((d >> 1) & 1)
        z2 = bits[2] ^ ((d >> 2) & 1)
        parts.append(ga[0, y, z1, z2, i])
        parts.append(gb[y, 0, z1, z2, i])
    return jnp.concatenate(parts, axis=0).astype(F32)


def att_fwd_kernel(bits, lens, qk, v, ga, gb, mixed, lse):
    length = qk.shape[1]
    heads = v.shape[2] // HEAD_DIM
    bias = key_bias(lens[pl.program_id(1)], length)
    count = length // (2 * ga.shape[-2])
    cols = [pl.ds(i * HEAD_DIM, HEAD_DIM) for i in range(2 * heads)]

    def score(i):
        return dot_nt(qk[0, :, cols[i]], qk[0, :, cols[heads + i]])

    ahead = score(0)
    outs = []
    stats = []
    for i in range(heads):
        s = ahead * (SCALE * LOG2E) + bias
        if i + 1 < heads:
            ahead = score(i + 1)
        top = jnp.max(s, axis=1, keepdims=True)
        e = jnp.exp2(s - top)
        total = jnp.sum(e, axis=1, keepdims=True)
        w = (e * gate_rows(ga, gb, bits, i, 0, count)).astype(BF16)
        outs.append(dot_nn(w, v[0, :, cols[i]]) * (1.0 / total))
        stats.append(top + jnp.log2(total))
    mixed[0] = jnp.concatenate(outs, axis=1).astype(BF16)
    lse[0] = jnp.concatenate(stats, axis=1)


def attention_forward(bits, lens, qk, v, ga, gb):
    _, rows, w2 = qk.shape
    w1 = v.shape[2]
    count = lens.shape[0]
    length = rows // count
    heads, sub, keys = ga.shape[-3:]
    sds = jax.ShapeDtypeStruct
    return pl.pallas_call(
        att_fwd_kernel,
        out_shape=(sds((2, rows, w1), BF16), sds((2, rows, heads), F32)),
        grid_spec=pltpu.PrefetchScalarGridSpec(
            num_scalar_prefetch=2, grid=(2, count),
            in_specs=[
                pl.BlockSpec((1, length, w2), lambda k, s, *_: (k, s, 0)),
                pl.BlockSpec((1, length, w1), lambda k, s, *_: (k, s, 0)),
                spec_a((heads, sub, keys), lambda k: k), spec_b((heads, sub, keys), lambda k: k),
            ],
            out_specs=[
                pl.BlockSpec((1, length, w1), lambda k, s, *_: (k, s, 0)),
                pl.BlockSpec((1, length, heads), lambda k, s, *_: (k, s, 0)),
            ],
        ),
        compiler_params=params(30, 2),
        cost_estimate=cost(16 * 2 * rows * length * w1, 16 * rows * w1),
    )(bits, lens, qk, v, ga, gb)


def att_bwd_kernel(last, bits, lens, qk, v, ga, gb, lse, dattn, wo, *rest):
    if last:
        ra, rb, dqk, dv, a_keep, a_send, b_keep, b_send, dm_s, dmt, qt, acc = rest
    else:
        dqk, dv, oga, ogb, dm_s, dmt, qt, acc = rest
    length = qk.shape[1]
    heads = v.shape[2] // HEAD_DIM
    hw = heads * HEAD_DIM
    k = pl.program_id(0)
    seq = pl.program_id(1)
    bias = key_bias(lens[seq], length)
    sub = ga.shape[-2]
    count = length // (2 * sub)
    cols = [pl.ds(i * HEAD_DIM, HEAD_DIM) for i in range(2 * heads)]

    dm = dot_nn(dattn[...], wo[0]).astype(BF16)
    dm_s[...] = dm
    dmt[...] = dm.T
    qt[...] = qk[0, :, pl.ds(0, hw)].T

    def products(i):
        return (
            dot_nt(qk[0, :, cols[i]], qk[0, :, cols[heads + i]]),
            dot_nt(dm_s[:, cols[i]], v[0, :, cols[i]]),
        )

    ahead = products(0)
    dqs, dks, dvs = [], [], []
    for i in range(heads):
        s, dw = ahead
        p = jnp.exp2(s * (SCALE * LOG2E) + bias - lse[0, :, pl.ds(i, 1)])
        if i + 1 < heads:
            ahead = products(i + 1)
        g = gate_rows(ga, gb, bits, i, 0, count)
        w = (p * g).astype(BF16)
        t = dw * p
        acc[i] = t + jnp.where(seq == 0, 0.0, acc[i])
        u = t * g
        ds = (u - p * jnp.sum(u, axis=1, keepdims=True)).astype(BF16)
        dqs.append(dot_nn(ds, qk[0, :, cols[heads + i]]) * SCALE)
        dvs.append(dot_nn(dmt[cols[i], :], w).astype(BF16).T)
        dks.append((dot_nn(qt[cols[i], :], ds) * SCALE).astype(BF16).T)
    dqk[0] = jnp.concatenate([d.astype(BF16) for d in dqs] + dks, axis=1)
    dv[0] = jnp.concatenate(dvs, axis=1)

    def first_rows(y, z1, z2):
        return pl.ds(pl.multiple_of(own(bits, y, z1, z2) * 2 * sub, sub), sub)

    def second_rows(y, z1, z2):
        return pl.ds(pl.multiple_of(own(bits, y, z1, z2) * 2 * sub + sub, sub), sub)

    @pl.when(seq == pl.num_programs(1) - 1)
    def _():
        if not last:
            for r in RELATIVE:
                for i in range(heads):
                    oga[(0,) + r + (i,)] = acc[i, first_rows(*r), :].astype(BF16)
                    ogb[(r[0], 0) + r[1:] + (i,)] = acc[i, second_rows(*r), :].astype(BF16)
            return

        def put_a(ref):
            for r in RELATIVE:
                for i in range(heads):
                    ref[r + (i,)] = (acc[i, first_rows(*r), :] + ra[(0,) + r + (i,)].astype(F32)).astype(BF16)

        @pl.when(k == 0)
        def _():
            put_a(a_keep)

        @pl.when(k == 1)
        def _():
            put_a(a_send)

        for r in RELATIVE:
            ref = b_send if r[0] else b_keep
            for i in range(heads):
                ref[(0,) + r[1:] + (i,)] = (
                    acc[i, second_rows(*r), :] + rb[(r[0], 0) + r[1:] + (i,)].astype(F32)
                ).astype(BF16)


def attention_backward(last, bits, lens, qk, v, ga, gb, lse, dattn, wo, got=()):
    _, rows, w2 = qk.shape
    w1 = v.shape[2]
    width = dattn.shape[1]
    count = lens.shape[0]
    length = rows // count
    tail = ga.shape[-3:]
    heads, sub, keys = tail
    sds = jax.ShapeDtypeStruct
    pick = lambda k: k
    in_specs = [
        pl.BlockSpec((1, length, w2), lambda k, s, *_: (k, s, 0)),
        pl.BlockSpec((1, length, w1), lambda k, s, *_: (k, s, 0)),
        spec_a(tail, pick), spec_b(tail, pick),
        pl.BlockSpec((1, length, heads), lambda k, s, *_: (k, s, 0)),
        pl.BlockSpec((length, width), lambda k, s, *_: (s, 0)),
        pl.BlockSpec((1, width, w1), lambda k, s, *_: (k, 0, 0)),
    ]
    out_shape = [sds((2, rows, w2), BF16), sds((2, rows, w1), BF16)]
    out_specs = [
        pl.BlockSpec((1, length, w2), lambda k, s, *_: (k, s, 0)),
        pl.BlockSpec((1, length, w1), lambda k, s, *_: (k, s, 0)),
    ]
    if last:
        in_specs += [spec_a(tail, pick), spec_b(tail, pick)]
        out_shape += [sds((2, 2, 2) + tail, BF16)] * 4
        out_specs += [whole((2, 2, 2) + tail)] * 2 + [
            pl.BlockSpec((1, 2, 2) + tail, lambda k, *_: (k, 0, 0, 0, 0, 0))
        ] * 2
    else:
        out_shape += [sds((2, 2, 2, 2) + tail, BF16)] * 2
        out_specs += [spec_a(tail, pick), spec_b(tail, pick)]
    return pl.pallas_call(
        functools.partial(att_bwd_kernel, last),
        out_shape=out_shape,
        grid_spec=pltpu.PrefetchScalarGridSpec(
            num_scalar_prefetch=2, grid=(2, count), in_specs=in_specs, out_specs=out_specs,
            scratch_shapes=[
                pltpu.VMEM((length, w1), BF16), pltpu.VMEM((w1, length), BF16),
                pltpu.VMEM((w1, length), BF16), pltpu.VMEM((heads, length, keys), F32),
            ],
        ),
        compiler_params=params(36, 2),
        cost_estimate=cost(40 * 2 * rows * length * w1, 30 * rows * w1),
    )(bits, lens, qk, v, ga, gb, lse, dattn, wo, *got)


def qkv_kernel(first, bits, x, wa, wb, qk, v, wqk, wv, wo, *rest):
    w1 = v.shape[2]
    wb_s = rest[-1]
    assemble(wqk.at[0], wa, bits, False)
    assemble(wb_s, wb, bits, True)

    if first:

        @pl.when(pl.program_id(0) == 0)
        def _():
            rest[0][...] = x[...].T

    wv[0] = wb_s[:, pl.ds(0, w1)]
    wo[0] = wb_s[:, pl.ds(w1, w1)]
    qk[0] = dot_nn(x[...], wqk[0]).astype(BF16)
    v[0] = dot_nn(x[...], wv[0]).astype(BF16)


def project(first, bits, x, wa, wb):
    rows, width = x.shape
    p, w2 = wa.shape[-2:]
    w1 = w2 // 2
    sds = jax.ShapeDtypeStruct
    pick = lambda k: k
    head = lambda s: pl.BlockSpec((1,) + s, lambda k, *_: (k, 0, 0))
    return pl.pallas_call(
        functools.partial(qkv_kernel, first),
        out_shape=[sds((2, rows, w2), BF16), sds((2, rows, w1), BF16), sds((2, width, w2), BF16),
                   sds((2, width, w1), BF16), sds((2, width, w1), BF16)]
        + ([sds((width, rows), BF16)] if first else []),
        grid_spec=pltpu.PrefetchScalarGridSpec(
            num_scalar_prefetch=1, grid=(2,),
            in_specs=[whole((rows, width)), spec_a((p, w2), pick), spec_b((p, w2), pick)],
            out_specs=[head((rows, w2)), head((rows, w1)), head((width, w2)), head((width, w1)), head((width, w1))]
            + ([whole((width, rows))] if first else []),
            scratch_shapes=[pltpu.VMEM((width, w2), BF16)],
        ),
        compiler_params=params(24),
        cost_estimate=cost(2 * rows * width * 2 * (w1 + w2), 8 * rows * width),
    )(bits, x, wa, wb)


def out_kernel(x, m0, m1, wo0, wo1, gain, bias, hid, unit, inverse, hidt):
    attn = dot_nt(m0[0], wo0[0]) + dot_nt(m0[1], wo0[1]) + dot_nt(m1[0], wo1[0]) + dot_nt(m1[1], wo1[1])
    u, inv = norm_stats(x[...].astype(F32) + attn)
    h = (u * gain[...] + bias[...]).astype(BF16)
    hid[...] = h
    hidt[...] = h.T
    unit[...] = u
    inverse[...] = inv


def out_forward(x, m0, m1, wo0, wo1, gain, bias, block=256):
    rows, width = x.shape
    w1 = wo0.shape[2]
    sds = jax.ShapeDtypeStruct
    row = lambda w: pl.BlockSpec((block, w), lambda r: (r, 0))
    mix = pl.BlockSpec((2, block, w1), lambda r: (0, r, 0))
    return pl.pallas_call(
        out_kernel,
        grid=(rows // block,),
        out_shape=(sds((rows, width), BF16), sds((rows, width), F32), sds((rows, 1), F32), sds((width, rows), BF16)),
        in_specs=[row(width), mix, mix, whole((2, width, w1)), whole((2, width, w1)), whole((1, width)), whole((1, width))],
        out_specs=[row(width), row(width), row(1), pl.BlockSpec((width, block), lambda r: (0, r))],
        compiler_params=params(20),
        cost_estimate=cost(2 * rows * width * 4 * w1, 12 * rows * width),
    )(x, m0, m1, wo0, wo1, gain, bias)


def qkv_grad_kernel(last, bits, xt, dat, dqk, dv, mixed, *rest):
    if last:
        ra, rb, a_keep, a_send, b_keep, b_send, ta, tb = rest
    else:
        ga, gb, ta, tb = rest
    w1 = dv.shape[2]
    k = pl.program_id(0)
    ta[...] = dot_nn(xt[...], dqk[0]).astype(ta.dtype)
    tb[:, pl.ds(0, w1)] = dot_nn(xt[...], dv[0]).astype(tb.dtype)
    tb[:, pl.ds(w1, w1)] = dot_nn(dat[...], mixed[0]).astype(tb.dtype)
    if not last:
        scatter(ga, ta, bits, False)
        scatter(gb, tb, bits, True)
        return
    p = ra.shape[-2]

    def rows(r):
        return pl.ds(pl.multiple_of(own(bits, *r) * p, 16), p)

    def put_a(ref):
        for r in RELATIVE:
            ref[r] = (ta[rows(r), :] + ra[(0,) + r].astype(F32)).astype(BF16)

    @pl.when(k == 0)
    def _():
        put_a(a_keep)

    @pl.when(k == 1)
    def _():
        put_a(a_send)

    for r in RELATIVE:
        ref = b_send if r[0] else b_keep
        ref[(0,) + r[1:]] = (tb[rows(r), :] + rb[(r[0], 0) + r[1:]].astype(F32)).astype(BF16)


def qkv_grads(last, bits, xt, dat, dqk, dv, mixed, got=()):
    width, rows = xt.shape
    w2 = dqk.shape[2]
    w1 = dv.shape[2]
    per = width // 8
    sds = jax.ShapeDtypeStruct
    pick = lambda k: k
    head = lambda w: pl.BlockSpec((1, rows, w), lambda k, *_: (k, 0, 0))
    in_specs = [whole((width, rows)), whole((width, rows)), head(w2), head(w1), head(w1)]
    if last:
        in_specs += [spec_a((per, w2), pick), spec_b((per, w2), pick)]
        out_shape = [sds((2, 2, 2, per, w2), BF16)] * 4
        out_specs = [whole((2, 2, 2, per, w2))] * 2 + [
            pl.BlockSpec((1, 2, 2, per, w2), lambda k, *_: (k, 0, 0, 0, 0))
        ] * 2
    else:
        out_shape = [sds((2, 2, 2, 2, per, w2), BF16)] * 2
        out_specs = [spec_a((per, w2), pick), spec_b((per, w2), pick)]
    kind = F32 if last else BF16
    return pl.pallas_call(
        functools.partial(qkv_grad_kernel, last),
        out_shape=out_shape,
        grid_spec=pltpu.PrefetchScalarGridSpec(
            num_scalar_prefetch=1, grid=(2,), in_specs=in_specs, out_specs=out_specs,
            scratch_shapes=[pltpu.VMEM((width, w2), kind), pltpu.VMEM((width, w2), kind)],
        ),
        compiler_params=params(26),
        cost_estimate=cost(2 * rows * width * 2 * 2 * w2, 8 * rows * width),
    )(bits, xt, dat, dqk, dv, mixed, *got)


def dinput_kernel(dfirst, dqk0, dqk1, dv0, dv1, wqk0, wqk1, wv0, wv1, out):
    total = dfirst[...]
    for a, b, wa, wb in ((dqk0, dv0, wqk0, wv0), (dqk1, dv1, wqk1, wv1)):
        for k in range(2):
            total = total + dot_nt(a[k], wa[k]) + dot_nt(b[k], wb[k])
    out[...] = total


def input_backward(dfirst, dqk0, dqk1, dv0, dv1, wqk0, wqk1, wv0, wv1, block=256):
    rows, width = dfirst.shape
    w2 = wqk0.shape[2]
    w1 = wv0.shape[2]
    row = pl.BlockSpec((block, width), lambda r: (r, 0))
    part = lambda w: pl.BlockSpec((2, block, w), lambda r: (0, r, 0))
    return pl.pallas_call(
        dinput_kernel,
        grid=(rows // block,),
        out_shape=jax.ShapeDtypeStruct((rows, width), F32),
        in_specs=[row, part(w2), part(w2), part(w1), part(w1)]
        + [whole((2, width, w2))] * 2 + [whole((2, width, w1))] * 2,
        out_specs=row,
        compiler_params=params(24),
        cost_estimate=cost(2 * rows * width * 4 * (w1 + w2), 14 * rows * width),
    )(dfirst, dqk0, dqk1, dv0, dv1, wqk0, wqk1, wv0, wv1)


GROUPS = 8


def partner_dp(value, bit):
    size = lax.axis_size("dp")
    step = (1 << bit) * (size // GROUPS)
    return lax.ppermute(value, "dp", [(i, i ^ step) for i in range(size)])


def partner_head(value, bit):
    size = lax.axis_size("head")
    return lax.ppermute(value, "head", [(i, i ^ (1 << bit)) for i in range(size)])


def over_y(value):
    return partner_dp(value, 0)


def over_near(value):
    return partner_dp(value, 1)


def over_far(value):
    return partner_dp(value, 2)


def over_pair(value):
    return partner_head(value, 0)


def over_x(value):
    return partner_head(value, 1)


def inner_groups():
    inner = lax.axis_size("dp") // GROUPS
    return inner, [[g * inner + i for i in range(inner)] for g in range(GROUPS)]


def inner_gather(value, axis):
    inner, groups = inner_groups()
    if inner == 1:
        return value
    return lax.all_gather(value, "dp", axis_index_groups=groups, axis=axis, tiled=True)


def inner_scatter(value, axis):
    inner, groups = inner_groups()
    if inner == 1:
        return value
    return lax.psum_scatter(value, "dp", axis_index_groups=groups, scatter_dimension=axis, tiled=True)


def after(values, *waits):
    return lax.optimization_barrier((tuple(values), waits))[0]


def wide(value):
    return value.astype(F32)


def first_sum(keep, got):
    return (wide(keep[1]) + wide(got[1])).astype(BF16)


def second_sum(keep, got, more):
    return (wide(keep[0, 1]) + wide(got[0, 1]) + wide(more[1])).astype(BF16)


def third_sum(keep, got, more, last):
    return wide(keep[0, 0]) + wide(got[0, 0]) + wide(more[0]) + wide(last)


def low_sum(keep, got):
    return (wide(keep[1]) + wide(got[1])).astype(BF16)


def high_sum(keep, got, more):
    return wide(keep[0]) + wide(got[0]) + wide(more)


def total_steps():
    steps = []
    for name in ("head", "dp"):
        size = lax.axis_size(name)
        step = 1
        while step < size:
            steps.append((name, [(i, i ^ step) for i in range(size)]))
            step *= 2
    return steps


def total_some(value, *steps):
    for name, pairs in steps:
        value = value + lax.ppermute(value, name, pairs)
    return value


def per_device(layer_input, output_grad, lengths, w_qkv, w_out, w_up, w_down,
               norm_gains, norm_biases, mask_logits, mask_noise):
    micro, seq, width = layer_input.shape
    rows = micro * seq
    x = layer_input.reshape(rows, width)
    dout = output_grad.reshape(rows, width)
    place = lax.axis_index("dp") // (lax.axis_size("dp") // GROUPS)
    bits = jnp.stack([place & 1, (place >> 1) & 1, (place >> 2) & 1]).astype(jnp.int32)
    lens = lax.dynamic_slice_in_dim(lengths, lax.axis_index("head"), 1, 1).reshape(micro)

    gate_part = jax.nn.sigmoid(mask_logits + mask_noise)
    gate_all = inner_gather(gate_part.astype(BF16), 1)
    sub = gate_all.shape[1] // 2
    gain1, gain2 = norm_gains[0:1], norm_gains[1:2]
    bias1, bias2 = norm_biases[0:1], norm_biases[1:2]

    ga = jnp.stack([
        inner_gather(jnp.concatenate([w_qkv[0], w_qkv[1]], axis=1), 0),
        inner_gather(jnp.concatenate([w_qkv[2], w_out.T], axis=1), 0),
    ])
    gb = jnp.stack([gate_all[:, :sub], gate_all[:, sub:]])
    up_all, down_all = inner_gather(w_up, 0), inner_gather(w_down.T, 0)
    units = up_all.shape[1]
    most = units * 2 // 3
    gc = jnp.stack([up_all[:, :most], down_all[:, :most]])
    ge = jnp.stack([up_all[:, most:], down_all[:, most:]])

    got = over_far(ga)
    ga = jnp.stack([ga, got], axis=1)
    got = over_near(ga)
    ga = jnp.stack([ga, got], axis=1)
    aa, ab = ga[0], ga[1]
    (gb,) = after((gb,), got)
    ra, rb = over_y(aa), over_x(ab)
    far_b = over_far(gb)
    aa, ab = jnp.stack([aa, ra]), jnp.stack([ab, rb])
    gb, = after((gb,), ra, rb)
    gb = jnp.stack([gb, far_b], axis=1)
    aa, ab = after((aa, ab), gb)
    ra, rb = over_x(aa), over_y(ab)
    near_b = over_near(gb)
    (gc,) = after((gc,), near_b)
    far_c = over_far(gc)
    gb = jnp.stack([gb, near_b], axis=1)
    ba, bb = gb[0], gb[1]
    aa, ab = jnp.stack([aa, ra]), jnp.stack([ab, rb])
    ba, bb = after((ba, bb), ra, rb)
    ca, cb = over_pair(aa), over_pair(ab)
    ra, rb = over_y(ba), over_x(bb)
    qk0, v0, wqk0, wv0, wo0, xt = project(True, bits, x, aa, ab)
    ba, bb = jnp.stack([ba, ra]), jnp.stack([bb, rb])
    ba, bb, gc, ca, cb = after((ba, bb, gc, ca, cb), qk0, ra, rb)
    ra, rb = over_x(ba), over_y(bb)
    gc = jnp.stack([gc, far_c], axis=1)
    near_c = over_near(gc)
    qk1, v1, wqk1, wv1, wo1 = project(False, bits, x, ca, cb)
    ba, bb = jnp.stack([ba, ra]), jnp.stack([bb, rb])
    gc = jnp.stack([gc, near_c], axis=1)
    fa, fb = gc[0], gc[1]
    fa, fb, ba, bb, ge = after((fa, fb, ba, bb, ge), ra, rb, near_c, qk1)
    ba1, bb1 = over_pair(ba), over_pair(bb)
    ra, rb = over_y(fa), over_x(fb)
    far_e = over_far(ge)
    m0, lse0 = attention_forward(bits, lens, qk0, v0, ba, bb)
    fa, fb = jnp.stack([fa, ra]), jnp.stack([fb, rb])
    ge = jnp.stack([ge, far_e], axis=1)
    fa, fb, ge, ba1, bb1 = after((fa, fb, ge, ba1, bb1), m0)
    ra, rb = over_x(fa), over_y(fb)
    near_e = over_near(ge)
    ge = jnp.stack([ge, near_e], axis=1)
    m1, lse1 = attention_forward(bits, lens, qk1, v1, ba1, bb1)
    hid, unit, inverse, hidt = out_forward(x, m0, m1, wo0, wo1, gain1, bias1)
    fa, fb = jnp.stack([fa, ra]), jnp.stack([fb, rb])
    ea, eb = ge[0], ge[1]
    fa, fb, ea, eb = after((fa, fb, ea, eb), hid, ra, rb)
    fa1, fb1 = over_pair(fa), over_pair(fb)
    ra, rb = over_y(ea), over_x(eb)
    ea, eb = jnp.stack([ea, ra]), jnp.stack([eb, rb])
    ea, eb, hid = after((ea, eb, hid), fa1, fb1)
    ra, rb = over_x(ea), over_y(eb)
    actp, gpp, part = ffn_part(bits, hid, fa, fa1, fb, fb1)
    ea, eb = jnp.stack([ea, ra]), jnp.stack([eb, rb])
    ea, eb = after((ea, eb), part)
    ea1, eb1 = over_pair(ea), over_pair(eb)
    actq, gpq, out, dsec, dffn, dffnt, dgain2, dbias2 = ffn_rest(
        bits, lens, hid, ea, ea1, eb, eb1, part, gain2, bias2, dout
    )

    steps = total_steps()
    down0, down1 = down_grads(bits, dffnt, actp, actq)
    cd = over_pair(down1)
    dffn, = after((dffn,), down1)
    up1, part = ffn_backward(False, bits, hidt, dffn, fa1, ea1, fb1, eb1, gpp, gpq)
    down0, cd, up1, dffn = after((down0, cd, up1, dffn), part)
    xd = over_y(first_sum(down0, cd))
    cu = over_pair(up1)
    up0, dfirst, dattn, dattnt, dgain1, dbias1 = ffn_backward(
        True, bits, hidt, dffn, fa, ea, fb, eb, gpp, gpq, (dsec, part, unit, inverse, gain1)
    )
    up0, cu, norms, dattn = after((up0, cu, jnp.concatenate([dgain1, dgain2, dbias1, dbias2]), dattn), up0)
    xu = over_x(first_sum(up0, cu))
    norms = total_some(norms, steps[0])
    dqk1, dv1, ga1, gb1 = attention_backward(False, bits, lens, qk1, v1, ba1, bb1, lse1, dattn, wo1)
    ga1, gb1, norms, dqk1, xd = after((ga1, gb1, norms, dqk1, xd), dv1)
    cga, cgb = over_pair(ga1), over_pair(gb1)
    norms = total_some(norms, steps[3])
    qka1, vo1 = qkv_grads(False, bits, xt, dattnt, dqk1, dv1, m1)
    qka1, vo1, dattn, norms, cga, cgb, xu, xd = after((qka1, vo1, dattn, norms, cga, cgb, xu, xd), vo1)
    cqk, cvo = over_pair(qka1), over_pair(vo1)
    norms, = after((norms,), xu, xd)
    norms = total_some(norms, steps[1])
    send_d, send_u = second_sum(down0, cd, xd), second_sum(up0, cu, xu)
    send_d, send_u, norms = after((send_d, send_u, norms), norms)
    yd, yu = over_x(send_d), over_y(send_u)
    norms = total_some(norms, steps[4])
    dqk0, dv0, ga0, ga_out, gb0, gb_out = attention_backward(
        True, bits, lens, qk0, v0, ba, bb, lse0, dattn, wo0, (cga, cgb)
    )
    ga_out, gb_out, dqk0, norms, cqk, cvo, yd, yu = after((ga_out, gb_out, dqk0, norms, cqk, cvo, yd, yu), dv0)
    xga = over_x(ga_out)
    norms = total_some(norms, *steps[2:3], *steps[5:])
    gb_out, yu, yd, norms = after((gb_out, yu, yd, norms), norms)
    xgb = over_y(gb_out)
    u, d = third_sum(up0, cu, xu, yu), third_sum(down0, cd, xd, yd)
    send_f = jnp.stack([u[1], d[1]]).astype(BF16)
    near_f = over_near(send_f)
    qka0, qka_out, vo0, vo_out = qkv_grads(True, bits, xt, dattnt, dqk0, dv0, m0, (cqk, cvo))
    xqk, xvo = over_x(qka_out), over_y(vo_out)
    near_f, xga, xgb, dqk0 = after((near_f, xga, xgb, dqk0), vo0)
    yga, ygb = over_y(low_sum(ga0, xga)), over_x(low_sum(gb0, xgb))
    far_f = over_far(jnp.stack([u[0, 1] + wide(near_f[0, 1]), d[0, 1] + wide(near_f[1, 1])]).astype(BF16))
    dinput = input_backward(dfirst, dqk0, dqk1, dv0, dv1, wqk0, wqk1, wv0, wv1)
    xqk, xvo, yga, ygb, far_f = after((xqk, xvo, yga, ygb, far_f), dinput)
    send_qk, send_vo = low_sum(qka0, xqk), low_sum(vo0, xvo)
    g1, g2 = high_sum(ga0, xga, yga), high_sum(gb0, xgb, ygb)
    send_g = jnp.stack([g1[1], g2[1]]).astype(BF16)
    yqk, yvo = over_y(send_qk), over_x(send_vo)
    near_g = over_near(send_g)
    w1, w2 = high_sum(qka0, xqk, yqk), high_sum(vo0, xvo, yvo)
    send_w = jnp.stack([w1[1], w2[1]]).astype(BF16)
    send_g = jnp.stack([g1[0, 1] + wide(near_g[0, 1]), g2[0, 1] + wide(near_g[1, 1])]).astype(BF16)
    near_w = over_near(send_w)
    far_g = over_far(send_g)
    far_w = over_far(jnp.stack([w1[0, 1] + wide(near_w[0, 1]), w2[0, 1] + wide(near_w[1, 1])]).astype(BF16))

    up_grad = u[0, 0] + wide(near_f[0, 0]) + wide(far_f[0])
    down_grad = d[0, 0] + wide(near_f[1, 0]) + wide(far_f[1])
    gate_a = g1[0, 0] + wide(near_g[0, 0]) + wide(far_g[0])
    gate_b = g2[0, 0] + wide(near_g[1, 0]) + wide(far_g[1])
    qk_grad = w1[0, 0] + wide(near_w[0, 0]) + wide(far_w[0])
    vo_grad = w2[0, 0] + wide(near_w[1, 0]) + wide(far_w[1])

    qk_grad, vo_grad = inner_scatter(qk_grad, 0), inner_scatter(vo_grad, 0)
    local = vo_grad.shape[1] // 2
    gate_grad = inner_scatter(jnp.concatenate([gate_a, gate_b], axis=1), 1)
    return (
        out.reshape(micro, seq, width),
        dinput.reshape(micro, seq, width),
        jnp.stack([qk_grad[:, :local], qk_grad[:, local:], vo_grad[:, :local]]),
        vo_grad[:, local:].T,
        inner_scatter(up_grad, 0),
        inner_scatter(down_grad, 0).T,
        norms[:2],
        norms[2:],
        gate_grad * gate_part * (1.0 - gate_part),
    )


def solution(mesh):
    rows = P(None, ("dp", "head"), None)
    gates = P("head", "dp", None)
    weights = (P(None, "dp", "head"), P("head", "dp"), P("dp", "head"), P("head", "dp"))
    return jax.shard_map(
        per_device,
        mesh=mesh,
        in_specs=(rows, rows, P(None, "dp")) + weights + (P(), P(), gates, gates),
        out_specs=(rows, rows) + weights + (P(), P(), gates),
        check_vma=False,
    )
```

```python
import functools, math
import jax, jax.numpy as jnp
from jax import lax
from jax.experimental import pallas as pl
from jax.experimental.pallas import tpu as pltpu
from jax.sharding import PartitionSpec as P

HEAD_DIM = 64
EPS = 1e-05
F32 = jnp.float32
BF16 = jnp.bfloat16
GP = jnp.bfloat16
SCALE = 1.0 / math.sqrt(HEAD_DIM)
LOG2E = math.log2(math.e)
NEG = -1e30
INV_SQRT2 = 1.0 / math.sqrt(2.0)
INV_SQRT2PI = 1.0 / math.sqrt(2.0 * math.pi)


def dot_nn(a, b):
    return lax.dot_general(a, b, (((1,), (0,)), ((), ())), preferred_element_type=F32)


def dot_nt(a, b):
    return lax.dot_general(a, b, (((1,), (1,)), ((), ())), preferred_element_type=F32)


def dot_tn(a, b):
    return lax.dot_general(a, b, (((0,), (0,)), ((), ())), preferred_element_type=F32)


def piece(ref, bits, d, flip):
    y = bits[0] ^ (d & 1)
    z1 = bits[1] ^ ((d >> 1) & 1)
    z2 = bits[2] ^ ((d >> 2) & 1)
    if flip:
        return ref.at[y, 0, z1, z2]
    return ref.at[0, y, z1, z2]


def assemble(dst, ref, bits, flip, cols=None):
    rows = ref.shape[-2]
    cols = pl.ds(0, ref.shape[-1]) if cols is None else cols
    for d in range(8):
        dst[pl.ds(d * rows, rows), cols] = piece(ref, bits, d, flip)[...]


def scatter(ref, src, bits, flip):
    rows = ref.shape[-2]
    for d in range(8):
        piece(ref, bits, d, flip)[...] = src[pl.ds(d * rows, rows), :]


def own(bits, y, z1, z2):
    return (bits[0] ^ y) + 2 * (bits[1] ^ z1) + 4 * (bits[2] ^ z2)


RELATIVE = [(y, z1, z2) for y in range(2) for z1 in range(2) for z2 in range(2)]


def spec_a(tail, pick):
    zeros = (0,) * len(tail)
    return pl.BlockSpec((1, 2, 2, 2) + tail, lambda k, *_: (pick(k), 0, 0, 0) + zeros)


def spec_b(tail, pick):
    zeros = (0,) * len(tail)
    return pl.BlockSpec((2, 1, 2, 2) + tail, lambda k, *_: (0, pick(k), 0, 0) + zeros)


def whole(shape):
    zeros = (0,) * len(shape)
    return pl.BlockSpec(shape, lambda *_: zeros, pipeline_mode=pl.Buffered(1))


def low_pick(k):
    return jnp.minimum(k, 1)


def high_pick(k):
    return jnp.maximum(k - 2, 0)


def norm_stats(z):
    mean = jnp.mean(z, axis=1, keepdims=True)
    centered = z - mean
    inverse = lax.rsqrt(jnp.mean(centered * centered, axis=1, keepdims=True) + EPS)
    return centered * inverse, inverse


def norm_back(du, unit, inverse):
    return inverse * (
        du
        - jnp.mean(du, axis=1, keepdims=True)
        - unit * jnp.mean(du * unit, axis=1, keepdims=True)
    )


def gelu_pair(up):
    cdf = 0.5 + 0.5 * lax.erf(up * INV_SQRT2)
    pdf = INV_SQRT2PI * jnp.exp(-0.5 * (up * up))
    return up * cdf, cdf + up * pdf


SHARE = 10


def cost(flops, moved):
    return pl.CostEstimate(flops=flops * SHARE, bytes_accessed=moved * SHARE, transcendentals=0)


def params(mib=60, n=1):
    return pltpu.CompilerParams(
        dimension_semantics=("arbitrary",) * n, vmem_limit_bytes=mib * 1024 * 1024
    )


def load_pair(k, bits, wu, wd, ua0, ua1, db0, db1):
    @pl.when(k < 2)
    def _():
        assemble(wu, ua0, bits, False)
        assemble(wd, db0, bits, True)

    @pl.when(k >= 2)
    def _():
        assemble(wu, ua1, bits, False)
        assemble(wd, db1, bits, True)


def ffn_units(chunk, hid, wu, wd, act_o, gp_o, acc, finish=None):
    rows = hid.shape[0]
    ats = [pl.ds(r * chunk, chunk) for r in range(rows // chunk)]
    ahead = dot_nn(hid[ats[0], :], wu[...])
    for r, at in enumerate(ats):
        act, gp = gelu_pair(ahead)
        if r + 1 < len(ats):
            ahead = dot_nn(hid[ats[r + 1], :], wu[...])
        act = act.astype(BF16)
        act_o[0, at, :] = act
        gp_o[0, at, :] = gp.astype(gp_o.dtype)
        acc[at, :] += dot_nt(act, wd[...])
        if finish is not None:
            finish(r * chunk, chunk)


def ffn_part_kernel(chunk, bits, hid, ua0, ua1, db0, db1, act_o, gp_o, acc, wu, wd):
    k = pl.program_id(0)
    load_pair(k, bits, wu, wd, ua0, ua1, db0, db1)

    @pl.when(k == 0)
    def _():
        acc[...] = hid[...].astype(F32)

    ffn_units(chunk, hid, wu, wd, act_o, gp_o, acc)


def ffn_part(bits, hid, ua0, ua1, db0, db1, chunk=512):
    rows, width = hid.shape
    p, n = ua0.shape[-2:]
    sds = jax.ShapeDtypeStruct
    col = pl.BlockSpec((1, rows, n), lambda k, *_: (k, 0, 0))
    return pl.pallas_call(
        functools.partial(ffn_part_kernel, chunk),
        out_shape=(pltpu.HBM((4, rows, n), BF16), pltpu.HBM((4, rows, n), GP), sds((rows, width), F32)),
        grid_spec=pltpu.PrefetchScalarGridSpec(
            num_scalar_prefetch=1, grid=(4,),
            in_specs=[whole((rows, width)), spec_a((p, n), low_pick), spec_a((p, n), high_pick),
                      spec_b((p, n), low_pick), spec_b((p, n), high_pick)],
            out_specs=[col, col, whole((rows, width))],
            scratch_shapes=[pltpu.VMEM((width, n), BF16), pltpu.VMEM((width, n), BF16)],
        ),
        compiler_params=params(26),
        cost_estimate=cost(4 * rows * width * 4 * n, 16 * rows * width),
    )(bits, hid, ua0, ua1, db0, db1)


def ffn_rest_kernel(chunk, bits, lens, hid, ua0, ua1, db0, db1, part, gain, bias, dout,
                    act_o, gp_o, out, acc, dffn, dffnt, dgain, dbias, wu, wd):
    k = pl.program_id(0)
    rows = hid.shape[0]
    load_pair(k, bits, wu, wd, ua0, ua1, db0, db1)

    @pl.when(k == 0)
    def _():
        acc[...] = part[...]

    @pl.when(k < 3)
    def _():
        ffn_units(chunk, hid, wu, wd, act_o, gp_o, acc)

    @pl.when(k == 3)
    def _():
        length = rows // lens.shape[0]
        small = 256
        g = gain[...]
        b = bias[...]
        sums = [jnp.zeros_like(g), jnp.zeros_like(g)]

        def finish(start, count):
            for at0 in range(start, start + count, small):
                at = pl.ds(at0, small)
                size = lens[at0 // length]
                pos = (at0 % length) + lax.broadcasted_iota(jnp.int32, (small, 1), 0)
                valid = pos < size
                unit, inverse = norm_stats(acc[at, :])
                out[at, :] = jnp.where(valid, unit * g + b, 0.0).astype(BF16)
                dy = jnp.where(valid, dout[at, :].astype(F32), 0.0)
                sums[0] = sums[0] + jnp.sum(dy * unit, axis=0, keepdims=True)
                sums[1] = sums[1] + jnp.sum(dy, axis=0, keepdims=True)
                dz = norm_back(dy * g, unit, inverse)
                acc[at, :] = dz
                low = dz.astype(BF16)
                dffn[at, :] = low
                dffnt[:, at] = low.T

        ffn_units(chunk, hid, wu, wd, act_o, gp_o, acc, finish)
        dgain[...] = sums[0]
        dbias[...] = sums[1]


def ffn_rest(bits, lens, hid, ua0, ua1, db0, db1, part, gain, bias, dout, chunk=512):
    rows, width = hid.shape
    p, n = ua0.shape[-2:]
    sds = jax.ShapeDtypeStruct
    full = whole((rows, width))
    line = whole((1, width))
    col = pl.BlockSpec((1, rows, n), lambda k, *_: (k, 0, 0))
    return pl.pallas_call(
        functools.partial(ffn_rest_kernel, chunk),
        out_shape=(sds((4, rows, n), BF16), sds((4, rows, n), GP), sds((rows, width), BF16), sds((rows, width), F32),
                   sds((rows, width), BF16), sds((width, rows), BF16), sds((1, width), F32), sds((1, width), F32)),
        grid_spec=pltpu.PrefetchScalarGridSpec(
            num_scalar_prefetch=2, grid=(4,),
            in_specs=[full, spec_a((p, n), low_pick), spec_a((p, n), high_pick),
                      spec_b((p, n), low_pick), spec_b((p, n), high_pick), full, line, line, full],
            out_specs=[col, col, full, full, full, whole((width, rows)), line, line],
            scratch_shapes=[pltpu.VMEM((width, n), BF16), pltpu.VMEM((width, n), BF16)],
        ),
        compiler_params=params(30),
        cost_estimate=cost(4 * rows * width * 4 * n, 20 * rows * width),
    )(bits, lens, hid, ua0, ua1, db0, db1, part, gain, bias, dout)


def down_grad_kernel(bits, dt, actp, actq, keep, send):
    k = pl.program_id(0)
    first = dot_nn(dt[...], actp[0]).astype(BF16)
    second = dot_nn(dt[...], actq[0]).astype(BF16)
    rows = keep.shape[-2]
    n = actp.shape[2]

    def put(ref):
        for d in range(8):
            at = piece(ref, bits, d, True)
            at[:, pl.ds(0, n)] = first[d * rows : (d + 1) * rows]
            at[:, pl.ds(n, actq.shape[2])] = second[d * rows : (d + 1) * rows]

    @pl.when(k < 2)
    def _():
        put(keep)

    @pl.when(k >= 2)
    def _():
        put(send)


def down_grads(bits, dt, actp, actq):
    width, rows = dt.shape
    col = lambda a: pl.BlockSpec((1, rows, a.shape[2]), lambda k, *_: (k, 0, 0))
    n = actp.shape[2] + actq.shape[2]
    p = width // 8
    sds = jax.ShapeDtypeStruct
    return pl.pallas_call(
        down_grad_kernel,
        out_shape=(sds((2, 2, 2, 2, p, n), BF16), sds((2, 2, 2, 2, p, n), BF16)),
        grid_spec=pltpu.PrefetchScalarGridSpec(
            num_scalar_prefetch=1, grid=(4,),
            in_specs=[whole((width, rows)), col(actp), col(actq)],
            out_specs=[spec_b((p, n), low_pick), spec_b((p, n), high_pick)],
        ),
        compiler_params=params(22),
        cost_estimate=cost(2 * rows * width * 4 * n, 14 * rows * width),
    )(bits, dt, actp, actq)


def ffn_bwd_kernel(chunk, last, bits, ht, dffn, uap, uaq, dbp, dbq, gpp, gpq, *rest):
    if last:
        dsec, part, unit, inverse, gain, gu, acc, dattn, dattnt, dgain, dbias, wu, wd, dup_s = rest
    else:
        gu, acc, wu, wd, dup_s = rest
    k = pl.program_id(0)
    rows, width = dffn.shape
    np = uap.shape[-1]
    left, right = pl.ds(0, np), pl.ds(np, uaq.shape[-1])

    assemble(wu, uap, bits, False, left)
    assemble(wu, uaq, bits, False, right)
    assemble(wd, dbp, bits, True, left)
    assemble(wd, dbq, bits, True, right)

    @pl.when(k == 0)
    def _():
        if last:
            acc[...] = part[...] + dsec[...]
        else:
            acc[...] = jnp.zeros_like(acc)

    def run(finish=None):
        ats = [pl.ds(r * chunk, chunk) for r in range(rows // chunk)]
        ahead = dot_nn(dffn[ats[0], :], wd[...])
        for r, at in enumerate(ats):
            dup_s[at, left] = (ahead[:, :np] * gpp[0, at, :].astype(F32)).astype(BF16)
            dup_s[at, right] = (ahead[:, np:] * gpq[0, at, :].astype(F32)).astype(BF16)
            if r + 1 < len(ats):
                ahead = dot_nn(dffn[ats[r + 1], :], wd[...])
            acc[at, :] += dot_nt(dup_s[at, :], wu[...])
            if finish is not None:
                finish(r * chunk, chunk)
        grad = dot_nn(ht[...], dup_s[...]).astype(BF16)
        p = gu.shape[-2]
        for d in range(8):
            piece(gu, bits, d, False)[...] = grad[d * p : (d + 1) * p]

    if not last:
        run()
        return

    @pl.when(k == 0)
    def _():
        run()

    @pl.when(k == 1)
    def _():
        small = 256
        g = gain[...]
        sums = [jnp.zeros_like(g), jnp.zeros_like(g)]

        def finish(start, count):
            for at0 in range(start, start + count, small):
                at = pl.ds(at0, small)
                dh = acc[at, :]
                u = unit[at, :]
                sums[0] = sums[0] + jnp.sum(dh * u, axis=0, keepdims=True)
                sums[1] = sums[1] + jnp.sum(dh, axis=0, keepdims=True)
                dz = norm_back(dh * g, u, inverse[at, :])
                acc[at, :] = dz
                low = dz.astype(BF16)
                dattn[at, :] = low
                dattnt[:, at] = low.T

        run(finish)
        dgain[...] = sums[0]
        dbias[...] = sums[1]


def ffn_backward(last, bits, ht, dffn, uap, uaq, dbp, dbq, gpp, gpq, extra=(), chunk=512):
    rows, width = dffn.shape
    p, np = uap.shape[-2:]
    nq = uaq.shape[-1]
    n = np + nq
    sds = jax.ShapeDtypeStruct
    off = 0 if last else 2
    pick = lambda k: k
    full = whole((rows, width))
    line = whole((1, width))
    out_shape = [sds((2, 2, 2, 2, p, n), BF16)]
    out_specs = [spec_a((p, n), pick)]
    in_specs = [
        whole((width, rows)), full,
        spec_a((p, np), pick), spec_a((p, nq), pick), spec_b((p, np), pick), spec_b((p, nq), pick),
        pl.BlockSpec((1, rows, np), lambda k, *_: (k + off, 0, 0)),
        pl.BlockSpec((1, rows, nq), lambda k, *_: (k + off, 0, 0)),
    ]
    scratch = [pltpu.VMEM((width, n), BF16), pltpu.VMEM((width, n), BF16), pltpu.VMEM((rows, n), BF16)]
    if last:
        in_specs += [full] * 3 + [whole((rows, 1)), line]
        out_shape += [sds((rows, width), F32), sds((rows, width), BF16), sds((width, rows), BF16), sds((1, width), F32), sds((1, width), F32)]
        out_specs += [full, full, whole((width, rows)), line, line]
    else:
        out_shape += [sds((rows, width), F32)]
        out_specs += [full]
    return pl.pallas_call(
        functools.partial(ffn_bwd_kernel, chunk, last),
        out_shape=out_shape,
        grid_spec=pltpu.PrefetchScalarGridSpec(
            num_scalar_prefetch=1, grid=(2,), in_specs=in_specs, out_specs=out_specs, scratch_shapes=scratch,
        ),
        compiler_params=params(36),
        cost_estimate=cost(6 * rows * width * 2 * n, 30 * rows * width),
    )(bits, ht, dffn, uap, uaq, dbp, dbq, gpp, gpq, *extra)


def key_bias(size, length):
    pos = lax.broadcasted_iota(jnp.int32, (1, length), 1)
    return jnp.where(pos < size, 0.0, NEG).astype(F32)


def gate_rows(ga, gb, bits, i, d0, count):
    parts = []
    for j in range(count):
        d = d0 + j
        y = bits[0] ^ (d & 1)
        z1 = bits[1] ^ ((d >> 1) & 1)
        z2 = bits[2] ^ ((d >> 2) & 1)
        parts.append(ga[0, y, z1, z2, i])
        parts.append(gb[y, 0, z1, z2, i])
    return jnp.concatenate(parts, axis=0).astype(F32)


def att_fwd_kernel(bits, lens, qk, v, ga, gb, mixed, lse):
    length = qk.shape[1]
    heads = v.shape[2] // HEAD_DIM
    bias = key_bias(lens[pl.program_id(1)], length)
    count = length // (2 * ga.shape[-2])
    cols = [pl.ds(i * HEAD_DIM, HEAD_DIM) for i in range(2 * heads)]

    def score(i):
        return dot_nt(qk[0, :, cols[i]], qk[0, :, cols[heads + i]])

    ahead = score(0)
    outs = []
    stats = []
    for i in range(heads):
        s = ahead * (SCALE * LOG2E) + bias
        if i + 1 < heads:
            ahead = score(i + 1)
        top = jnp.max(s, axis=1, keepdims=True)
        e = jnp.exp2(s - top)
        total = jnp.sum(e, axis=1, keepdims=True)
        w = (e * gate_rows(ga, gb, bits, i, 0, count)).astype(BF16)
        outs.append(dot_nn(w, v[0, :, cols[i]]) * (1.0 / total))
        stats.append(top + jnp.log2(total))
    mixed[0] = jnp.concatenate(outs, axis=1).astype(BF16)
    lse[0] = jnp.concatenate(stats, axis=1)


def attention_forward(bits, lens, qk, v, ga, gb):
    _, rows, w2 = qk.shape
    w1 = v.shape[2]
    count = lens.shape[0]
    length = rows // count
    heads, sub, keys = ga.shape[-3:]
    sds = jax.ShapeDtypeStruct
    return pl.pallas_call(
        att_fwd_kernel,
        out_shape=(sds((2, rows, w1), BF16), sds((2, rows, heads), F32)),
        grid_spec=pltpu.PrefetchScalarGridSpec(
            num_scalar_prefetch=2, grid=(2, count),
            in_specs=[
                pl.BlockSpec((1, length, w2), lambda k, s, *_: (k, s, 0)),
                pl.BlockSpec((1, length, w1), lambda k, s, *_: (k, s, 0)),
                spec_a((heads, sub, keys), lambda k: k), spec_b((heads, sub, keys), lambda k: k),
            ],
            out_specs=[
                pl.BlockSpec((1, length, w1), lambda k, s, *_: (k, s, 0)),
                pl.BlockSpec((1, length, heads), lambda k, s, *_: (k, s, 0)),
            ],
        ),
        compiler_params=params(22, 2),
        cost_estimate=cost(16 * 2 * rows * length * w1, 16 * rows * w1),
    )(bits, lens, qk, v, ga, gb)


def att_bwd_kernel(last, bits, lens, qk, v, ga, gb, lse, dattn, wo, *rest):
    if last:
        ra, rb, dqk, dv, a_keep, a_send, b_keep, b_send, dm_s, dmt, qt, acc = rest
    else:
        dqk, dv, oga, ogb, dm_s, dmt, qt, acc = rest
    length = qk.shape[1]
    heads = v.shape[2] // HEAD_DIM
    hw = heads * HEAD_DIM
    k = pl.program_id(0)
    seq = pl.program_id(1)
    bias = key_bias(lens[seq], length)
    sub = ga.shape[-2]
    count = length // (2 * sub)
    cols = [pl.ds(i * HEAD_DIM, HEAD_DIM) for i in range(2 * heads)]

    dm = dot_nn(dattn[...], wo[0]).astype(BF16)
    dm_s[...] = dm
    dmt[...] = dm.T
    qt[...] = qk[0, :, pl.ds(0, hw)].T

    def products(i):
        return (
            dot_nt(qk[0, :, cols[i]], qk[0, :, cols[heads + i]]),
            dot_nt(dm_s[:, cols[i]], v[0, :, cols[i]]),
        )

    ahead = products(0)
    dqs, dks, dvs = [], [], []
    for i in range(heads):
        s, dw = ahead
        p = jnp.exp2(s * (SCALE * LOG2E) + bias - lse[0, :, pl.ds(i, 1)])
        if i + 1 < heads:
            ahead = products(i + 1)
        g = gate_rows(ga, gb, bits, i, 0, count)
        w = (p * g).astype(BF16)
        t = dw * p
        acc[i] = t + jnp.where(seq == 0, 0.0, acc[i])
        u = t * g
        ds = (u - p * jnp.sum(u, axis=1, keepdims=True)).astype(BF16)
        dqs.append(dot_nn(ds, qk[0, :, cols[heads + i]]) * SCALE)
        dvs.append(dot_nn(dmt[cols[i], :], w).astype(BF16).T)
        dks.append((dot_nn(qt[cols[i], :], ds) * SCALE).astype(BF16).T)
    dqk[0] = jnp.concatenate([d.astype(BF16) for d in dqs] + dks, axis=1)
    dv[0] = jnp.concatenate(dvs, axis=1)

    def first_rows(y, z1, z2):
        return pl.ds(pl.multiple_of(own(bits, y, z1, z2) * 2 * sub, sub), sub)

    def second_rows(y, z1, z2):
        return pl.ds(pl.multiple_of(own(bits, y, z1, z2) * 2 * sub + sub, sub), sub)

    @pl.when(seq == pl.num_programs(1) - 1)
    def _():
        if not last:
            for r in RELATIVE:
                for i in range(heads):
                    oga[(0,) + r + (i,)] = acc[i, first_rows(*r), :].astype(BF16)
                    ogb[(r[0], 0) + r[1:] + (i,)] = acc[i, second_rows(*r), :].astype(BF16)
            return

        def put_a(ref):
            for r in RELATIVE:
                for i in range(heads):
                    ref[r + (i,)] = (acc[i, first_rows(*r), :] + ra[(0,) + r + (i,)].astype(F32)).astype(BF16)

        @pl.when(k == 0)
        def _():
            put_a(a_keep)

        @pl.when(k == 1)
        def _():
            put_a(a_send)

        for r in RELATIVE:
            ref = b_send if r[0] else b_keep
            for i in range(heads):
                ref[(0,) + r[1:] + (i,)] = (
                    acc[i, second_rows(*r), :] + rb[(r[0], 0) + r[1:] + (i,)].astype(F32)
                ).astype(BF16)


def attention_backward(last, bits, lens, qk, v, ga, gb, lse, dattn, wo, got=()):
    _, rows, w2 = qk.shape
    w1 = v.shape[2]
    width = dattn.shape[1]
    count = lens.shape[0]
    length = rows // count
    tail = ga.shape[-3:]
    heads, sub, keys = tail
    sds = jax.ShapeDtypeStruct
    pick = lambda k: k
    in_specs = [
        pl.BlockSpec((1, length, w2), lambda k, s, *_: (k, s, 0)),
        pl.BlockSpec((1, length, w1), lambda k, s, *_: (k, s, 0)),
        spec_a(tail, pick), spec_b(tail, pick),
        pl.BlockSpec((1, length, heads), lambda k, s, *_: (k, s, 0)),
        pl.BlockSpec((length, width), lambda k, s, *_: (s, 0)),
        pl.BlockSpec((1, width, w1), lambda k, s, *_: (k, 0, 0)),
    ]
    out_shape = [sds((2, rows, w2), BF16), sds((2, rows, w1), BF16)]
    out_specs = [
        pl.BlockSpec((1, length, w2), lambda k, s, *_: (k, s, 0)),
        pl.BlockSpec((1, length, w1), lambda k, s, *_: (k, s, 0)),
    ]
    if last:
        in_specs += [spec_a(tail, pick), spec_b(tail, pick)]
        out_shape += [sds((2, 2, 2) + tail, BF16)] * 4
        out_specs += [whole((2, 2, 2) + tail)] * 2 + [
            pl.BlockSpec((1, 2, 2) + tail, lambda k, *_: (k, 0, 0, 0, 0, 0))
        ] * 2
    else:
        out_shape += [sds((2, 2, 2, 2) + tail, BF16)] * 2
        out_specs += [spec_a(tail, pick), spec_b(tail, pick)]
    return pl.pallas_call(
        functools.partial(att_bwd_kernel, last),
        out_shape=out_shape,
        grid_spec=pltpu.PrefetchScalarGridSpec(
            num_scalar_prefetch=2, grid=(2, count), in_specs=in_specs, out_specs=out_specs,
            scratch_shapes=[
                pltpu.VMEM((length, w1), BF16), pltpu.VMEM((w1, length), BF16),
                pltpu.VMEM((w1, length), BF16), pltpu.VMEM((heads, length, keys), F32),
            ],
        ),
        compiler_params=params(30, 2),
        cost_estimate=cost(40 * 2 * rows * length * w1, 30 * rows * w1),
    )(bits, lens, qk, v, ga, gb, lse, dattn, wo, *got)


def qkv_kernel(first, bits, x, wa, wb, qk, v, wqk, wv, wo, *rest):
    w1 = v.shape[2]
    wb_s = rest[-1]
    assemble(wqk.at[0], wa, bits, False)
    assemble(wb_s, wb, bits, True)

    if first:

        @pl.when(pl.program_id(0) == 0)
        def _():
            rest[0][...] = x[...].T

    wv[0] = wb_s[:, pl.ds(0, w1)]
    wo[0] = wb_s[:, pl.ds(w1, w1)]
    qk[0] = dot_nn(x[...], wqk[0]).astype(BF16)
    v[0] = dot_nn(x[...], wv[0]).astype(BF16)


def project(first, bits, x, wa, wb):
    rows, width = x.shape
    p, w2 = wa.shape[-2:]
    w1 = w2 // 2
    sds = jax.ShapeDtypeStruct
    pick = lambda k: k
    head = lambda s: pl.BlockSpec((1,) + s, lambda k, *_: (k, 0, 0))
    return pl.pallas_call(
        functools.partial(qkv_kernel, first),
        out_shape=[sds((2, rows, w2), BF16), sds((2, rows, w1), BF16), pltpu.HBM((2, width, w2), BF16),
                   pltpu.HBM((2, width, w1), BF16), sds((2, width, w1), BF16)]
        + ([pltpu.HBM((width, rows), BF16)] if first else []),
        grid_spec=pltpu.PrefetchScalarGridSpec(
            num_scalar_prefetch=1, grid=(2,),
            in_specs=[whole((rows, width)), spec_a((p, w2), pick), spec_b((p, w2), pick)],
            out_specs=[head((rows, w2)), head((rows, w1)), head((width, w2)), head((width, w1)), head((width, w1))]
            + ([whole((width, rows))] if first else []),
            scratch_shapes=[pltpu.VMEM((width, w2), BF16)],
        ),
        compiler_params=params(24),
        cost_estimate=cost(2 * rows * width * 2 * (w1 + w2), 8 * rows * width),
    )(bits, x, wa, wb)


def out_kernel(x, m0, m1, wo0, wo1, gain, bias, hid, unit, inverse, hidt):
    attn = dot_nt(m0[0], wo0[0]) + dot_nt(m0[1], wo0[1]) + dot_nt(m1[0], wo1[0]) + dot_nt(m1[1], wo1[1])
    u, inv = norm_stats(x[...].astype(F32) + attn)
    h = (u * gain[...] + bias[...]).astype(BF16)
    hid[...] = h
    hidt[...] = h.T
    unit[...] = u
    inverse[...] = inv


def out_forward(x, m0, m1, wo0, wo1, gain, bias, block=256):
    rows, width = x.shape
    w1 = wo0.shape[2]
    sds = jax.ShapeDtypeStruct
    row = lambda w: pl.BlockSpec((block, w), lambda r: (r, 0))
    mix = pl.BlockSpec((2, block, w1), lambda r: (0, r, 0))
    return pl.pallas_call(
        out_kernel,
        grid=(rows // block,),
        out_shape=(sds((rows, width), BF16), pltpu.HBM((rows, width), F32), sds((rows, 1), F32), pltpu.HBM((width, rows), BF16)),
        in_specs=[row(width), mix, mix, whole((2, width, w1)), whole((2, width, w1)), whole((1, width)), whole((1, width))],
        out_specs=[row(width), row(width), row(1), pl.BlockSpec((width, block), lambda r: (0, r))],
        compiler_params=params(20),
        cost_estimate=cost(2 * rows * width * 4 * w1, 12 * rows * width),
    )(x, m0, m1, wo0, wo1, gain, bias)


def qkv_grad_kernel(last, bits, xt, dat, dqk, dv, mixed, *rest):
    if last:
        ra, rb, a_keep, a_send, b_keep, b_send, ta, tb = rest
    else:
        ga, gb, ta, tb = rest
    w1 = dv.shape[2]
    k = pl.program_id(0)
    ta[...] = dot_nn(xt[...], dqk[0]).astype(ta.dtype)
    tb[:, pl.ds(0, w1)] = dot_nn(xt[...], dv[0]).astype(tb.dtype)
    tb[:, pl.ds(w1, w1)] = dot_nn(dat[...], mixed[0]).astype(tb.dtype)
    if not last:
        scatter(ga, ta, bits, False)
        scatter(gb, tb, bits, True)
        return
    p = ra.shape[-2]

    def rows(r):
        return pl.ds(pl.multiple_of(own(bits, *r) * p, 16), p)

    def put_a(ref):
        for r in RELATIVE:
            ref[r] = (ta[rows(r), :] + ra[(0,) + r].astype(F32)).astype(BF16)

    @pl.when(k == 0)
    def _():
        put_a(a_keep)

    @pl.when(k == 1)
    def _():
        put_a(a_send)

    for r in RELATIVE:
        ref = b_send if r[0] else b_keep
        ref[(0,) + r[1:]] = (tb[rows(r), :] + rb[(r[0], 0) + r[1:]].astype(F32)).astype(BF16)


def qkv_grads(last, bits, xt, dat, dqk, dv, mixed, got=()):
    width, rows = xt.shape
    w2 = dqk.shape[2]
    w1 = dv.shape[2]
    per = width // 8
    sds = jax.ShapeDtypeStruct
    pick = lambda k: k
    head = lambda w: pl.BlockSpec((1, rows, w), lambda k, *_: (k, 0, 0))
    in_specs = [whole((width, rows)), whole((width, rows)), head(w2), head(w1), head(w1)]
    if last:
        in_specs += [spec_a((per, w2), pick), spec_b((per, w2), pick)]
        out_shape = [sds((2, 2, 2, per, w2), BF16)] * 4
        out_specs = [whole((2, 2, 2, per, w2))] * 2 + [
            pl.BlockSpec((1, 2, 2, per, w2), lambda k, *_: (k, 0, 0, 0, 0))
        ] * 2
    else:
        out_shape = [sds((2, 2, 2, 2, per, w2), BF16)] * 2
        out_specs = [spec_a((per, w2), pick), spec_b((per, w2), pick)]
    kind = F32 if last else BF16
    return pl.pallas_call(
        functools.partial(qkv_grad_kernel, last),
        out_shape=out_shape,
        grid_spec=pltpu.PrefetchScalarGridSpec(
            num_scalar_prefetch=1, grid=(2,), in_specs=in_specs, out_specs=out_specs,
            scratch_shapes=[pltpu.VMEM((width, w2), kind), pltpu.VMEM((width, w2), kind)],
        ),
        compiler_params=params(26),
        cost_estimate=cost(2 * rows * width * 2 * 2 * w2, 8 * rows * width),
    )(bits, xt, dat, dqk, dv, mixed, *got)


def dinput_kernel(dfirst, dqk0, dqk1, dv0, dv1, wqk0, wqk1, wv0, wv1, out):
    total = dfirst[...]
    for a, b, wa, wb in ((dqk0, dv0, wqk0, wv0), (dqk1, dv1, wqk1, wv1)):
        for k in range(2):
            total = total + dot_nt(a[k], wa[k]) + dot_nt(b[k], wb[k])
    out[...] = total


def input_backward(dfirst, dqk0, dqk1, dv0, dv1, wqk0, wqk1, wv0, wv1, block=256):
    rows, width = dfirst.shape
    w2 = wqk0.shape[2]
    w1 = wv0.shape[2]
    row = pl.BlockSpec((block, width), lambda r: (r, 0))
    part = lambda w: pl.BlockSpec((2, block, w), lambda r: (0, r, 0))
    return pl.pallas_call(
        dinput_kernel,
        grid=(rows // block,),
        out_shape=jax.ShapeDtypeStruct((rows, width), F32),
        in_specs=[row, part(w2), part(w2), part(w1), part(w1)]
        + [whole((2, width, w2))] * 2 + [whole((2, width, w1))] * 2,
        out_specs=row,
        compiler_params=params(24),
        cost_estimate=cost(2 * rows * width * 4 * (w1 + w2), 14 * rows * width),
    )(dfirst, dqk0, dqk1, dv0, dv1, wqk0, wqk1, wv0, wv1)


GROUPS = 8


def partner_dp(value, bit):
    size = lax.axis_size("dp")
    step = (1 << bit) * (size // GROUPS)
    return lax.ppermute(value, "dp", [(i, i ^ step) for i in range(size)])


def partner_head(value, bit):
    size = lax.axis_size("head")
    return lax.ppermute(value, "head", [(i, i ^ (1 << bit)) for i in range(size)])


def over_y(value):
    return partner_dp(value, 0)


def over_near(value):
    return partner_dp(value, 1)


def over_far(value):
    return partner_dp(value, 2)


def over_pair(value):
    return partner_head(value, 0)


def over_x(value):
    return partner_head(value, 1)


def inner_groups():
    inner = lax.axis_size("dp") // GROUPS
    return inner, [[g * inner + i for i in range(inner)] for g in range(GROUPS)]


def inner_gather(value, axis):
    inner, groups = inner_groups()
    if inner == 1:
        return value
    return lax.all_gather(value, "dp", axis_index_groups=groups, axis=axis, tiled=True)


def inner_scatter(value, axis):
    inner, groups = inner_groups()
    if inner == 1:
        return value
    return lax.psum_scatter(value, "dp", axis_index_groups=groups, scatter_dimension=axis, tiled=True)


def after(values, *waits):
    return lax.optimization_barrier((tuple(values), waits))[0]


def wide(value):
    return value.astype(F32)


def first_sum(keep, got):
    return (wide(keep[1]) + wide(got[1])).astype(BF16)


def second_sum(keep, got, more):
    return (wide(keep[0, 1]) + wide(got[0, 1]) + wide(more[1])).astype(BF16)


def third_sum(keep, got, more, last):
    return wide(keep[0, 0]) + wide(got[0, 0]) + wide(more[0]) + wide(last)


def low_sum(keep, got):
    return (wide(keep[1]) + wide(got[1])).astype(BF16)


def high_sum(keep, got, more):
    return wide(keep[0]) + wide(got[0]) + wide(more)


def total_steps():
    steps = []
    for name in ("head", "dp"):
        size = lax.axis_size(name)
        step = 1
        while step < size:
            steps.append((name, [(i, i ^ step) for i in range(size)]))
            step *= 2
    return steps


def total_some(value, *steps):
    for name, pairs in steps:
        value = value + lax.ppermute(value, name, pairs)
    return value


def per_device(layer_input, output_grad, lengths, w_qkv, w_out, w_up, w_down,
               norm_gains, norm_biases, mask_logits, mask_noise):
    micro, seq, width = layer_input.shape
    rows = micro * seq
    x = layer_input.reshape(rows, width)
    dout = output_grad.reshape(rows, width)
    place = lax.axis_index("dp") // (lax.axis_size("dp") // GROUPS)
    bits = jnp.stack([place & 1, (place >> 1) & 1, (place >> 2) & 1]).astype(jnp.int32)
    lens = lax.dynamic_slice_in_dim(lengths, lax.axis_index("head"), 1, 1).reshape(micro)

    gate_part = jax.nn.sigmoid(mask_logits + mask_noise)
    gate_all = inner_gather(gate_part.astype(BF16), 1)
    sub = gate_all.shape[1] // 2
    gain1, gain2 = norm_gains[0:1], norm_gains[1:2]
    bias1, bias2 = norm_biases[0:1], norm_biases[1:2]

    ga = jnp.stack([
        inner_gather(jnp.concatenate([w_qkv[0], w_qkv[1]], axis=1), 0),
        inner_gather(jnp.concatenate([w_qkv[2], w_out.T], axis=1), 0),
    ])
    gb = jnp.stack([gate_all[:, :sub], gate_all[:, sub:]])
    up_all, down_all = inner_gather(w_up, 0), inner_gather(w_down.T, 0)
    units = up_all.shape[1]
    most = units * 2 // 3
    gc = jnp.stack([up_all[:, :most], down_all[:, :most]])
    ge = jnp.stack([up_all[:, most:], down_all[:, most:]])

    got = over_far(ga)
    ga = jnp.stack([ga, got], axis=1)
    got = over_near(ga)
    ga = jnp.stack([ga, got], axis=1)
    aa, ab = ga[0], ga[1]
    (gb,) = after((gb,), got)
    ra, rb = over_y(aa), over_x(ab)
    far_b = over_far(gb)
    aa, ab = jnp.stack([aa, ra]), jnp.stack([ab, rb])
    gb, = after((gb,), ra, rb)
    gb = jnp.stack([gb, far_b], axis=1)
    aa, ab = after((aa, ab), gb)
    ra, rb = over_x(aa), over_y(ab)
    near_b = over_near(gb)
    (gc,) = after((gc,), near_b)
    far_c = over_far(gc)
    gb = jnp.stack([gb, near_b], axis=1)
    ba, bb = gb[0], gb[1]
    aa, ab = jnp.stack([aa, ra]), jnp.stack([ab, rb])
    ba, bb = after((ba, bb), ra, rb)
    ca, cb = over_pair(aa), over_pair(ab)
    ra, rb = over_y(ba), over_x(bb)
    qk0, v0, wqk0, wv0, wo0, xt = project(True, bits, x, aa, ab)
    ba, bb = jnp.stack([ba, ra]), jnp.stack([bb, rb])
    ba, bb, gc, ca, cb = after((ba, bb, gc, ca, cb), qk0, ra, rb)
    ra, rb = over_x(ba), over_y(bb)
    gc = jnp.stack([gc, far_c], axis=1)
    near_c = over_near(gc)
    qk1, v1, wqk1, wv1, wo1 = project(False, bits, x, ca, cb)
    ba, bb = jnp.stack([ba, ra]), jnp.stack([bb, rb])
    gc = jnp.stack([gc, near_c], axis=1)
    fa, fb = gc[0], gc[1]
    fa, fb, ba, bb, ge = after((fa, fb, ba, bb, ge), ra, rb, near_c, qk1)
    ba1, bb1 = over_pair(ba), over_pair(bb)
    ra, rb = over_y(fa), over_x(fb)
    far_e = over_far(ge)
    m0, lse0 = attention_forward(bits, lens, qk0, v0, ba, bb)
    fa, fb = jnp.stack([fa, ra]), jnp.stack([fb, rb])
    ge = jnp.stack([ge, far_e], axis=1)
    fa, fb, ge, ba1, bb1 = after((fa, fb, ge, ba1, bb1), m0)
    ra, rb = over_x(fa), over_y(fb)
    near_e = over_near(ge)
    ge = jnp.stack([ge, near_e], axis=1)
    m1, lse1 = attention_forward(bits, lens, qk1, v1, ba1, bb1)
    hid, unit, inverse, hidt = out_forward(x, m0, m1, wo0, wo1, gain1, bias1)
    fa, fb = jnp.stack([fa, ra]), jnp.stack([fb, rb])
    ea, eb = ge[0], ge[1]
    fa, fb, ea, eb = after((fa, fb, ea, eb), hid, ra, rb)
    fa1, fb1 = over_pair(fa), over_pair(fb)
    ra, rb = over_y(ea), over_x(eb)
    ea, eb = jnp.stack([ea, ra]), jnp.stack([eb, rb])
    ea, eb, hid = after((ea, eb, hid), fa1, fb1)
    ra, rb = over_x(ea), over_y(eb)
    actp, gpp, part = ffn_part(bits, hid, fa, fa1, fb, fb1)
    ea, eb = jnp.stack([ea, ra]), jnp.stack([eb, rb])
    ea, eb = after((ea, eb), part)
    ea1, eb1 = over_pair(ea), over_pair(eb)
    actq, gpq, out, dsec, dffn, dffnt, dgain2, dbias2 = ffn_rest(
        bits, lens, hid, ea, ea1, eb, eb1, part, gain2, bias2, dout
    )

    steps = total_steps()
    down0, down1 = down_grads(bits, dffnt, actp, actq)
    cd = over_pair(down1)
    dffn, = after((dffn,), down1)
    up1, part = ffn_backward(False, bits, hidt, dffn, fa1, ea1, fb1, eb1, gpp, gpq)
    down0, cd, up1, dffn = after((down0, cd, up1, dffn), part)
    xd = over_y(first_sum(down0, cd))
    cu = over_pair(up1)
    up0, dfirst, dattn, dattnt, dgain1, dbias1 = ffn_backward(
        True, bits, hidt, dffn, fa, ea, fb, eb, gpp, gpq, (dsec, part, unit, inverse, gain1)
    )
    up0, cu, norms, dattn = after((up0, cu, jnp.concatenate([dgain1, dgain2, dbias1, dbias2]), dattn), up0)
    xu = over_x(first_sum(up0, cu))
    norms = total_some(norms, steps[0])
    dqk1, dv1, ga1, gb1 = attention_backward(False, bits, lens, qk1, v1, ba1, bb1, lse1, dattn, wo1)
    ga1, gb1, norms, dqk1, xd = after((ga1, gb1, norms, dqk1, xd), dv1)
    cga, cgb = over_pair(ga1), over_pair(gb1)
    norms = total_some(norms, steps[3])
    qka1, vo1 = qkv_grads(False, bits, xt, dattnt, dqk1, dv1, m1)
    qka1, vo1, dattn, norms, cga, cgb, xu, xd = after((qka1, vo1, dattn, norms, cga, cgb, xu, xd), vo1)
    cqk, cvo = over_pair(qka1), over_pair(vo1)
    norms, = after((norms,), xu, xd)
    norms = total_some(norms, steps[1])
    send_d, send_u = second_sum(down0, cd, xd), second_sum(up0, cu, xu)
    send_d, send_u, norms = after((send_d, send_u, norms), norms)
    yd, yu = over_x(send_d), over_y(send_u)
    norms = total_some(norms, steps[4])
    dqk0, dv0, ga0, ga_out, gb0, gb_out = attention_backward(
        True, bits, lens, qk0, v0, ba, bb, lse0, dattn, wo0, (cga, cgb)
    )
    ga_out, gb_out, dqk0, norms, cqk, cvo, yd, yu = after((ga_out, gb_out, dqk0, norms, cqk, cvo, yd, yu), dv0)
    xga = over_x(ga_out)
    norms = total_some(norms, *steps[2:3], *steps[5:])
    gb_out, yu, yd, norms = after((gb_out, yu, yd, norms), norms)
    xgb = over_y(gb_out)
    u, d = third_sum(up0, cu, xu, yu), third_sum(down0, cd, xd, yd)
    send_f = jnp.stack([u[1], d[1]]).astype(BF16)
    near_f = over_near(send_f)
    qka0, qka_out, vo0, vo_out = qkv_grads(True, bits, xt, dattnt, dqk0, dv0, m0, (cqk, cvo))
    xqk, xvo = over_x(qka_out), over_y(vo_out)
    near_f, xga, xgb, dqk0 = after((near_f, xga, xgb, dqk0), vo0)
    yga, ygb = over_y(low_sum(ga0, xga)), over_x(low_sum(gb0, xgb))
    far_f = over_far(jnp.stack([u[0, 1] + wide(near_f[0, 1]), d[0, 1] + wide(near_f[1, 1])]).astype(BF16))
    dinput = input_backward(dfirst, dqk0, dqk1, dv0, dv1, wqk0, wqk1, wv0, wv1)
    xqk, xvo, yga, ygb, far_f = after((xqk, xvo, yga, ygb, far_f), dinput)
    send_qk, send_vo = low_sum(qka0, xqk), low_sum(vo0, xvo)
    g1, g2 = high_sum(ga0, xga, yga), high_sum(gb0, xgb, ygb)
    send_g = jnp.stack([g1[1], g2[1]]).astype(BF16)
    yqk, yvo = over_y(send_qk), over_x(send_vo)
    near_g = over_near(send_g)
    w1, w2 = high_sum(qka0, xqk, yqk), high_sum(vo0, xvo, yvo)
    send_w = jnp.stack([w1[1], w2[1]]).astype(BF16)
    send_g = jnp.stack([g1[0, 1] + wide(near_g[0, 1]), g2[0, 1] + wide(near_g[1, 1])]).astype(BF16)
    near_w = over_near(send_w)
    far_g = over_far(send_g)
    far_w = over_far(jnp.stack([w1[0, 1] + wide(near_w[0, 1]), w2[0, 1] + wide(near_w[1, 1])]).astype(BF16))

    up_grad = u[0, 0] + wide(near_f[0, 0]) + wide(far_f[0])
    down_grad = d[0, 0] + wide(near_f[1, 0]) + wide(far_f[1])
    gate_a = g1[0, 0] + wide(near_g[0, 0]) + wide(far_g[0])
    gate_b = g2[0, 0] + wide(near_g[1, 0]) + wide(far_g[1])
    qk_grad = w1[0, 0] + wide(near_w[0, 0]) + wide(far_w[0])
    vo_grad = w2[0, 0] + wide(near_w[1, 0]) + wide(far_w[1])

    qk_grad, vo_grad = inner_scatter(qk_grad, 0), inner_scatter(vo_grad, 0)
    local = vo_grad.shape[1] // 2
    gate_grad = inner_scatter(jnp.concatenate([gate_a, gate_b], axis=1), 1)
    return (
        out.reshape(micro, seq, width),
        dinput.reshape(micro, seq, width),
        jnp.stack([qk_grad[:, :local], qk_grad[:, local:], vo_grad[:, :local]]),
        vo_grad[:, local:].T,
        inner_scatter(up_grad, 0),
        inner_scatter(down_grad, 0).T,
        norms[:2],
        norms[2:],
        gate_grad * gate_part * (1.0 - gate_part),
    )


def solution(mesh):
    rows = P(None, ("dp", "head"), None)
    gates = P("head", "dp", None)
    weights = (P(None, "dp", "head"), P("head", "dp"), P("dp", "head"), P("head", "dp"))
    return jax.shard_map(
        per_device,
        mesh=mesh,
        in_specs=(rows, rows, P(None, "dp")) + weights + (P(), P(), gates, gates),
        out_specs=(rows, rows) + weights + (P(), P(), gates),
        check_vma=False,
    )
```

```python
import functools, math
import jax, jax.numpy as jnp
from jax import lax
from jax.experimental import pallas as pl
from jax.experimental.pallas import tpu as pltpu
from jax.sharding import PartitionSpec as P

HEAD_DIM = 64
EPS = 1e-05
F32 = jnp.float32
BF16 = jnp.bfloat16
GP = jnp.bfloat16
SCALE = 1.0 / math.sqrt(HEAD_DIM)
LOG2E = math.log2(math.e)
NEG = -1e30
INV_SQRT2 = 1.0 / math.sqrt(2.0)
INV_SQRT2PI = 1.0 / math.sqrt(2.0 * math.pi)


def dot_nn(a, b):
    return lax.dot_general(a, b, (((1,), (0,)), ((), ())), preferred_element_type=F32)


def dot_nt(a, b):
    return lax.dot_general(a, b, (((1,), (1,)), ((), ())), preferred_element_type=F32)


def dot_tn(a, b):
    return lax.dot_general(a, b, (((0,), (0,)), ((), ())), preferred_element_type=F32)


def piece(ref, bits, d, flip):
    y = bits[0] ^ (d & 1)
    z1 = bits[1] ^ ((d >> 1) & 1)
    z2 = bits[2] ^ ((d >> 2) & 1)
    if flip:
        return ref.at[y, 0, z1, z2]
    return ref.at[0, y, z1, z2]


def assemble(dst, ref, bits, flip, cols=None):
    rows = ref.shape[-2]
    cols = pl.ds(0, ref.shape[-1]) if cols is None else cols
    for d in range(8):
        dst[pl.ds(d * rows, rows), cols] = piece(ref, bits, d, flip)[...]


def scatter(ref, src, bits, flip):
    rows = ref.shape[-2]
    for d in range(8):
        piece(ref, bits, d, flip)[...] = src[pl.ds(d * rows, rows), :]


def own(bits, y, z1, z2):
    return (bits[0] ^ y) + 2 * (bits[1] ^ z1) + 4 * (bits[2] ^ z2)


RELATIVE = [(y, z1, z2) for y in range(2) for z1 in range(2) for z2 in range(2)]


def spec_a(tail, pick):
    zeros = (0,) * len(tail)
    return pl.BlockSpec((1, 2, 2, 2) + tail, lambda k, *_: (pick(k), 0, 0, 0) + zeros)


def spec_b(tail, pick):
    zeros = (0,) * len(tail)
    return pl.BlockSpec((2, 1, 2, 2) + tail, lambda k, *_: (0, pick(k), 0, 0) + zeros)


def whole(shape):
    zeros = (0,) * len(shape)
    return pl.BlockSpec(shape, lambda *_: zeros, pipeline_mode=pl.Buffered(1))


def low_pick(k):
    return jnp.minimum(k, 1)


def high_pick(k):
    return jnp.maximum(k - 2, 0)


def norm_stats(z):
    mean = jnp.mean(z, axis=1, keepdims=True)
    centered = z - mean
    inverse = lax.rsqrt(jnp.mean(centered * centered, axis=1, keepdims=True) + EPS)
    return centered * inverse, inverse


def norm_back(du, unit, inverse):
    return inverse * (
        du
        - jnp.mean(du, axis=1, keepdims=True)
        - unit * jnp.mean(du * unit, axis=1, keepdims=True)
    )


def gelu_pair(up):
    cdf = 0.5 + 0.5 * lax.erf(up * INV_SQRT2)
    pdf = INV_SQRT2PI * jnp.exp(-0.5 * (up * up))
    return up * cdf, cdf + up * pdf


SHARE = 10


def cost(flops, moved):
    return pl.CostEstimate(flops=flops * SHARE, bytes_accessed=moved * SHARE, transcendentals=0)


def params(mib=60, n=1):
    return pltpu.CompilerParams(
        dimension_semantics=("arbitrary",) * n, vmem_limit_bytes=mib * 1024 * 1024
    )


def load_pair(k, bits, wu, wd, ua0, ua1, db0, db1):
    @pl.when(k < 2)
    def _():
        assemble(wu, ua0, bits, False)
        assemble(wd, db0, bits, True)

    @pl.when(k >= 2)
    def _():
        assemble(wu, ua1, bits, False)
        assemble(wd, db1, bits, True)


def ffn_units(chunk, hid, wu, wd, act_o, gp_o, acc, finish=None):
    rows = hid.shape[0]
    ats = [pl.ds(r * chunk, chunk) for r in range(rows // chunk)]
    ahead = dot_nn(hid[ats[0], :], wu[...])
    for r, at in enumerate(ats):
        act, gp = gelu_pair(ahead)
        if r + 1 < len(ats):
            ahead = dot_nn(hid[ats[r + 1], :], wu[...])
        act = act.astype(BF16)
        act_o[0, at, :] = act
        gp_o[0, at, :] = gp.astype(gp_o.dtype)
        acc[at, :] += dot_nt(act, wd[...])
        if finish is not None:
            finish(r * chunk, chunk)


def ffn_part_kernel(chunk, bits, hid, ua0, ua1, db0, db1, act_o, gp_o, acc, wu, wd):
    k = pl.program_id(0)
    load_pair(k, bits, wu, wd, ua0, ua1, db0, db1)

    @pl.when(k == 0)
    def _():
        acc[...] = hid[...].astype(F32)

    ffn_units(chunk, hid, wu, wd, act_o, gp_o, acc)


def ffn_part(bits, hid, ua0, ua1, db0, db1, chunk=512):
    rows, width = hid.shape
    p, n = ua0.shape[-2:]
    sds = jax.ShapeDtypeStruct
    col = pl.BlockSpec((1, rows, n), lambda k, *_: (k, 0, 0))
    return pl.pallas_call(
        functools.partial(ffn_part_kernel, chunk),
        out_shape=(pltpu.HBM((4, rows, n), BF16), pltpu.HBM((4, rows, n), GP), sds((rows, width), F32)),
        grid_spec=pltpu.PrefetchScalarGridSpec(
            num_scalar_prefetch=1, grid=(4,),
            in_specs=[whole((rows, width)), spec_a((p, n), low_pick), spec_a((p, n), high_pick),
                      spec_b((p, n), low_pick), spec_b((p, n), high_pick)],
            out_specs=[col, col, whole((rows, width))],
            scratch_shapes=[pltpu.VMEM((width, n), BF16), pltpu.VMEM((width, n), BF16)],
        ),
        compiler_params=params(26),
        cost_estimate=cost(4 * rows * width * 4 * n, 16 * rows * width),
    )(bits, hid, ua0, ua1, db0, db1)


def ffn_rest_kernel(chunk, bits, lens, hid, ua0, ua1, db0, db1, part, gain, bias, dout,
                    act_o, gp_o, out, acc, dffn, dffnt, dgain, dbias, wu, wd):
    k = pl.program_id(0)
    rows = hid.shape[0]
    load_pair(k, bits, wu, wd, ua0, ua1, db0, db1)

    @pl.when(k == 0)
    def _():
        acc[...] = part[...]

    @pl.when(k < 3)
    def _():
        ffn_units(chunk, hid, wu, wd, act_o, gp_o, acc)

    @pl.when(k == 3)
    def _():
        length = rows // lens.shape[0]
        small = 256
        g = gain[...]
        b = bias[...]
        sums = [jnp.zeros_like(g), jnp.zeros_like(g)]

        def finish(start, count):
            for at0 in range(start, start + count, small):
                at = pl.ds(at0, small)
                size = lens[at0 // length]
                pos = (at0 % length) + lax.broadcasted_iota(jnp.int32, (small, 1), 0)
                valid = pos < size
                unit, inverse = norm_stats(acc[at, :])
                out[at, :] = jnp.where(valid, unit * g + b, 0.0).astype(BF16)
                dy = jnp.where(valid, dout[at, :].astype(F32), 0.0)
                sums[0] = sums[0] + jnp.sum(dy * unit, axis=0, keepdims=True)
                sums[1] = sums[1] + jnp.sum(dy, axis=0, keepdims=True)
                dz = norm_back(dy * g, unit, inverse)
                acc[at, :] = dz
                low = dz.astype(BF16)
                dffn[at, :] = low
                dffnt[:, at] = low.T

        ffn_units(chunk, hid, wu, wd, act_o, gp_o, acc, finish)
        dgain[...] = sums[0]
        dbias[...] = sums[1]


def ffn_rest(bits, lens, hid, ua0, ua1, db0, db1, part, gain, bias, dout, chunk=512):
    rows, width = hid.shape
    p, n = ua0.shape[-2:]
    sds = jax.ShapeDtypeStruct
    full = whole((rows, width))
    line = whole((1, width))
    col = pl.BlockSpec((1, rows, n), lambda k, *_: (k, 0, 0))
    return pl.pallas_call(
        functools.partial(ffn_rest_kernel, chunk),
        out_shape=(sds((4, rows, n), BF16), sds((4, rows, n), GP), sds((rows, width), BF16), sds((rows, width), F32),
                   sds((rows, width), BF16), sds((width, rows), BF16), sds((1, width), F32), sds((1, width), F32)),
        grid_spec=pltpu.PrefetchScalarGridSpec(
            num_scalar_prefetch=2, grid=(4,),
            in_specs=[full, spec_a((p, n), low_pick), spec_a((p, n), high_pick),
                      spec_b((p, n), low_pick), spec_b((p, n), high_pick), full, line, line, full],
            out_specs=[col, col, full, full, full, whole((width, rows)), line, line],
            scratch_shapes=[pltpu.VMEM((width, n), BF16), pltpu.VMEM((width, n), BF16)],
        ),
        compiler_params=params(30),
        cost_estimate=cost(4 * rows * width * 4 * n, 20 * rows * width),
    )(bits, lens, hid, ua0, ua1, db0, db1, part, gain, bias, dout)


def down_grad_kernel(bits, dt, actp, actq, keep, send):
    k = pl.program_id(0)
    first = dot_nn(dt[...], actp[0]).astype(BF16)
    second = dot_nn(dt[...], actq[0]).astype(BF16)
    rows = keep.shape[-2]
    n = actp.shape[2]

    def put(ref):
        for d in range(8):
            at = piece(ref, bits, d, True)
            at[:, pl.ds(0, n)] = first[d * rows : (d + 1) * rows]
            at[:, pl.ds(n, actq.shape[2])] = second[d * rows : (d + 1) * rows]

    @pl.when(k < 2)
    def _():
        put(keep)

    @pl.when(k >= 2)
    def _():
        put(send)


def down_grads(bits, dt, actp, actq):
    width, rows = dt.shape
    col = lambda a: pl.BlockSpec((1, rows, a.shape[2]), lambda k, *_: (k, 0, 0))
    n = actp.shape[2] + actq.shape[2]
    p = width // 8
    sds = jax.ShapeDtypeStruct
    return pl.pallas_call(
        down_grad_kernel,
        out_shape=(sds((2, 2, 2, 2, p, n), BF16), sds((2, 2, 2, 2, p, n), BF16)),
        grid_spec=pltpu.PrefetchScalarGridSpec(
            num_scalar_prefetch=1, grid=(4,),
            in_specs=[whole((width, rows)), col(actp), col(actq)],
            out_specs=[spec_b((p, n), low_pick), spec_b((p, n), high_pick)],
        ),
        compiler_params=params(22),
        cost_estimate=cost(2 * rows * width * 4 * n, 14 * rows * width),
    )(bits, dt, actp, actq)


def ffn_bwd_kernel(chunk, last, bits, ht, dffn, uap, uaq, dbp, dbq, gpp, gpq, *rest):
    if last:
        dsec, part, unit, inverse, gain, gu, acc, dattn, dattnt, dgain, dbias, wu, wd, dup_s = rest
    else:
        gu, acc, wu, wd, dup_s = rest
    k = pl.program_id(0)
    rows, width = dffn.shape
    np = uap.shape[-1]
    left, right = pl.ds(0, np), pl.ds(np, uaq.shape[-1])

    assemble(wu, uap, bits, False, left)
    assemble(wu, uaq, bits, False, right)
    assemble(wd, dbp, bits, True, left)
    assemble(wd, dbq, bits, True, right)

    @pl.when(k == 0)
    def _():
        if last:
            acc[...] = part[...] + dsec[...]
        else:
            acc[...] = jnp.zeros_like(acc)

    def run(finish=None):
        ats = [pl.ds(r * chunk, chunk) for r in range(rows // chunk)]
        ahead = dot_nn(dffn[ats[0], :], wd[...])
        for r, at in enumerate(ats):
            dup_s[at, left] = (ahead[:, :np] * gpp[0, at, :].astype(F32)).astype(BF16)
            dup_s[at, right] = (ahead[:, np:] * gpq[0, at, :].astype(F32)).astype(BF16)
            if r + 1 < len(ats):
                ahead = dot_nn(dffn[ats[r + 1], :], wd[...])
            acc[at, :] += dot_nt(dup_s[at, :], wu[...])
            if finish is not None:
                finish(r * chunk, chunk)
        grad = dot_nn(ht[...], dup_s[...]).astype(BF16)
        p = gu.shape[-2]
        for d in range(8):
            piece(gu, bits, d, False)[...] = grad[d * p : (d + 1) * p]

    if not last:
        run()
        return

    @pl.when(k == 0)
    def _():
        run()

    @pl.when(k == 1)
    def _():
        small = 256
        g = gain[...]
        sums = [jnp.zeros_like(g), jnp.zeros_like(g)]

        def finish(start, count):
            for at0 in range(start, start + count, small):
                at = pl.ds(at0, small)
                dh = acc[at, :]
                u = unit[at, :]
                sums[0] = sums[0] + jnp.sum(dh * u, axis=0, keepdims=True)
                sums[1] = sums[1] + jnp.sum(dh, axis=0, keepdims=True)
                dz = norm_back(dh * g, u, inverse[at, :])
                acc[at, :] = dz
                low = dz.astype(BF16)
                dattn[at, :] = low
                dattnt[:, at] = low.T

        run(finish)
        dgain[...] = sums[0]
        dbias[...] = sums[1]


def ffn_backward(last, bits, ht, dffn, uap, uaq, dbp, dbq, gpp, gpq, extra=(), chunk=512):
    rows, width = dffn.shape
    p, np = uap.shape[-2:]
    nq = uaq.shape[-1]
    n = np + nq
    sds = jax.ShapeDtypeStruct
    off = 0 if last else 2
    pick = lambda k: k
    full = whole((rows, width))
    line = whole((1, width))
    out_shape = [sds((2, 2, 2, 2, p, n), BF16)]
    out_specs = [spec_a((p, n), pick)]
    in_specs = [
        whole((width, rows)), full,
        spec_a((p, np), pick), spec_a((p, nq), pick), spec_b((p, np), pick), spec_b((p, nq), pick),
        pl.BlockSpec((1, rows, np), lambda k, *_: (k + off, 0, 0)),
        pl.BlockSpec((1, rows, nq), lambda k, *_: (k + off, 0, 0)),
    ]
    scratch = [pltpu.VMEM((width, n), BF16), pltpu.VMEM((width, n), BF16), pltpu.VMEM((rows, n), BF16)]
    if last:
        in_specs += [full] * 3 + [whole((rows, 1)), line]
        out_shape += [sds((rows, width), F32), sds((rows, width), BF16), sds((width, rows), BF16), sds((1, width), F32), sds((1, width), F32)]
        out_specs += [full, full, whole((width, rows)), line, line]
    else:
        out_shape += [sds((rows, width), F32)]
        out_specs += [full]
    return pl.pallas_call(
        functools.partial(ffn_bwd_kernel, chunk, last),
        out_shape=out_shape,
        grid_spec=pltpu.PrefetchScalarGridSpec(
            num_scalar_prefetch=1, grid=(2,), in_specs=in_specs, out_specs=out_specs, scratch_shapes=scratch,
        ),
        compiler_params=params(36),
        cost_estimate=cost(6 * rows * width * 2 * n, 30 * rows * width),
    )(bits, ht, dffn, uap, uaq, dbp, dbq, gpp, gpq, *extra)


def key_bias(size, length):
    pos = lax.broadcasted_iota(jnp.int32, (1, length), 1)
    return jnp.where(pos < size, 0.0, NEG).astype(F32)


def gate_rows(ga, gb, bits, i, d0, count):
    parts = []
    for j in range(count):
        d = d0 + j
        y = bits[0] ^ (d & 1)
        z1 = bits[1] ^ ((d >> 1) & 1)
        z2 = bits[2] ^ ((d >> 2) & 1)
        parts.append(ga[0, y, z1, z2, i])
        parts.append(gb[y, 0, z1, z2, i])
    return jnp.concatenate(parts, axis=0).astype(F32)


def att_fwd_kernel(bits, lens, qk, v, ga, gb, mixed, lse):
    length = qk.shape[1]
    heads = v.shape[2] // HEAD_DIM
    bias = key_bias(lens[pl.program_id(1)], length)
    count = length // (2 * ga.shape[-2])
    cols = [pl.ds(i * HEAD_DIM, HEAD_DIM) for i in range(2 * heads)]

    def score(i):
        return dot_nt(qk[0, :, cols[i]], qk[0, :, cols[heads + i]])

    ahead = score(0)
    outs = []
    stats = []
    for i in range(heads):
        s = ahead * (SCALE * LOG2E) + bias
        if i + 1 < heads:
            ahead = score(i + 1)
        top = jnp.max(s, axis=1, keepdims=True)
        e = jnp.exp2(s - top)
        total = jnp.sum(e, axis=1, keepdims=True)
        w = (e * gate_rows(ga, gb, bits, i, 0, count)).astype(BF16)
        outs.append(dot_nn(w, v[0, :, cols[i]]) * (1.0 / total))
        stats.append(top + jnp.log2(total))
    mixed[0] = jnp.concatenate(outs, axis=1).astype(BF16)
    lse[0] = jnp.concatenate(stats, axis=1)


def attention_forward(bits, lens, qk, v, ga, gb):
    _, rows, w2 = qk.shape
    w1 = v.shape[2]
    count = lens.shape[0]
    length = rows // count
    heads, sub, keys = ga.shape[-3:]
    sds = jax.ShapeDtypeStruct
    return pl.pallas_call(
        att_fwd_kernel,
        out_shape=(sds((2, rows, w1), BF16), sds((2, rows, heads), F32)),
        grid_spec=pltpu.PrefetchScalarGridSpec(
            num_scalar_prefetch=2, grid=(2, count),
            in_specs=[
                pl.BlockSpec((1, length, w2), lambda k, s, *_: (k, s, 0)),
                pl.BlockSpec((1, length, w1), lambda k, s, *_: (k, s, 0)),
                spec_a((heads, sub, keys), lambda k: k), spec_b((heads, sub, keys), lambda k: k),
            ],
            out_specs=[
                pl.BlockSpec((1, length, w1), lambda k, s, *_: (k, s, 0)),
                pl.BlockSpec((1, length, heads), lambda k, s, *_: (k, s, 0)),
            ],
        ),
        compiler_params=params(22, 2),
        cost_estimate=cost(16 * 2 * rows * length * w1, 16 * rows * w1),
    )(bits, lens, qk, v, ga, gb)


def att_bwd_kernel(last, bits, lens, qk, v, ga, gb, lse, dattn, wo, *rest):
    if last:
        ra, rb, dqk, dv, a_keep, a_send, b_keep, b_send, dm_s, dmt, qt, acc = rest
    else:
        dqk, dv, oga, ogb, dm_s, dmt, qt, acc = rest
    length = qk.shape[1]
    heads = v.shape[2] // HEAD_DIM
    hw = heads * HEAD_DIM
    k = pl.program_id(0)
    seq = pl.program_id(1)
    bias = key_bias(lens[seq], length)
    sub = ga.shape[-2]
    count = length // (2 * sub)
    cols = [pl.ds(i * HEAD_DIM, HEAD_DIM) for i in range(2 * heads)]

    dm = dot_nn(dattn[...], wo[0]).astype(BF16)
    dm_s[...] = dm
    dmt[...] = dm.T
    qt[...] = qk[0, :, pl.ds(0, hw)].T

    def products(i):
        return (
            dot_nt(qk[0, :, cols[i]], qk[0, :, cols[heads + i]]),
            dot_nt(dm_s[:, cols[i]], v[0, :, cols[i]]),
        )

    ahead = products(0)
    dqs, dks, dvs = [], [], []
    for i in range(heads):
        s, dw = ahead
        p = jnp.exp2(s * (SCALE * LOG2E) + bias - lse[0, :, pl.ds(i, 1)])
        if i + 1 < heads:
            ahead = products(i + 1)
        g = gate_rows(ga, gb, bits, i, 0, count)
        w = (p * g).astype(BF16)
        t = dw * p
        acc[i] = t + jnp.where(seq == 0, 0.0, acc[i])
        u = t * g
        ds = (u - p * jnp.sum(u, axis=1, keepdims=True)).astype(BF16)
        dqs.append(dot_nn(ds, qk[0, :, cols[heads + i]]) * SCALE)
        dvs.append(dot_nn(dmt[cols[i], :], w).astype(BF16).T)
        dks.append((dot_nn(qt[cols[i], :], ds) * SCALE).astype(BF16).T)
    dqk[0] = jnp.concatenate([d.astype(BF16) for d in dqs] + dks, axis=1)
    dv[0] = jnp.concatenate(dvs, axis=1)

    def first_rows(y, z1, z2):
        return pl.ds(pl.multiple_of(own(bits, y, z1, z2) * 2 * sub, sub), sub)

    def second_rows(y, z1, z2):
        return pl.ds(pl.multiple_of(own(bits, y, z1, z2) * 2 * sub + sub, sub), sub)

    @pl.when(seq == pl.num_programs(1) - 1)
    def _():
        if not last:
            for r in RELATIVE:
                for i in range(heads):
                    oga[(0,) + r + (i,)] = acc[i, first_rows(*r), :].astype(BF16)
                    ogb[(r[0], 0) + r[1:] + (i,)] = acc[i, second_rows(*r), :].astype(BF16)
            return

        def put_a(ref):
            for r in RELATIVE:
                for i in range(heads):
                    ref[r + (i,)] = (acc[i, first_rows(*r), :] + ra[(0,) + r + (i,)].astype(F32)).astype(BF16)

        @pl.when(k == 0)
        def _():
            put_a(a_keep)

        @pl.when(k == 1)
        def _():
            put_a(a_send)

        for r in RELATIVE:
            ref = b_send if r[0] else b_keep
            for i in range(heads):
                ref[(0,) + r[1:] + (i,)] = (
                    acc[i, second_rows(*r), :] + rb[(r[0], 0) + r[1:] + (i,)].astype(F32)
                ).astype(BF16)


def attention_backward(last, bits, lens, qk, v, ga, gb, lse, dattn, wo, got=()):
    _, rows, w2 = qk.shape
    w1 = v.shape[2]
    width = dattn.shape[1]
    count = lens.shape[0]
    length = rows // count
    tail = ga.shape[-3:]
    heads, sub, keys = tail
    sds = jax.ShapeDtypeStruct
    pick = lambda k: k
    in_specs = [
        pl.BlockSpec((1, length, w2), lambda k, s, *_: (k, s, 0)),
        pl.BlockSpec((1, length, w1), lambda k, s, *_: (k, s, 0)),
        spec_a(tail, pick), spec_b(tail, pick),
        pl.BlockSpec((1, length, heads), lambda k, s, *_: (k, s, 0)),
        pl.BlockSpec((length, width), lambda k, s, *_: (s, 0)),
        pl.BlockSpec((1, width, w1), lambda k, s, *_: (k, 0, 0)),
    ]
    out_shape = [sds((2, rows, w2), BF16), sds((2, rows, w1), BF16)]
    out_specs = [
        pl.BlockSpec((1, length, w2), lambda k, s, *_: (k, s, 0)),
        pl.BlockSpec((1, length, w1), lambda k, s, *_: (k, s, 0)),
    ]
    if last:
        in_specs += [spec_a(tail, pick), spec_b(tail, pick)]
        out_shape += [sds((2, 2, 2) + tail, BF16)] * 4
        out_specs += [whole((2, 2, 2) + tail)] * 2 + [
            pl.BlockSpec((1, 2, 2) + tail, lambda k, *_: (k, 0, 0, 0, 0, 0))
        ] * 2
    else:
        out_shape += [sds((2, 2, 2, 2) + tail, BF16)] * 2
        out_specs += [spec_a(tail, pick), spec_b(tail, pick)]
    return pl.pallas_call(
        functools.partial(att_bwd_kernel, last),
        out_shape=out_shape,
        grid_spec=pltpu.PrefetchScalarGridSpec(
            num_scalar_prefetch=2, grid=(2, count), in_specs=in_specs, out_specs=out_specs,
            scratch_shapes=[
                pltpu.VMEM((length, w1), BF16), pltpu.VMEM((w1, length), BF16),
                pltpu.VMEM((w1, length), BF16), pltpu.VMEM((heads, length, keys), F32),
            ],
        ),
        compiler_params=params(30, 2),
        cost_estimate=cost(40 * 2 * rows * length * w1, 30 * rows * w1),
    )(bits, lens, qk, v, ga, gb, lse, dattn, wo, *got)


def qkv_kernel(first, bits, x, wa, wb, qk, v, wqk, wv, wo, *rest):
    w1 = v.shape[2]
    wb_s = rest[-1]
    assemble(wqk.at[0], wa, bits, False)
    assemble(wb_s, wb, bits, True)

    if first:

        @pl.when(pl.program_id(0) == 0)
        def _():
            rest[0][...] = x[...].T

    wv[0] = wb_s[:, pl.ds(0, w1)]
    wo[0] = wb_s[:, pl.ds(w1, w1)]
    qk[0] = dot_nn(x[...], wqk[0]).astype(BF16)
    v[0] = dot_nn(x[...], wv[0]).astype(BF16)


def project(first, bits, x, wa, wb):
    rows, width = x.shape
    p, w2 = wa.shape[-2:]
    w1 = w2 // 2
    sds = jax.ShapeDtypeStruct
    pick = lambda k: k
    head = lambda s: pl.BlockSpec((1,) + s, lambda k, *_: (k, 0, 0))
    return pl.pallas_call(
        functools.partial(qkv_kernel, first),
        out_shape=[sds((2, rows, w2), BF16), sds((2, rows, w1), BF16), pltpu.HBM((2, width, w2), BF16),
                   pltpu.HBM((2, width, w1), BF16), sds((2, width, w1), BF16)]
        + ([pltpu.HBM((width, rows), BF16)] if first else []),
        grid_spec=pltpu.PrefetchScalarGridSpec(
            num_scalar_prefetch=1, grid=(2,),
            in_specs=[whole((rows, width)), spec_a((p, w2), pick), spec_b((p, w2), pick)],
            out_specs=[head((rows, w2)), head((rows, w1)), head((width, w2)), head((width, w1)), head((width, w1))]
            + ([whole((width, rows))] if first else []),
            scratch_shapes=[pltpu.VMEM((width, w2), BF16)],
        ),
        compiler_params=params(24),
        cost_estimate=cost(2 * rows * width * 2 * (w1 + w2), 8 * rows * width),
    )(bits, x, wa, wb)


def out_kernel(x, m0, m1, wo0, wo1, gain, bias, hid, unit, inverse, hidt):
    attn = dot_nt(m0[0], wo0[0]) + dot_nt(m0[1], wo0[1]) + dot_nt(m1[0], wo1[0]) + dot_nt(m1[1], wo1[1])
    u, inv = norm_stats(x[...].astype(F32) + attn)
    h = (u * gain[...] + bias[...]).astype(BF16)
    hid[...] = h
    hidt[...] = h.T
    unit[...] = u
    inverse[...] = inv


def out_forward(x, m0, m1, wo0, wo1, gain, bias, block=256):
    rows, width = x.shape
    w1 = wo0.shape[2]
    sds = jax.ShapeDtypeStruct
    row = lambda w: pl.BlockSpec((block, w), lambda r: (r, 0))
    mix = pl.BlockSpec((2, block, w1), lambda r: (0, r, 0))
    return pl.pallas_call(
        out_kernel,
        grid=(rows // block,),
        out_shape=(sds((rows, width), BF16), pltpu.HBM((rows, width), F32), sds((rows, 1), F32), pltpu.HBM((width, rows), BF16)),
        in_specs=[row(width), mix, mix, whole((2, width, w1)), whole((2, width, w1)), whole((1, width)), whole((1, width))],
        out_specs=[row(width), row(width), row(1), pl.BlockSpec((width, block), lambda r: (0, r))],
        compiler_params=params(20),
        cost_estimate=cost(2 * rows * width * 4 * w1, 12 * rows * width),
    )(x, m0, m1, wo0, wo1, gain, bias)


def qkv_grad_kernel(last, bits, xt, dat, dqk, dv, mixed, *rest):
    if last:
        ra, rb, a_keep, a_send, b_keep, b_send, ta, tb = rest
    else:
        ga, gb, ta, tb = rest
    w1 = dv.shape[2]
    k = pl.program_id(0)
    ta[...] = dot_nn(xt[...], dqk[0]).astype(ta.dtype)
    tb[:, pl.ds(0, w1)] = dot_nn(xt[...], dv[0]).astype(tb.dtype)
    tb[:, pl.ds(w1, w1)] = dot_nn(dat[...], mixed[0]).astype(tb.dtype)
    if not last:
        scatter(ga, ta, bits, False)
        scatter(gb, tb, bits, True)
        return
    p = ra.shape[-2]

    def rows(r):
        return pl.ds(pl.multiple_of(own(bits, *r) * p, 16), p)

    def put_a(ref):
        for r in RELATIVE:
            ref[r] = (ta[rows(r), :] + ra[(0,) + r].astype(F32)).astype(BF16)

    @pl.when(k == 0)
    def _():
        put_a(a_keep)

    @pl.when(k == 1)
    def _():
        put_a(a_send)

    for r in RELATIVE:
        ref = b_send if r[0] else b_keep
        ref[(0,) + r[1:]] = (tb[rows(r), :] + rb[(r[0], 0) + r[1:]].astype(F32)).astype(BF16)


def qkv_grads(last, bits, xt, dat, dqk, dv, mixed, got=()):
    width, rows = xt.shape
    w2 = dqk.shape[2]
    w1 = dv.shape[2]
    per = width // 8
    sds = jax.ShapeDtypeStruct
    pick = lambda k: k
    head = lambda w: pl.BlockSpec((1, rows, w), lambda k, *_: (k, 0, 0))
    in_specs = [whole((width, rows)), whole((width, rows)), head(w2), head(w1), head(w1)]
    if last:
        in_specs += [spec_a((per, w2), pick), spec_b((per, w2), pick)]
        out_shape = [sds((2, 2, 2, per, w2), BF16)] * 4
        out_specs = [whole((2, 2, 2, per, w2))] * 2 + [
            pl.BlockSpec((1, 2, 2, per, w2), lambda k, *_: (k, 0, 0, 0, 0))
        ] * 2
    else:
        out_shape = [sds((2, 2, 2, 2, per, w2), BF16)] * 2
        out_specs = [spec_a((per, w2), pick), spec_b((per, w2), pick)]
    kind = F32 if last else BF16
    return pl.pallas_call(
        functools.partial(qkv_grad_kernel, last),
        out_shape=out_shape,
        grid_spec=pltpu.PrefetchScalarGridSpec(
            num_scalar_prefetch=1, grid=(2,), in_specs=in_specs, out_specs=out_specs,
            scratch_shapes=[pltpu.VMEM((width, w2), kind), pltpu.VMEM((width, w2), kind)],
        ),
        compiler_params=params(26),
        cost_estimate=cost(1 if last else 8 * rows * width * w2, 1 if last else 8 * rows * width),
    )(bits, xt, dat, dqk, dv, mixed, *got)


def dinput_kernel(dfirst, dqk0, dqk1, dv0, dv1, wqk0, wqk1, wv0, wv1, out):
    total = dfirst[...]
    for a, b, wa, wb in ((dqk0, dv0, wqk0, wv0), (dqk1, dv1, wqk1, wv1)):
        for k in range(2):
            total = total + dot_nt(a[k], wa[k]) + dot_nt(b[k], wb[k])
    out[...] = total


def input_backward(dfirst, dqk0, dqk1, dv0, dv1, wqk0, wqk1, wv0, wv1, block=256):
    rows, width = dfirst.shape
    w2 = wqk0.shape[2]
    w1 = wv0.shape[2]
    row = pl.BlockSpec((block, width), lambda r: (r, 0))
    part = lambda w: pl.BlockSpec((2, block, w), lambda r: (0, r, 0))
    return pl.pallas_call(
        dinput_kernel,
        grid=(rows // block,),
        out_shape=jax.ShapeDtypeStruct((rows, width), F32),
        in_specs=[row, part(w2), part(w2), part(w1), part(w1)]
        + [whole((2, width, w2))] * 2 + [whole((2, width, w1))] * 2,
        out_specs=row,
        compiler_params=params(24),
        cost_estimate=cost(2 * rows * width * 4 * (w1 + w2), 14 * rows * width),
    )(dfirst, dqk0, dqk1, dv0, dv1, wqk0, wqk1, wv0, wv1)


GROUPS = 8


def partner_dp(value, bit):
    size = lax.axis_size("dp")
    step = (1 << bit) * (size // GROUPS)
    return lax.ppermute(value, "dp", [(i, i ^ step) for i in range(size)])


def partner_head(value, bit):
    size = lax.axis_size("head")
    return lax.ppermute(value, "head", [(i, i ^ (1 << bit)) for i in range(size)])


def over_y(value):
    return partner_dp(value, 0)


def over_near(value):
    return partner_dp(value, 1)


def over_far(value):
    return partner_dp(value, 2)


def over_pair(value):
    return partner_head(value, 0)


def over_x(value):
    return partner_head(value, 1)


def inner_groups():
    inner = lax.axis_size("dp") // GROUPS
    return inner, [[g * inner + i for i in range(inner)] for g in range(GROUPS)]


def inner_gather(value, axis):
    inner, groups = inner_groups()
    if inner == 1:
        return value
    return lax.all_gather(value, "dp", axis_index_groups=groups, axis=axis, tiled=True)


def inner_scatter(value, axis):
    inner, groups = inner_groups()
    if inner == 1:
        return value
    return lax.psum_scatter(value, "dp", axis_index_groups=groups, scatter_dimension=axis, tiled=True)


def after(values, *waits):
    return lax.optimization_barrier((tuple(values), waits))[0]


def wide(value):
    return value.astype(F32)


def first_sum(keep, got):
    return (wide(keep[1]) + wide(got[1])).astype(BF16)


def second_sum(keep, got, more):
    return (wide(keep[0, 1]) + wide(got[0, 1]) + wide(more[1])).astype(BF16)


def third_sum(keep, got, more, last):
    return wide(keep[0, 0]) + wide(got[0, 0]) + wide(more[0]) + wide(last)


def low_sum(keep, got):
    return (wide(keep[1]) + wide(got[1])).astype(BF16)


def high_sum(keep, got, more):
    return wide(keep[0]) + wide(got[0]) + wide(more)


def total_steps():
    steps = []
    for name in ("head", "dp"):
        size = lax.axis_size(name)
        step = 1
        while step < size:
            steps.append((name, [(i, i ^ step) for i in range(size)]))
            step *= 2
    return steps


def total_some(value, *steps):
    for name, pairs in steps:
        value = value + lax.ppermute(value, name, pairs)
    return value


def per_device(layer_input, output_grad, lengths, w_qkv, w_out, w_up, w_down,
               norm_gains, norm_biases, mask_logits, mask_noise):
    micro, seq, width = layer_input.shape
    rows = micro * seq
    x = layer_input.reshape(rows, width)
    dout = output_grad.reshape(rows, width)
    place = lax.axis_index("dp") // (lax.axis_size("dp") // GROUPS)
    bits = jnp.stack([place & 1, (place >> 1) & 1, (place >> 2) & 1]).astype(jnp.int32)
    lens = lax.dynamic_slice_in_dim(lengths, lax.axis_index("head"), 1, 1).reshape(micro)

    gate_part = jax.nn.sigmoid(mask_logits + mask_noise)
    gate_all = inner_gather(gate_part.astype(BF16), 1)
    sub = gate_all.shape[1] // 2
    gain1, gain2 = norm_gains[0:1], norm_gains[1:2]
    bias1, bias2 = norm_biases[0:1], norm_biases[1:2]

    ga = jnp.stack([
        inner_gather(jnp.concatenate([w_qkv[0], w_qkv[1]], axis=1), 0),
        inner_gather(jnp.concatenate([w_qkv[2], w_out.T], axis=1), 0),
    ])
    gb = jnp.stack([gate_all[:, :sub], gate_all[:, sub:]])
    up_all, down_all = inner_gather(w_up, 0), inner_gather(w_down.T, 0)
    units = up_all.shape[1]
    most = units * 2 // 3
    gc = jnp.stack([up_all[:, :most], down_all[:, :most]])
    ge = jnp.stack([up_all[:, most:], down_all[:, most:]])

    got = over_far(ga)
    ga = jnp.stack([ga, got], axis=1)
    got = over_near(ga)
    ga = jnp.stack([ga, got], axis=1)
    aa, ab = ga[0], ga[1]
    (gb,) = after((gb,), got)
    ra, rb = over_y(aa), over_x(ab)
    far_b = over_far(gb)
    aa, ab = jnp.stack([aa, ra]), jnp.stack([ab, rb])
    gb, = after((gb,), ra, rb)
    gb = jnp.stack([gb, far_b], axis=1)
    aa, ab = after((aa, ab), gb)
    ra, rb = over_x(aa), over_y(ab)
    near_b = over_near(gb)
    (gc,) = after((gc,), near_b)
    far_c = over_far(gc)
    gb = jnp.stack([gb, near_b], axis=1)
    ba, bb = gb[0], gb[1]
    aa, ab = jnp.stack([aa, ra]), jnp.stack([ab, rb])
    ba, bb = after((ba, bb), ra, rb)
    ca, cb = over_pair(aa), over_pair(ab)
    ra, rb = over_y(ba), over_x(bb)
    qk0, v0, wqk0, wv0, wo0, xt = project(True, bits, x, aa, ab)
    ba, bb = jnp.stack([ba, ra]), jnp.stack([bb, rb])
    ba, bb, gc, ca, cb = after((ba, bb, gc, ca, cb), qk0, ra, rb)
    ra, rb = over_x(ba), over_y(bb)
    gc = jnp.stack([gc, far_c], axis=1)
    near_c = over_near(gc)
    qk1, v1, wqk1, wv1, wo1 = project(False, bits, x, ca, cb)
    ba, bb = jnp.stack([ba, ra]), jnp.stack([bb, rb])
    gc = jnp.stack([gc, near_c], axis=1)
    fa, fb = gc[0], gc[1]
    fa, fb, ba, bb, ge = after((fa, fb, ba, bb, ge), ra, rb, near_c, qk1)
    ba1, bb1 = over_pair(ba), over_pair(bb)
    ra, rb = over_y(fa), over_x(fb)
    far_e = over_far(ge)
    m0, lse0 = attention_forward(bits, lens, qk0, v0, ba, bb)
    fa, fb = jnp.stack([fa, ra]), jnp.stack([fb, rb])
    ge = jnp.stack([ge, far_e], axis=1)
    fa, fb, ge, ba1, bb1 = after((fa, fb, ge, ba1, bb1), m0)
    ra, rb = over_x(fa), over_y(fb)
    near_e = over_near(ge)
    ge = jnp.stack([ge, near_e], axis=1)
    m1, lse1 = attention_forward(bits, lens, qk1, v1, ba1, bb1)
    hid, unit, inverse, hidt = out_forward(x, m0, m1, wo0, wo1, gain1, bias1)
    fa, fb = jnp.stack([fa, ra]), jnp.stack([fb, rb])
    ea, eb = ge[0], ge[1]
    fa, fb, ea, eb = after((fa, fb, ea, eb), hid, ra, rb)
    fa1, fb1 = over_pair(fa), over_pair(fb)
    ra, rb = over_y(ea), over_x(eb)
    ea, eb = jnp.stack([ea, ra]), jnp.stack([eb, rb])
    ea, eb, hid = after((ea, eb, hid), fa1, fb1)
    ra, rb = over_x(ea), over_y(eb)
    actp, gpp, part = ffn_part(bits, hid, fa, fa1, fb, fb1)
    ea, eb = jnp.stack([ea, ra]), jnp.stack([eb, rb])
    ea, eb = after((ea, eb), part)
    ea1, eb1 = over_pair(ea), over_pair(eb)
    actq, gpq, out, dsec, dffn, dffnt, dgain2, dbias2 = ffn_rest(
        bits, lens, hid, ea, ea1, eb, eb1, part, gain2, bias2, dout
    )

    steps = total_steps()
    down0, down1 = down_grads(bits, dffnt, actp, actq)
    cd = over_pair(down1)
    dffn, = after((dffn,), down1)
    up1, part = ffn_backward(False, bits, hidt, dffn, fa1, ea1, fb1, eb1, gpp, gpq)
    down0, cd, up1, dffn = after((down0, cd, up1, dffn), part)
    xd = over_y(first_sum(down0, cd))
    cu = over_pair(up1)
    up0, dfirst, dattn, dattnt, dgain1, dbias1 = ffn_backward(
        True, bits, hidt, dffn, fa, ea, fb, eb, gpp, gpq, (dsec, part, unit, inverse, gain1)
    )
    up0, cu, norms, dattn = after((up0, cu, jnp.concatenate([dgain1, dgain2, dbias1, dbias2]), dattn), up0)
    xu = over_x(first_sum(up0, cu))
    norms = total_some(norms, steps[0])
    dqk1, dv1, ga1, gb1 = attention_backward(False, bits, lens, qk1, v1, ba1, bb1, lse1, dattn, wo1)
    ga1, gb1, norms, dqk1, xd = after((ga1, gb1, norms, dqk1, xd), dv1)
    cga, cgb = over_pair(ga1), over_pair(gb1)
    norms = total_some(norms, steps[3])
    qka1, vo1 = qkv_grads(False, bits, xt, dattnt, dqk1, dv1, m1)
    qka1, vo1, dattn, norms, cga, cgb, xu, xd = after((qka1, vo1, dattn, norms, cga, cgb, xu, xd), vo1)
    cqk, cvo = over_pair(qka1), over_pair(vo1)
    norms, = after((norms,), xu, xd)
    norms = total_some(norms, steps[1])
    send_d, send_u = second_sum(down0, cd, xd), second_sum(up0, cu, xu)
    send_d, send_u, norms = after((send_d, send_u, norms), norms)
    yd, yu = over_x(send_d), over_y(send_u)
    norms = total_some(norms, steps[4])
    dqk0, dv0, ga0, ga_out, gb0, gb_out = attention_backward(
        True, bits, lens, qk0, v0, ba, bb, lse0, dattn, wo0, (cga, cgb)
    )
    ga_out, gb_out, dqk0, norms, cqk, cvo, yd, yu = after((ga_out, gb_out, dqk0, norms, cqk, cvo, yd, yu), dv0)
    xga = over_x(ga_out)
    norms = total_some(norms, *steps[2:3], *steps[5:])
    gb_out, yu, yd, norms = after((gb_out, yu, yd, norms), norms)
    xgb = over_y(gb_out)
    u, d = third_sum(up0, cu, xu, yu), third_sum(down0, cd, xd, yd)
    send_f = jnp.stack([u[1], d[1]]).astype(BF16)
    near_f = over_near(send_f)
    qka0, qka_out, vo0, vo_out = qkv_grads(True, bits, xt, dattnt, dqk0, dv0, m0, (cqk, cvo))
    xqk, xvo = over_x(qka_out), over_y(vo_out)
    near_f, xga, xgb, dqk0 = after((near_f, xga, xgb, dqk0), vo0)
    yga, ygb = over_y(low_sum(ga0, xga)), over_x(low_sum(gb0, xgb))
    far_f = over_far(jnp.stack([u[0, 1] + wide(near_f[0, 1]), d[0, 1] + wide(near_f[1, 1])]).astype(BF16))
    dinput = input_backward(dfirst, dqk0, dqk1, dv0, dv1, wqk0, wqk1, wv0, wv1)
    xqk, xvo, yga, ygb, far_f = after((xqk, xvo, yga, ygb, far_f), dinput)
    send_qk, send_vo = low_sum(qka0, xqk), low_sum(vo0, xvo)
    g1, g2 = high_sum(ga0, xga, yga), high_sum(gb0, xgb, ygb)
    send_g = jnp.stack([g1[1], g2[1]]).astype(BF16)
    yqk, yvo = over_y(send_qk), over_x(send_vo)
    near_g = over_near(send_g)
    w1, w2 = high_sum(qka0, xqk, yqk), high_sum(vo0, xvo, yvo)
    send_w = jnp.stack([w1[1], w2[1]]).astype(BF16)
    send_g = jnp.stack([g1[0, 1] + wide(near_g[0, 1]), g2[0, 1] + wide(near_g[1, 1])]).astype(BF16)
    near_w = over_near(send_w)
    far_g = over_far(send_g)
    far_w = over_far(jnp.stack([w1[0, 1] + wide(near_w[0, 1]), w2[0, 1] + wide(near_w[1, 1])]).astype(BF16))

    up_grad = u[0, 0] + wide(near_f[0, 0]) + wide(far_f[0])
    down_grad = d[0, 0] + wide(near_f[1, 0]) + wide(far_f[1])
    gate_a = g1[0, 0] + wide(near_g[0, 0]) + wide(far_g[0])
    gate_b = g2[0, 0] + wide(near_g[1, 0]) + wide(far_g[1])
    qk_grad = w1[0, 0] + wide(near_w[0, 0]) + wide(far_w[0])
    vo_grad = w2[0, 0] + wide(near_w[1, 0]) + wide(far_w[1])

    qk_grad, vo_grad = inner_scatter(qk_grad, 0), inner_scatter(vo_grad, 0)
    local = vo_grad.shape[1] // 2
    gate_grad = inner_scatter(jnp.concatenate([gate_a, gate_b], axis=1), 1)
    return (
        out.reshape(micro, seq, width),
        dinput.reshape(micro, seq, width),
        jnp.stack([qk_grad[:, :local], qk_grad[:, local:], vo_grad[:, :local]]),
        vo_grad[:, local:].T,
        inner_scatter(up_grad, 0),
        inner_scatter(down_grad, 0).T,
        norms[:2],
        norms[2:],
        gate_grad * gate_part * (1.0 - gate_part),
    )


def solution(mesh):
    rows = P(None, ("dp", "head"), None)
    gates = P("head", "dp", None)
    weights = (P(None, "dp", "head"), P("head", "dp"), P("dp", "head"), P("head", "dp"))
    return jax.shard_map(
        per_device,
        mesh=mesh,
        in_specs=(rows, rows, P(None, "dp")) + weights + (P(), P(), gates, gates),
        out_specs=(rows, rows) + weights + (P(), P(), gates),
        check_vma=False,
    )
```

```python
import functools, math
import jax, jax.numpy as jnp
from jax import lax
from jax.experimental import pallas as pl
from jax.experimental.pallas import tpu as pltpu
from jax.sharding import PartitionSpec as P

HEAD_DIM = 64
EPS = 1e-05
F32 = jnp.float32
BF16 = jnp.bfloat16
GP = jnp.bfloat16
SCALE = 1.0 / math.sqrt(HEAD_DIM)
LOG2E = math.log2(math.e)
NEG = -1e30
INV_SQRT2 = 1.0 / math.sqrt(2.0)
INV_SQRT2PI = 1.0 / math.sqrt(2.0 * math.pi)


def dot_nn(a, b):
    return lax.dot_general(a, b, (((1,), (0,)), ((), ())), preferred_element_type=F32)


def dot_nt(a, b):
    return lax.dot_general(a, b, (((1,), (1,)), ((), ())), preferred_element_type=F32)


def dot_tn(a, b):
    return lax.dot_general(a, b, (((0,), (0,)), ((), ())), preferred_element_type=F32)


def piece(ref, bits, d, flip):
    y = bits[0] ^ (d & 1)
    z1 = bits[1] ^ ((d >> 1) & 1)
    z2 = bits[2] ^ ((d >> 2) & 1)
    if flip:
        return ref.at[y, 0, z1, z2]
    return ref.at[0, y, z1, z2]


def assemble(dst, ref, bits, flip, cols=None):
    rows = ref.shape[-2]
    cols = pl.ds(0, ref.shape[-1]) if cols is None else cols
    for d in range(8):
        dst[pl.ds(d * rows, rows), cols] = piece(ref, bits, d, flip)[...]


def scatter(ref, src, bits, flip):
    rows = ref.shape[-2]
    for d in range(8):
        piece(ref, bits, d, flip)[...] = src[pl.ds(d * rows, rows), :]


def own(bits, y, z1, z2):
    return (bits[0] ^ y) + 2 * (bits[1] ^ z1) + 4 * (bits[2] ^ z2)


RELATIVE = [(y, z1, z2) for y in range(2) for z1 in range(2) for z2 in range(2)]


def spec_a(tail, pick):
    zeros = (0,) * len(tail)
    return pl.BlockSpec((1, 2, 2, 2) + tail, lambda k, *_: (pick(k), 0, 0, 0) + zeros)


def spec_b(tail, pick):
    zeros = (0,) * len(tail)
    return pl.BlockSpec((2, 1, 2, 2) + tail, lambda k, *_: (0, pick(k), 0, 0) + zeros)


def whole(shape):
    zeros = (0,) * len(shape)
    return pl.BlockSpec(shape, lambda *_: zeros, pipeline_mode=pl.Buffered(1))


def low_pick(k):
    return jnp.minimum(k, 1)


def high_pick(k):
    return jnp.maximum(k - 2, 0)


def norm_stats(z):
    mean = jnp.mean(z, axis=1, keepdims=True)
    centered = z - mean
    inverse = lax.rsqrt(jnp.mean(centered * centered, axis=1, keepdims=True) + EPS)
    return centered * inverse, inverse


def norm_back(du, unit, inverse):
    return inverse * (
        du
        - jnp.mean(du, axis=1, keepdims=True)
        - unit * jnp.mean(du * unit, axis=1, keepdims=True)
    )


def gelu_pair(up):
    cdf = 0.5 + 0.5 * lax.erf(up * INV_SQRT2)
    pdf = INV_SQRT2PI * jnp.exp(-0.5 * (up * up))
    return up * cdf, cdf + up * pdf


SHARE = 10


def cost(flops, moved):
    return pl.CostEstimate(flops=flops * SHARE, bytes_accessed=moved * SHARE, transcendentals=0)


def params(mib=60, n=1):
    return pltpu.CompilerParams(
        dimension_semantics=("arbitrary",) * n, vmem_limit_bytes=mib * 1024 * 1024
    )


def load_pair(k, bits, wu, wd, ua0, ua1, db0, db1):
    @pl.when(k < 2)
    def _():
        assemble(wu, ua0, bits, False)
        assemble(wd, db0, bits, True)

    @pl.when(k >= 2)
    def _():
        assemble(wu, ua1, bits, False)
        assemble(wd, db1, bits, True)


def ffn_units(chunk, hid, wu, wd, act_o, gp_o, acc, finish=None):
    rows = hid.shape[0]
    ats = [pl.ds(r * chunk, chunk) for r in range(rows // chunk)]
    ahead = dot_nn(hid[ats[0], :], wu[...])
    for r, at in enumerate(ats):
        act, gp = gelu_pair(ahead)
        if r + 1 < len(ats):
            ahead = dot_nn(hid[ats[r + 1], :], wu[...])
        act = act.astype(BF16)
        act_o[0, at, :] = act
        gp_o[0, at, :] = gp.astype(gp_o.dtype)
        acc[at, :] += dot_nt(act, wd[...])
        if finish is not None:
            finish(r * chunk, chunk)


def ffn_part_kernel(chunk, bits, hid, ua0, ua1, db0, db1, act_o, gp_o, acc, wu, wd):
    k = pl.program_id(0)
    load_pair(k, bits, wu, wd, ua0, ua1, db0, db1)

    @pl.when(k == 0)
    def _():
        acc[...] = hid[...].astype(F32)

    ffn_units(chunk, hid, wu, wd, act_o, gp_o, acc)


def ffn_part(bits, hid, ua0, ua1, db0, db1, chunk=512):
    rows, width = hid.shape
    p, n = ua0.shape[-2:]
    sds = jax.ShapeDtypeStruct
    col = pl.BlockSpec((1, rows, n), lambda k, *_: (k, 0, 0))
    return pl.pallas_call(
        functools.partial(ffn_part_kernel, chunk),
        out_shape=(pltpu.HBM((4, rows, n), BF16), pltpu.HBM((4, rows, n), GP), sds((rows, width), F32)),
        grid_spec=pltpu.PrefetchScalarGridSpec(
            num_scalar_prefetch=1, grid=(4,),
            in_specs=[whole((rows, width)), spec_a((p, n), low_pick), spec_a((p, n), high_pick),
                      spec_b((p, n), low_pick), spec_b((p, n), high_pick)],
            out_specs=[col, col, whole((rows, width))],
            scratch_shapes=[pltpu.VMEM((width, n), BF16), pltpu.VMEM((width, n), BF16)],
        ),
        compiler_params=params(26),
        cost_estimate=cost(4 * rows * width * 4 * n, 16 * rows * width),
    )(bits, hid, ua0, ua1, db0, db1)


def ffn_rest_kernel(chunk, bits, lens, hid, ua0, ua1, db0, db1, part, gain, bias, dout,
                    act_o, gp_o, out, acc, dffn, dffnt, dgain, dbias, wu, wd):
    k = pl.program_id(0)
    rows = hid.shape[0]
    load_pair(k, bits, wu, wd, ua0, ua1, db0, db1)

    @pl.when(k == 0)
    def _():
        acc[...] = part[...]

    @pl.when(k < 3)
    def _():
        ffn_units(chunk, hid, wu, wd, act_o, gp_o, acc)

    @pl.when(k == 3)
    def _():
        length = rows // lens.shape[0]
        small = 256
        g = gain[...]
        b = bias[...]
        sums = [jnp.zeros_like(g), jnp.zeros_like(g)]

        def finish(start, count):
            for at0 in range(start, start + count, small):
                at = pl.ds(at0, small)
                size = lens[at0 // length]
                pos = (at0 % length) + lax.broadcasted_iota(jnp.int32, (small, 1), 0)
                valid = pos < size
                unit, inverse = norm_stats(acc[at, :])
                out[at, :] = jnp.where(valid, unit * g + b, 0.0).astype(BF16)
                dy = jnp.where(valid, dout[at, :].astype(F32), 0.0)
                sums[0] = sums[0] + jnp.sum(dy * unit, axis=0, keepdims=True)
                sums[1] = sums[1] + jnp.sum(dy, axis=0, keepdims=True)
                dz = norm_back(dy * g, unit, inverse)
                acc[at, :] = dz
                low = dz.astype(BF16)
                dffn[at, :] = low
                dffnt[:, at] = low.T

        ffn_units(chunk, hid, wu, wd, act_o, gp_o, acc, finish)
        dgain[...] = sums[0]
        dbias[...] = sums[1]


def ffn_rest(bits, lens, hid, ua0, ua1, db0, db1, part, gain, bias, dout, chunk=512):
    rows, width = hid.shape
    p, n = ua0.shape[-2:]
    sds = jax.ShapeDtypeStruct
    full = whole((rows, width))
    line = whole((1, width))
    col = pl.BlockSpec((1, rows, n), lambda k, *_: (k, 0, 0))
    return pl.pallas_call(
        functools.partial(ffn_rest_kernel, chunk),
        out_shape=(sds((4, rows, n), BF16), sds((4, rows, n), GP), sds((rows, width), BF16), sds((rows, width), F32),
                   sds((rows, width), BF16), sds((width, rows), BF16), sds((1, width), F32), sds((1, width), F32)),
        grid_spec=pltpu.PrefetchScalarGridSpec(
            num_scalar_prefetch=2, grid=(4,),
            in_specs=[full, spec_a((p, n), low_pick), spec_a((p, n), high_pick),
                      spec_b((p, n), low_pick), spec_b((p, n), high_pick), full, line, line, full],
            out_specs=[col, col, full, full, full, whole((width, rows)), line, line],
            scratch_shapes=[pltpu.VMEM((width, n), BF16), pltpu.VMEM((width, n), BF16)],
        ),
        compiler_params=params(30),
        cost_estimate=cost(4 * rows * width * 4 * n, 20 * rows * width),
    )(bits, lens, hid, ua0, ua1, db0, db1, part, gain, bias, dout)


def down_grad_kernel(bits, dt, actp, actq, keep, send):
    k = pl.program_id(0)
    first = dot_nn(dt[...], actp[0]).astype(BF16)
    second = dot_nn(dt[...], actq[0]).astype(BF16)
    rows = keep.shape[-2]
    n = actp.shape[2]

    def put(ref):
        for d in range(8):
            at = piece(ref, bits, d, True)
            at[:, pl.ds(0, n)] = first[d * rows : (d + 1) * rows]
            at[:, pl.ds(n, actq.shape[2])] = second[d * rows : (d + 1) * rows]

    @pl.when(k < 2)
    def _():
        put(keep)

    @pl.when(k >= 2)
    def _():
        put(send)


def down_grads(bits, dt, actp, actq):
    width, rows = dt.shape
    col = lambda a: pl.BlockSpec((1, rows, a.shape[2]), lambda k, *_: (k, 0, 0))
    n = actp.shape[2] + actq.shape[2]
    p = width // 8
    sds = jax.ShapeDtypeStruct
    return pl.pallas_call(
        down_grad_kernel,
        out_shape=(sds((2, 2, 2, 2, p, n), BF16), sds((2, 2, 2, 2, p, n), BF16)),
        grid_spec=pltpu.PrefetchScalarGridSpec(
            num_scalar_prefetch=1, grid=(4,),
            in_specs=[whole((width, rows)), col(actp), col(actq)],
            out_specs=[spec_b((p, n), low_pick), spec_b((p, n), high_pick)],
        ),
        compiler_params=params(22),
        cost_estimate=cost(2 * rows * width * 4 * n, 14 * rows * width),
    )(bits, dt, actp, actq)


def ffn_bwd_kernel(chunk, last, bits, ht, dffn, uap, uaq, dbp, dbq, gpp, gpq, *rest):
    if last:
        dsec, part, unit, inverse, gain, gu, acc, dattn, dattnt, dgain, dbias, wu, wd, dup_s = rest
    else:
        gu, acc, wu, wd, dup_s = rest
    k = pl.program_id(0)
    rows, width = dffn.shape
    np = uap.shape[-1]
    left, right = pl.ds(0, np), pl.ds(np, uaq.shape[-1])

    assemble(wu, uap, bits, False, left)
    assemble(wu, uaq, bits, False, right)
    assemble(wd, dbp, bits, True, left)
    assemble(wd, dbq, bits, True, right)

    @pl.when(k == 0)
    def _():
        if last:
            acc[...] = part[...] + dsec[...]
        else:
            acc[...] = jnp.zeros_like(acc)

    def run(finish=None):
        ats = [pl.ds(r * chunk, chunk) for r in range(rows // chunk)]
        ahead = dot_nn(dffn[ats[0], :], wd[...])
        for r, at in enumerate(ats):
            dup_s[at, left] = (ahead[:, :np] * gpp[0, at, :].astype(F32)).astype(BF16)
            dup_s[at, right] = (ahead[:, np:] * gpq[0, at, :].astype(F32)).astype(BF16)
            if r + 1 < len(ats):
                ahead = dot_nn(dffn[ats[r + 1], :], wd[...])
            acc[at, :] += dot_nt(dup_s[at, :], wu[...])
            if finish is not None:
                finish(r * chunk, chunk)
        grad = dot_nn(ht[...], dup_s[...]).astype(BF16)
        p = gu.shape[-2]
        for d in range(8):
            piece(gu, bits, d, False)[...] = grad[d * p : (d + 1) * p]

    if not last:
        run()
        return

    @pl.when(k == 0)
    def _():
        run()

    @pl.when(k == 1)
    def _():
        small = 256
        g = gain[...]
        sums = [jnp.zeros_like(g), jnp.zeros_like(g)]

        def finish(start, count):
            for at0 in range(start, start + count, small):
                at = pl.ds(at0, small)
                dh = acc[at, :]
                u = unit[at, :]
                sums[0] = sums[0] + jnp.sum(dh * u, axis=0, keepdims=True)
                sums[1] = sums[1] + jnp.sum(dh, axis=0, keepdims=True)
                dz = norm_back(dh * g, u, inverse[at, :])
                acc[at, :] = dz
                low = dz.astype(BF16)
                dattn[at, :] = low
                dattnt[:, at] = low.T

        run(finish)
        dgain[...] = sums[0]
        dbias[...] = sums[1]


def ffn_backward(last, bits, ht, dffn, uap, uaq, dbp, dbq, gpp, gpq, extra=(), chunk=512):
    rows, width = dffn.shape
    p, np = uap.shape[-2:]
    nq = uaq.shape[-1]
    n = np + nq
    sds = jax.ShapeDtypeStruct
    off = 0 if last else 2
    pick = lambda k: k
    full = whole((rows, width))
    line = whole((1, width))
    out_shape = [sds((2, 2, 2, 2, p, n), BF16)]
    out_specs = [spec_a((p, n), pick)]
    in_specs = [
        whole((width, rows)), full,
        spec_a((p, np), pick), spec_a((p, nq), pick), spec_b((p, np), pick), spec_b((p, nq), pick),
        pl.BlockSpec((1, rows, np), lambda k, *_: (k + off, 0, 0)),
        pl.BlockSpec((1, rows, nq), lambda k, *_: (k + off, 0, 0)),
    ]
    scratch = [pltpu.VMEM((width, n), BF16), pltpu.VMEM((width, n), BF16), pltpu.VMEM((rows, n), BF16)]
    if last:
        in_specs += [full] * 3 + [whole((rows, 1)), line]
        out_shape += [sds((rows, width), F32), sds((rows, width), BF16), sds((width, rows), BF16), sds((1, width), F32), sds((1, width), F32)]
        out_specs += [full, full, whole((width, rows)), line, line]
    else:
        out_shape += [sds((rows, width), F32)]
        out_specs += [full]
    return pl.pallas_call(
        functools.partial(ffn_bwd_kernel, chunk, last),
        out_shape=out_shape,
        grid_spec=pltpu.PrefetchScalarGridSpec(
            num_scalar_prefetch=1, grid=(2,), in_specs=in_specs, out_specs=out_specs, scratch_shapes=scratch,
        ),
        compiler_params=params(36),
        cost_estimate=cost(6 * rows * width * 2 * n, 30 * rows * width),
    )(bits, ht, dffn, uap, uaq, dbp, dbq, gpp, gpq, *extra)


def key_bias(size, length):
    pos = lax.broadcasted_iota(jnp.int32, (1, length), 1)
    return jnp.where(pos < size, 0.0, NEG).astype(F32)


def gate_rows(ga, gb, bits, i, d0, count):
    parts = []
    for j in range(count):
        d = d0 + j
        y = bits[0] ^ (d & 1)
        z1 = bits[1] ^ ((d >> 1) & 1)
        z2 = bits[2] ^ ((d >> 2) & 1)
        parts.append(ga[0, y, z1, z2, i])
        parts.append(gb[y, 0, z1, z2, i])
    return jnp.concatenate(parts, axis=0).astype(F32)


def att_fwd_kernel(bits, lens, qk, v, ga, gb, mixed, lse):
    length = qk.shape[1]
    heads = v.shape[2] // HEAD_DIM
    bias = key_bias(lens[pl.program_id(1)], length)
    count = length // (2 * ga.shape[-2])
    cols = [pl.ds(i * HEAD_DIM, HEAD_DIM) for i in range(2 * heads)]

    def score(i):
        return dot_nt(qk[0, :, cols[i]], qk[0, :, cols[heads + i]])

    ahead = score(0)
    outs = []
    stats = []
    for i in range(heads):
        s = ahead * (SCALE * LOG2E) + bias
        if i + 1 < heads:
            ahead = score(i + 1)
        top = jnp.max(s, axis=1, keepdims=True)
        e = jnp.exp2(s - top)
        total = jnp.sum(e, axis=1, keepdims=True)
        w = (e * gate_rows(ga, gb, bits, i, 0, count)).astype(BF16)
        outs.append(dot_nn(w, v[0, :, cols[i]]) * (1.0 / total))
        stats.append(top + jnp.log2(total))
    mixed[0] = jnp.concatenate(outs, axis=1).astype(BF16)
    lse[0] = jnp.concatenate(stats, axis=1)


def attention_forward(bits, lens, qk, v, ga, gb):
    _, rows, w2 = qk.shape
    w1 = v.shape[2]
    count = lens.shape[0]
    length = rows // count
    heads, sub, keys = ga.shape[-3:]
    sds = jax.ShapeDtypeStruct
    return pl.pallas_call(
        att_fwd_kernel,
        out_shape=(sds((2, rows, w1), BF16), sds((2, rows, heads), F32)),
        grid_spec=pltpu.PrefetchScalarGridSpec(
            num_scalar_prefetch=2, grid=(2, count),
            in_specs=[
                pl.BlockSpec((1, length, w2), lambda k, s, *_: (k, s, 0)),
                pl.BlockSpec((1, length, w1), lambda k, s, *_: (k, s, 0)),
                spec_a((heads, sub, keys), lambda k: k), spec_b((heads, sub, keys), lambda k: k),
            ],
            out_specs=[
                pl.BlockSpec((1, length, w1), lambda k, s, *_: (k, s, 0)),
                pl.BlockSpec((1, length, heads), lambda k, s, *_: (k, s, 0)),
            ],
        ),
        compiler_params=params(22, 2),
        cost_estimate=cost(16 * 2 * rows * length * w1, 16 * rows * w1),
    )(bits, lens, qk, v, ga, gb)


def att_bwd_kernel(last, bits, lens, qk, v, ga, gb, lse, dattn, wo, *rest):
    if last:
        ra, rb, dqk, dv, a_keep, a_send, b_keep, b_send, dm_s, dmt, qt, acc = rest
    else:
        dqk, dv, oga, ogb, dm_s, dmt, qt, acc = rest
    length = qk.shape[1]
    heads = v.shape[2] // HEAD_DIM
    hw = heads * HEAD_DIM
    k = pl.program_id(0)
    seq = pl.program_id(1)
    bias = key_bias(lens[seq], length)
    sub = ga.shape[-2]
    count = length // (2 * sub)
    cols = [pl.ds(i * HEAD_DIM, HEAD_DIM) for i in range(2 * heads)]

    dm = dot_nn(dattn[...], wo[0]).astype(BF16)
    dm_s[...] = dm
    dmt[...] = dm.T
    qt[...] = qk[0, :, pl.ds(0, hw)].T

    def products(i):
        return (
            dot_nt(qk[0, :, cols[i]], qk[0, :, cols[heads + i]]),
            dot_nt(dm_s[:, cols[i]], v[0, :, cols[i]]),
        )

    ahead = products(0)
    dqs, dks, dvs = [], [], []
    for i in range(heads):
        s, dw = ahead
        p = jnp.exp2(s * (SCALE * LOG2E) + bias - lse[0, :, pl.ds(i, 1)])
        if i + 1 < heads:
            ahead = products(i + 1)
        g = gate_rows(ga, gb, bits, i, 0, count)
        w = (p * g).astype(BF16)
        t = dw * p
        acc[i] = t + jnp.where(seq == 0, 0.0, acc[i])
        u = t * g
        ds = (u - p * jnp.sum(u, axis=1, keepdims=True)).astype(BF16)
        dqs.append(dot_nn(ds, qk[0, :, cols[heads + i]]) * SCALE)
        dvs.append(dot_nn(dmt[cols[i], :], w).astype(BF16).T)
        dks.append((dot_nn(qt[cols[i], :], ds) * SCALE).astype(BF16).T)
    dqk[0] = jnp.concatenate([d.astype(BF16) for d in dqs] + dks, axis=1)
    dv[0] = jnp.concatenate(dvs, axis=1)

    def first_rows(y, z1, z2):
        return pl.ds(pl.multiple_of(own(bits, y, z1, z2) * 2 * sub, sub), sub)

    def second_rows(y, z1, z2):
        return pl.ds(pl.multiple_of(own(bits, y, z1, z2) * 2 * sub + sub, sub), sub)

    @pl.when(seq == pl.num_programs(1) - 1)
    def _():
        if not last:
            for r in RELATIVE:
                for i in range(heads):
                    oga[(0,) + r + (i,)] = acc[i, first_rows(*r), :].astype(BF16)
                    ogb[(r[0], 0) + r[1:] + (i,)] = acc[i, second_rows(*r), :].astype(BF16)
            return

        def put_a(ref):
            for r in RELATIVE:
                for i in range(heads):
                    ref[r + (i,)] = (acc[i, first_rows(*r), :] + ra[(0,) + r + (i,)].astype(F32)).astype(BF16)

        @pl.when(k == 0)
        def _():
            put_a(a_keep)

        @pl.when(k == 1)
        def _():
            put_a(a_send)

        for r in RELATIVE:
            ref = b_send if r[0] else b_keep
            for i in range(heads):
                ref[(0,) + r[1:] + (i,)] = (
                    acc[i, second_rows(*r), :] + rb[(r[0], 0) + r[1:] + (i,)].astype(F32)
                ).astype(BF16)


def attention_backward(last, bits, lens, qk, v, ga, gb, lse, dattn, wo, got=()):
    _, rows, w2 = qk.shape
    w1 = v.shape[2]
    width = dattn.shape[1]
    count = lens.shape[0]
    length = rows // count
    tail = ga.shape[-3:]
    heads, sub, keys = tail
    sds = jax.ShapeDtypeStruct
    pick = lambda k: k
    in_specs = [
        pl.BlockSpec((1, length, w2), lambda k, s, *_: (k, s, 0)),
        pl.BlockSpec((1, length, w1), lambda k, s, *_: (k, s, 0)),
        spec_a(tail, pick), spec_b(tail, pick),
        pl.BlockSpec((1, length, heads), lambda k, s, *_: (k, s, 0)),
        pl.BlockSpec((length, width), lambda k, s, *_: (s, 0)),
        pl.BlockSpec((1, width, w1), lambda k, s, *_: (k, 0, 0)),
    ]
    out_shape = [sds((2, rows, w2), BF16), sds((2, rows, w1), BF16)]
    out_specs = [
        pl.BlockSpec((1, length, w2), lambda k, s, *_: (k, s, 0)),
        pl.BlockSpec((1, length, w1), lambda k, s, *_: (k, s, 0)),
    ]
    if last:
        in_specs += [spec_a(tail, pick), spec_b(tail, pick)]
        out_shape += [sds((2, 2, 2) + tail, BF16)] * 4
        out_specs += [whole((2, 2, 2) + tail)] * 2 + [
            pl.BlockSpec((1, 2, 2) + tail, lambda k, *_: (k, 0, 0, 0, 0, 0))
        ] * 2
    else:
        out_shape += [sds((2, 2, 2, 2) + tail, BF16)] * 2
        out_specs += [spec_a(tail, pick), spec_b(tail, pick)]
    return pl.pallas_call(
        functools.partial(att_bwd_kernel, last),
        out_shape=out_shape,
        grid_spec=pltpu.PrefetchScalarGridSpec(
            num_scalar_prefetch=2, grid=(2, count), in_specs=in_specs, out_specs=out_specs,
            scratch_shapes=[
                pltpu.VMEM((length, w1), BF16), pltpu.VMEM((w1, length), BF16),
                pltpu.VMEM((w1, length), BF16), pltpu.VMEM((heads, length, keys), F32),
            ],
        ),
        compiler_params=params(30, 2),
        cost_estimate=cost(40 * 2 * rows * length * w1, 30 * rows * w1),
    )(bits, lens, qk, v, ga, gb, lse, dattn, wo, *got)


def qkv_kernel(first, bits, x, wa, wb, qk, v, wqk, wv, wo, *rest):
    w1 = v.shape[2]
    wb_s = rest[-1]
    assemble(wqk.at[0], wa, bits, False)
    assemble(wb_s, wb, bits, True)

    if first:

        @pl.when(pl.program_id(0) == 0)
        def _():
            rest[0][...] = x[...].T

    wv[0] = wb_s[:, pl.ds(0, w1)]
    wo[0] = wb_s[:, pl.ds(w1, w1)]
    qk[0] = dot_nn(x[...], wqk[0]).astype(BF16)
    v[0] = dot_nn(x[...], wv[0]).astype(BF16)


def project(first, bits, x, wa, wb):
    rows, width = x.shape
    p, w2 = wa.shape[-2:]
    w1 = w2 // 2
    sds = jax.ShapeDtypeStruct
    pick = lambda k: k
    head = lambda s: pl.BlockSpec((1,) + s, lambda k, *_: (k, 0, 0))
    return pl.pallas_call(
        functools.partial(qkv_kernel, first),
        out_shape=[sds((2, rows, w2), BF16), sds((2, rows, w1), BF16), pltpu.HBM((2, width, w2), BF16),
                   pltpu.HBM((2, width, w1), BF16), sds((2, width, w1), BF16)]
        + ([pltpu.HBM((width, rows), BF16)] if first else []),
        grid_spec=pltpu.PrefetchScalarGridSpec(
            num_scalar_prefetch=1, grid=(2,),
            in_specs=[whole((rows, width)), spec_a((p, w2), pick), spec_b((p, w2), pick)],
            out_specs=[head((rows, w2)), head((rows, w1)), head((width, w2)), head((width, w1)), head((width, w1))]
            + ([whole((width, rows))] if first else []),
            scratch_shapes=[pltpu.VMEM((width, w2), BF16)],
        ),
        compiler_params=params(24),
        cost_estimate=cost(2 * rows * width * 2 * (w1 + w2), 8 * rows * width),
    )(bits, x, wa, wb)


def out_kernel(x, m0, m1, wo0, wo1, gain, bias, hid, unit, inverse, hidt):
    attn = dot_nt(m0[0], wo0[0]) + dot_nt(m0[1], wo0[1]) + dot_nt(m1[0], wo1[0]) + dot_nt(m1[1], wo1[1])
    u, inv = norm_stats(x[...].astype(F32) + attn)
    h = (u * gain[...] + bias[...]).astype(BF16)
    hid[...] = h
    hidt[...] = h.T
    unit[...] = u
    inverse[...] = inv


def out_forward(x, m0, m1, wo0, wo1, gain, bias, block=256):
    rows, width = x.shape
    w1 = wo0.shape[2]
    sds = jax.ShapeDtypeStruct
    row = lambda w: pl.BlockSpec((block, w), lambda r: (r, 0))
    mix = pl.BlockSpec((2, block, w1), lambda r: (0, r, 0))
    return pl.pallas_call(
        out_kernel,
        grid=(rows // block,),
        out_shape=(sds((rows, width), BF16), pltpu.HBM((rows, width), F32), sds((rows, 1), F32), pltpu.HBM((width, rows), BF16)),
        in_specs=[row(width), mix, mix, whole((2, width, w1)), whole((2, width, w1)), whole((1, width)), whole((1, width))],
        out_specs=[row(width), row(width), row(1), pl.BlockSpec((width, block), lambda r: (0, r))],
        compiler_params=params(20),
        cost_estimate=cost(2 * rows * width * 4 * w1, 12 * rows * width),
    )(x, m0, m1, wo0, wo1, gain, bias)


def qkv_grad_kernel(last, bits, xt, dat, dqk, dv, mixed, *rest):
    if last:
        ra, rb, a_keep, a_send, b_keep, b_send, ta, tb = rest
    else:
        ga, gb, ta, tb = rest
    w1 = dv.shape[2]
    k = pl.program_id(0)
    ta[...] = dot_nn(xt[...], dqk[0]).astype(ta.dtype)
    tb[:, pl.ds(0, w1)] = dot_nn(xt[...], dv[0]).astype(tb.dtype)
    tb[:, pl.ds(w1, w1)] = dot_nn(dat[...], mixed[0]).astype(tb.dtype)
    if not last:
        scatter(ga, ta, bits, False)
        scatter(gb, tb, bits, True)
        return
    p = ra.shape[-2]

    def rows(r):
        return pl.ds(pl.multiple_of(own(bits, *r) * p, 16), p)

    def put_a(ref):
        for r in RELATIVE:
            ref[r] = (ta[rows(r), :] + ra[(0,) + r].astype(F32)).astype(BF16)

    @pl.when(k == 0)
    def _():
        put_a(a_keep)

    @pl.when(k == 1)
    def _():
        put_a(a_send)

    for r in RELATIVE:
        ref = b_send if r[0] else b_keep
        ref[(0,) + r[1:]] = (tb[rows(r), :] + rb[(r[0], 0) + r[1:]].astype(F32)).astype(BF16)


def qkv_grads(last, bits, xt, dat, dqk, dv, mixed, got=()):
    width, rows = xt.shape
    w2 = dqk.shape[2]
    w1 = dv.shape[2]
    per = width // 8
    sds = jax.ShapeDtypeStruct
    pick = lambda k: k
    head = lambda w: pl.BlockSpec((1, rows, w), lambda k, *_: (k, 0, 0))
    in_specs = [whole((width, rows)), whole((width, rows)), head(w2), head(w1), head(w1)]
    if last:
        in_specs += [spec_a((per, w2), pick), spec_b((per, w2), pick)]
        out_shape = [sds((2, 2, 2, per, w2), BF16)] * 4
        out_specs = [whole((2, 2, 2, per, w2))] * 2 + [
            pl.BlockSpec((1, 2, 2, per, w2), lambda k, *_: (k, 0, 0, 0, 0))
        ] * 2
    else:
        out_shape = [sds((2, 2, 2, 2, per, w2), BF16)] * 2
        out_specs = [spec_a((per, w2), pick), spec_b((per, w2), pick)]
    kind = F32 if last else BF16
    return pl.pallas_call(
        functools.partial(qkv_grad_kernel, last),
        out_shape=out_shape,
        grid_spec=pltpu.PrefetchScalarGridSpec(
            num_scalar_prefetch=1, grid=(2,), in_specs=in_specs, out_specs=out_specs,
            scratch_shapes=[pltpu.VMEM((width, w2), kind), pltpu.VMEM((width, w2), kind)],
        ),
        compiler_params=params(26),
        cost_estimate=cost(1 if last else 8 * rows * width * w2, 1 if last else 8 * rows * width),
    )(bits, xt, dat, dqk, dv, mixed, *got)


def dinput_kernel(dfirst, dqk0, dqk1, dv0, dv1, wqk0, wqk1, wv0, wv1, out):
    total = dfirst[...]
    for a, b, wa, wb in ((dqk0, dv0, wqk0, wv0), (dqk1, dv1, wqk1, wv1)):
        for k in range(2):
            total = total + dot_nt(a[k], wa[k]) + dot_nt(b[k], wb[k])
    out[...] = total


def input_backward(dfirst, dqk0, dqk1, dv0, dv1, wqk0, wqk1, wv0, wv1, block=256):
    rows, width = dfirst.shape
    w2 = wqk0.shape[2]
    w1 = wv0.shape[2]
    row = pl.BlockSpec((block, width), lambda r: (r, 0))
    part = lambda w: pl.BlockSpec((2, block, w), lambda r: (0, r, 0))
    return pl.pallas_call(
        dinput_kernel,
        grid=(rows // block,),
        out_shape=jax.ShapeDtypeStruct((rows, width), F32),
        in_specs=[row, part(w2), part(w2), part(w1), part(w1)]
        + [whole((2, width, w2))] * 2 + [whole((2, width, w1))] * 2,
        out_specs=row,
        compiler_params=params(24),
        cost_estimate=cost(1, 1),
    )(dfirst, dqk0, dqk1, dv0, dv1, wqk0, wqk1, wv0, wv1)


GROUPS = 8


def partner_dp(value, bit):
    size = lax.axis_size("dp")
    step = (1 << bit) * (size // GROUPS)
    return lax.ppermute(value, "dp", [(i, i ^ step) for i in range(size)])


def partner_head(value, bit):
    size = lax.axis_size("head")
    return lax.ppermute(value, "head", [(i, i ^ (1 << bit)) for i in range(size)])


def over_y(value):
    return partner_dp(value, 0)


def over_near(value):
    return partner_dp(value, 1)


def over_far(value):
    return partner_dp(value, 2)


def over_pair(value):
    return partner_head(value, 0)


def over_x(value):
    return partner_head(value, 1)


def inner_groups():
    inner = lax.axis_size("dp") // GROUPS
    return inner, [[g * inner + i for i in range(inner)] for g in range(GROUPS)]


def inner_gather(value, axis):
    inner, groups = inner_groups()
    if inner == 1:
        return value
    return lax.all_gather(value, "dp", axis_index_groups=groups, axis=axis, tiled=True)


def inner_scatter(value, axis):
    inner, groups = inner_groups()
    if inner == 1:
        return value
    return lax.psum_scatter(value, "dp", axis_index_groups=groups, scatter_dimension=axis, tiled=True)


def after(values, *waits):
    return lax.optimization_barrier((tuple(values), waits))[0]


def wide(value):
    return value.astype(F32)


def first_sum(keep, got):
    return (wide(keep[1]) + wide(got[1])).astype(BF16)


def second_sum(keep, got, more):
    return (wide(keep[0, 1]) + wide(got[0, 1]) + wide(more[1])).astype(BF16)


def third_sum(keep, got, more, last):
    return wide(keep[0, 0]) + wide(got[0, 0]) + wide(more[0]) + wide(last)


def low_sum(keep, got):
    return (wide(keep[1]) + wide(got[1])).astype(BF16)


def high_sum(keep, got, more):
    return wide(keep[0]) + wide(got[0]) + wide(more)


def total_steps():
    steps = []
    for name in ("head", "dp"):
        size = lax.axis_size(name)
        step = 1
        while step < size:
            steps.append((name, [(i, i ^ step) for i in range(size)]))
            step *= 2
    return steps


def total_some(value, *steps):
    for name, pairs in steps:
        value = value + lax.ppermute(value, name, pairs)
    return value


def per_device(layer_input, output_grad, lengths, w_qkv, w_out, w_up, w_down,
               norm_gains, norm_biases, mask_logits, mask_noise):
    micro, seq, width = layer_input.shape
    rows = micro * seq
    x = layer_input.reshape(rows, width)
    dout = output_grad.reshape(rows, width)
    place = lax.axis_index("dp") // (lax.axis_size("dp") // GROUPS)
    bits = jnp.stack([place & 1, (place >> 1) & 1, (place >> 2) & 1]).astype(jnp.int32)
    lens = lax.dynamic_slice_in_dim(lengths, lax.axis_index("head"), 1, 1).reshape(micro)

    gate_part = jax.nn.sigmoid(mask_logits + mask_noise)
    gate_all = inner_gather(gate_part.astype(BF16), 1)
    sub = gate_all.shape[1] // 2
    gain1, gain2 = norm_gains[0:1], norm_gains[1:2]
    bias1, bias2 = norm_biases[0:1], norm_biases[1:2]

    ga = jnp.stack([
        inner_gather(jnp.concatenate([w_qkv[0], w_qkv[1]], axis=1), 0),
        inner_gather(jnp.concatenate([w_qkv[2], w_out.T], axis=1), 0),
    ])
    gb = jnp.stack([gate_all[:, :sub], gate_all[:, sub:]])
    up_all, down_all = inner_gather(w_up, 0), inner_gather(w_down.T, 0)
    units = up_all.shape[1]
    most = units * 2 // 3
    gc = jnp.stack([up_all[:, :most], down_all[:, :most]])
    ge = jnp.stack([up_all[:, most:], down_all[:, most:]])

    got = over_far(ga)
    ga = jnp.stack([ga, got], axis=1)
    got = over_near(ga)
    ga = jnp.stack([ga, got], axis=1)
    aa, ab = ga[0], ga[1]
    (gb,) = after((gb,), got)
    ra, rb = over_y(aa), over_x(ab)
    far_b = over_far(gb)
    aa, ab = jnp.stack([aa, ra]), jnp.stack([ab, rb])
    gb, = after((gb,), ra, rb)
    gb = jnp.stack([gb, far_b], axis=1)
    aa, ab = after((aa, ab), gb)
    ra, rb = over_x(aa), over_y(ab)
    near_b = over_near(gb)
    (gc,) = after((gc,), near_b)
    far_c = over_far(gc)
    gb = jnp.stack([gb, near_b], axis=1)
    ba, bb = gb[0], gb[1]
    aa, ab = jnp.stack([aa, ra]), jnp.stack([ab, rb])
    ba, bb = after((ba, bb), ra, rb)
    ca, cb = over_pair(aa), over_pair(ab)
    ra, rb = over_y(ba), over_x(bb)
    qk0, v0, wqk0, wv0, wo0, xt = project(True, bits, x, aa, ab)
    ba, bb = jnp.stack([ba, ra]), jnp.stack([bb, rb])
    ba, bb, gc, ca, cb = after((ba, bb, gc, ca, cb), qk0, ra, rb)
    ra, rb = over_x(ba), over_y(bb)
    gc = jnp.stack([gc, far_c], axis=1)
    near_c = over_near(gc)
    qk1, v1, wqk1, wv1, wo1 = project(False, bits, x, ca, cb)
    ba, bb = jnp.stack([ba, ra]), jnp.stack([bb, rb])
    gc = jnp.stack([gc, near_c], axis=1)
    fa, fb = gc[0], gc[1]
    fa, fb, ba, bb, ge = after((fa, fb, ba, bb, ge), ra, rb, near_c, qk1)
    ba1, bb1 = over_pair(ba), over_pair(bb)
    ra, rb = over_y(fa), over_x(fb)
    far_e = over_far(ge)
    m0, lse0 = attention_forward(bits, lens, qk0, v0, ba, bb)
    fa, fb = jnp.stack([fa, ra]), jnp.stack([fb, rb])
    ge = jnp.stack([ge, far_e], axis=1)
    fa, fb, ge, ba1, bb1 = after((fa, fb, ge, ba1, bb1), m0)
    ra, rb = over_x(fa), over_y(fb)
    near_e = over_near(ge)
    ge = jnp.stack([ge, near_e], axis=1)
    m1, lse1 = attention_forward(bits, lens, qk1, v1, ba1, bb1)
    hid, unit, inverse, hidt = out_forward(x, m0, m1, wo0, wo1, gain1, bias1)
    fa, fb = jnp.stack([fa, ra]), jnp.stack([fb, rb])
    ea, eb = ge[0], ge[1]
    fa, fb, ea, eb = after((fa, fb, ea, eb), hid, ra, rb)
    fa1, fb1 = over_pair(fa), over_pair(fb)
    ra, rb = over_y(ea), over_x(eb)
    ea, eb = jnp.stack([ea, ra]), jnp.stack([eb, rb])
    ea, eb, hid = after((ea, eb, hid), fa1, fb1)
    ra, rb = over_x(ea), over_y(eb)
    actp, gpp, part = ffn_part(bits, hid, fa, fa1, fb, fb1)
    ea, eb = jnp.stack([ea, ra]), jnp.stack([eb, rb])
    ea, eb = after((ea, eb), part)
    ea1, eb1 = over_pair(ea), over_pair(eb)
    actq, gpq, out, dsec, dffn, dffnt, dgain2, dbias2 = ffn_rest(
        bits, lens, hid, ea, ea1, eb, eb1, part, gain2, bias2, dout
    )

    steps = total_steps()
    down0, down1 = down_grads(bits, dffnt, actp, actq)
    cd = over_pair(down1)
    dffn, = after((dffn,), down1)
    up1, part = ffn_backward(False, bits, hidt, dffn, fa1, ea1, fb1, eb1, gpp, gpq)
    down0, cd, up1, dffn = after((down0, cd, up1, dffn), part)
    xd = over_y(first_sum(down0, cd))
    cu = over_pair(up1)
    up0, dfirst, dattn, dattnt, dgain1, dbias1 = ffn_backward(
        True, bits, hidt, dffn, fa, ea, fb, eb, gpp, gpq, (dsec, part, unit, inverse, gain1)
    )
    up0, cu, norms, dattn = after((up0, cu, jnp.concatenate([dgain1, dgain2, dbias1, dbias2]), dattn), up0)
    xu = over_x(first_sum(up0, cu))
    norms = total_some(norms, steps[0])
    dqk1, dv1, ga1, gb1 = attention_backward(False, bits, lens, qk1, v1, ba1, bb1, lse1, dattn, wo1)
    ga1, gb1, norms, dqk1, xd = after((ga1, gb1, norms, dqk1, xd), dv1)
    cga, cgb = over_pair(ga1), over_pair(gb1)
    norms = total_some(norms, steps[3])
    qka1, vo1 = qkv_grads(False, bits, xt, dattnt, dqk1, dv1, m1)
    qka1, vo1, dattn, norms, cga, cgb, xu, xd = after((qka1, vo1, dattn, norms, cga, cgb, xu, xd), vo1)
    cqk, cvo = over_pair(qka1), over_pair(vo1)
    norms, = after((norms,), xu, xd)
    norms = total_some(norms, steps[1])
    send_d, send_u = second_sum(down0, cd, xd), second_sum(up0, cu, xu)
    send_d, send_u, norms = after((send_d, send_u, norms), norms)
    yd, yu = over_x(send_d), over_y(send_u)
    norms = total_some(norms, steps[4])
    dqk0, dv0, ga0, ga_out, gb0, gb_out = attention_backward(
        True, bits, lens, qk0, v0, ba, bb, lse0, dattn, wo0, (cga, cgb)
    )
    ga_out, gb_out, dqk0, norms, cqk, cvo, yd, yu = after((ga_out, gb_out, dqk0, norms, cqk, cvo, yd, yu), dv0)
    xga = over_x(ga_out)
    norms = total_some(norms, *steps[2:3], *steps[5:])
    gb_out, yu, yd, norms = after((gb_out, yu, yd, norms), norms)
    xgb = over_y(gb_out)
    u, d = third_sum(up0, cu, xu, yu), third_sum(down0, cd, xd, yd)
    send_f = jnp.stack([u[1], d[1]]).astype(BF16)
    near_f = over_near(send_f)
    qka0, qka_out, vo0, vo_out = qkv_grads(True, bits, xt, dattnt, dqk0, dv0, m0, (cqk, cvo))
    xqk, xvo = over_x(qka_out), over_y(vo_out)
    near_f, xga, xgb, dqk0 = after((near_f, xga, xgb, dqk0), vo0)
    yga, ygb = over_y(low_sum(ga0, xga)), over_x(low_sum(gb0, xgb))
    far_f = over_far(jnp.stack([u[0, 1] + wide(near_f[0, 1]), d[0, 1] + wide(near_f[1, 1])]).astype(BF16))
    dinput = input_backward(dfirst, dqk0, dqk1, dv0, dv1, wqk0, wqk1, wv0, wv1)
    xqk, xvo, yga, ygb, far_f = after((xqk, xvo, yga, ygb, far_f), dinput)
    send_qk, send_vo = low_sum(qka0, xqk), low_sum(vo0, xvo)
    g1, g2 = high_sum(ga0, xga, yga), high_sum(gb0, xgb, ygb)
    send_g = jnp.stack([g1[1], g2[1]]).astype(BF16)
    yqk, yvo = over_y(send_qk), over_x(send_vo)
    near_g = over_near(send_g)
    w1, w2 = high_sum(qka0, xqk, yqk), high_sum(vo0, xvo, yvo)
    send_w = jnp.stack([w1[1], w2[1]]).astype(BF16)
    send_g = jnp.stack([g1[0, 1] + wide(near_g[0, 1]), g2[0, 1] + wide(near_g[1, 1])]).astype(BF16)
    near_w = over_near(send_w)
    far_g = over_far(send_g)
    far_w = over_far(jnp.stack([w1[0, 1] + wide(near_w[0, 1]), w2[0, 1] + wide(near_w[1, 1])]).astype(BF16))

    up_grad = u[0, 0] + wide(near_f[0, 0]) + wide(far_f[0])
    down_grad = d[0, 0] + wide(near_f[1, 0]) + wide(far_f[1])
    gate_a = g1[0, 0] + wide(near_g[0, 0]) + wide(far_g[0])
    gate_b = g2[0, 0] + wide(near_g[1, 0]) + wide(far_g[1])
    qk_grad = w1[0, 0] + wide(near_w[0, 0]) + wide(far_w[0])
    vo_grad = w2[0, 0] + wide(near_w[1, 0]) + wide(far_w[1])

    qk_grad, vo_grad = inner_scatter(qk_grad, 0), inner_scatter(vo_grad, 0)
    local = vo_grad.shape[1] // 2
    gate_grad = inner_scatter(jnp.concatenate([gate_a, gate_b], axis=1), 1)
    return (
        out.reshape(micro, seq, width),
        dinput.reshape(micro, seq, width),
        jnp.stack([qk_grad[:, :local], qk_grad[:, local:], vo_grad[:, :local]]),
        vo_grad[:, local:].T,
        inner_scatter(up_grad, 0),
        inner_scatter(down_grad, 0).T,
        norms[:2],
        norms[2:],
        gate_grad * gate_part * (1.0 - gate_part),
    )


def solution(mesh):
    rows = P(None, ("dp", "head"), None)
    gates = P("head", "dp", None)
    weights = (P(None, "dp", "head"), P("head", "dp"), P("dp", "head"), P("head", "dp"))
    return jax.shard_map(
        per_device,
        mesh=mesh,
        in_specs=(rows, rows, P(None, "dp")) + weights + (P(), P(), gates, gates),
        out_specs=(rows, rows) + weights + (P(), P(), gates),
        check_vma=False,
    )
```
